32 devices in a mesh: dp: 8 (over z, y), tensor: 4 (over x, core).
Axes of the slice: x: 2, y: 2, z: 4, core: 2. Of those that a mesh axis runs over, the one named last changes fastest.
Arguments:
- embedded: bfloat16 [8192, 768], P(('dp', 'tensor')), may hold values from -6 to 6
- ids_two: int32 [8192], P('dp'), may hold values from 0 to 8191
- ids_three: int32 [8192], P('dp'), may hold values from 0 to 8191
- parents: int32 [8192], P('dp'), may hold values from 0 to 4, as said below
- table_two: float32 [8192, 192], P('dp', 'tensor'), may hold values from -6 to 6
- table_three: float32 [8192, 192], P('dp', 'tensor'), may hold values from -6 to 6
- w_two: float32 [192, 768], P('tensor', 'dp'), may hold values from -0.4375 to 0.4375
- w_three: float32 [192, 768], P('tensor', 'dp'), may hold values from -0.4375 to 0.4375
- norm_attn: float32 [768], replicated, may hold values from 0.5 to 1.5
- w_query: float32 [768, 768], P('dp', 'tensor'), may hold values from -0.21875 to 0.21875
- w_key: float32 [768, 768], P('dp', 'tensor'), may hold values from -0.21875 to 0.21875
- w_value: float32 [768, 768], P('dp', 'tensor'), may hold values from -0.21875 to 0.21875
- w_output: float32 [768, 768], P('tensor', 'dp'), may hold values from -0.875 to 0.875
- norm_ffn: float32 [768], replicated, may hold values from 0.5 to 1.5
- w_gate: float32 [768, 2048], P('dp', 'tensor'), may hold values from -0.21875 to 0.21875
- w_up: float32 [768, 2048], P('dp', 'tensor'), may hold values from -0.21875 to 0.21875
- w_down: float32 [2048, 768], P('tensor', 'dp'), may hold values from -0.125 to 0.125
- cotangent: bfloat16 [8192, 768], P(('dp', 'tensor')), may hold values from -6 to 6
Outputs:
- output: bfloat16 [8192, 768], P(('dp', 'tensor'))
- embed_grad: bfloat16 [8192, 768], P(('dp', 'tensor'))
- table_two_grad: float32 [8192, 192], P('dp', 'tensor')
- table_three_grad: float32 [8192, 192], P('dp', 'tensor')
- w_two_grad: float32 [192, 768], P('tensor', 'dp')
- w_three_grad: float32 [192, 768], P('tensor', 'dp')
- norm_attn_grad: float32 [768], replicated
- w_query_grad: float32 [768, 768], P('dp', 'tensor')
- w_key_grad: float32 [768, 768], P('dp', 'tensor')
- w_value_grad: float32 [768, 768], P('dp', 'tensor')
- w_output_grad: float32 [768, 768], P('tensor', 'dp')
- norm_ffn_grad: float32 [768], replicated
- w_gate_grad: float32 [768, 2048], P('dp', 'tensor')
- w_up_grad: float32 [768, 2048], P('dp', 'tensor')
- w_down_grad: float32 [2048, 768], P('tensor', 'dp')
The draws below stay inside these ranges and needn't reach their ends.
Inputs may be any that keep to these rules, and one draw needn't show every extreme that they name: Every tree has seven blocks: the trunk, then six blocks that are two branches and their two leaves each, every leaf after its branch, in an order drawn for each tree. parents holds, for every token of a block, the index of the parent block: 0 for the trunk and for branches, the branch's block index for a leaf.
All inputs are finite; a program needn't handle non-finite values.
Results may differ from the reference program's by a relative error of at most 0.015.
Values may be sent and summed in bfloat16 or wider, within the bound.
No kernel may reach another device: no remote copies, remote signals or barrier semaphores. Data moves between devices by JAX's collectives and lax.ppermute only.
A program may use at most 192 MiB of HBM per device.

```python
import math
import jax
import jax.numpy as jnp
import numpy as np
from jax import lax

D = 768
HD = 64
FF = 2048
NG = 192
SEG = 128
TREE = 1024
TABLE_ROWS = 8192
TOKENS = 8192


def draw_parents(key, part):
    trees = TOKENS // TREE
    base_key = jax.random.fold_in(key, 11)
    keys_list = jax.random.split(base_key, 3)
    leaf_keys = jax.random.split(keys_list[0], trees)
    leaf_order = jax.vmap(lambda single: jax.random.permutation(single, 4))(leaf_keys).astype(jnp.int32)
    owner = (1 + jnp.argsort(leaf_order, axis=1) // 2).astype(jnp.int32)
    branch_value = jax.random.randint(keys_list[1], (trees, 2), 0, 4, dtype=jnp.int32)
    branch_value = branch_value.at[0].set(jnp.array([0, 3], jnp.int32))
    leaf_extra = jax.random.randint(keys_list[2], (trees, 4), 0, 4, dtype=jnp.int32)
    leaf_extra = leaf_extra.at[0].set(jnp.zeros((4,), jnp.int32))
    leaf_value = jnp.take_along_axis(branch_value, owner - 1, axis=1) + 1 + leaf_extra
    node_value = jnp.concatenate([-jnp.ones((trees, 1), jnp.int32), branch_value, leaf_value], axis=1)
    node_score = node_value * 8 + jnp.arange(7, dtype=jnp.int32)[None, :]
    order = jnp.argsort(node_score, axis=1).astype(jnp.int32)
    node_rank = jnp.argsort(order, axis=1).astype(jnp.int32)
    node_parent = jnp.concatenate([jnp.zeros((trees, 3), jnp.int32), owner], axis=1)
    parent_rank = jnp.take_along_axis(node_rank, node_parent, axis=1)
    block_parent = jnp.take_along_axis(parent_rank, order, axis=1)
    token_index = jnp.arange(TREE, dtype=jnp.int32)
    block_of = jnp.where(token_index < 2 * SEG, 0, (token_index - 2 * SEG) // SEG + 1).astype(jnp.int32)
    per_token = jnp.take(block_parent, block_of, axis=1)
    return per_token.reshape(-1).astype(jnp.int32)


def place_ends(drawn, rng, least, top_value):
    spot = [jax.random.randint(jax.random.fold_in(rng, axis), (), 0, length) for axis, length in enumerate(drawn.shape)]
    main_axis = drawn.shape.index(max(drawn.shape))
    beside = spot[:main_axis] + [(spot[main_axis] + 1) % drawn.shape[main_axis]] + spot[main_axis + 1:]
    return drawn.at[tuple(spot)].set(least).at[tuple(beside)].set(top_value)


def shard_levels(own_key, dims, pieces, smallest, largest):
    gain, own = 1.0, jax.random.fold_in(own_key, 6)
    for dim, shards_of in pieces:
        draws = jnp.exp(jax.random.uniform(jax.random.fold_in(own, dim), (shards_of,), jnp.float32, smallest / len(pieces), largest / len(pieces)))
        gain = gain * jnp.repeat(draws, dims[dim] // shards_of).reshape([-1 if axis == dim else 1 for axis in range(len(dims))])
    return gain


def rank_bounds(number_of, skew):
    weights = [(1 << 20) // math.isqrt(standing ** skew) + 1 for standing in range(1, number_of + 1)]
    deviation = 1 + sum(weights) // (1 << 30)
    return np.cumsum(np.array([max(1, weight // deviation) for weight in weights]))


def ranked_ids(key, shape, amount, slope):
    grid = rank_bounds(amount, slope)
    lot = jax.random.randint(jax.random.fold_in(key, 1), shape, 0, int(grid[amount - 1]))
    grade = jnp.searchsorted(jnp.asarray(grid, jnp.int32), lot, side="right")
    return jax.random.permutation(jax.random.fold_in(key, 2), amount)[grade].astype(jnp.int32)


def normal_values(stream_key, shape, deviation, limit, shards=(), kind=jnp.bfloat16):
    entries = jax.random.normal(stream_key, shape, jnp.float32) * deviation
    if len(shards) > 0:
        entries = shard_levels(stream_key, shape, shards, -0.22, 0.18) * entries
    return jnp.clip(entries, min=-limit, max=limit).astype(kind)


def setup_inputs(seed: int = 0) -> dict:
    key_list = jax.random.split(jax.random.key(seed), 19)
    embedded = normal_values(key_list[0], (TOKENS, D), 1.0, 6.0, ((0, 32),))
    ids_two = place_ends(ranked_ids(key_list[1], (TOKENS,), TABLE_ROWS, 2), jax.random.fold_in(key_list[1], 3), 0, TABLE_ROWS - 1).astype(jnp.int32)
    ids_three = place_ends(ranked_ids(key_list[2], (TOKENS,), TABLE_ROWS, 2), jax.random.fold_in(key_list[2], 3), 0, TABLE_ROWS - 1).astype(jnp.int32)
    parents = draw_parents(jax.random.fold_in(key_list[18], 71), 0)
    table_two = normal_values(key_list[4], (TABLE_ROWS, NG), 1.0, 6.0, ((0, 8), (1, 4)), jnp.float32)
    table_three = normal_values(key_list[5], (TABLE_ROWS, NG), 1.0, 6.0, ((0, 8), (1, 4)), jnp.float32)
    w_two = normal_values(key_list[6], (NG, D), NG ** -0.5, 0.4375, ((0, 4), (1, 8)), jnp.float32)
    w_three = normal_values(key_list[7], (NG, D), NG ** -0.5, 0.4375, ((0, 4), (1, 8)), jnp.float32)
    norm_attn = jnp.clip(1.0 + 0.1 * jax.random.normal(key_list[8], (D,), jnp.float32), 0.5, 1.5)
    w_query = normal_values(key_list[9], (D, D), D ** -0.5, 0.21875, ((0, 8), (1, 4)), jnp.float32)
    w_key = normal_values(key_list[10], (D, D), D ** -0.5, 0.21875, ((0, 8), (1, 4)), jnp.float32)
    w_value = normal_values(key_list[11], (D, D), D ** -0.5, 0.21875, ((0, 8), (1, 4)), jnp.float32)
    w_output = normal_values(key_list[12], (D, D), (D // 16) ** -0.5, 0.875, ((0, 4), (1, 8)), jnp.float32)
    norm_ffn = jnp.clip(1.0 + 0.1 * jax.random.normal(key_list[13], (D,), jnp.float32), 0.5, 1.5)
    w_gate = normal_values(key_list[14], (D, FF), D ** -0.5, 0.21875, ((0, 8), (1, 4)), jnp.float32)
    w_up = normal_values(key_list[15], (D, FF), D ** -0.5, 0.21875, ((0, 8), (1, 4)), jnp.float32)
    w_down = normal_values(key_list[16], (FF, D), FF ** -0.5, 0.125, ((0, 4), (1, 8)), jnp.float32)
    cotangent = normal_values(key_list[17], (TOKENS, D), 1.0, 6.0, ((0, 32),))
    return {"embedded": embedded, "ids_two": ids_two, "ids_three": ids_three, "parents": parents, "table_two": table_two, "table_three": table_three, "w_two": w_two, "w_three": w_three, "norm_attn": norm_attn, "w_query": w_query, "w_key": w_key, "w_value": w_value, "w_output": w_output, "norm_ffn": norm_ffn, "w_gate": w_gate, "w_up": w_up, "w_down": w_down, "cotangent": cotangent}


@jax.custom_vjp
def low(v):
    return lax.optimization_barrier(v.astype(jnp.bfloat16)).astype(jnp.float32)

@jax.custom_vjp
def low_back(v):
    return v

def low_keep(v):
    return (low(v), None)

def low_pass(kept, grad):
    return (grad,)

def back_keep(v):
    return (v, None)

def back_low(kept, grad):
    return (low(grad),)
low.defvjp(low_keep, low_pass)
low_back.defvjp(back_keep, back_low)
epsilon = 1e-05
masked_score = -1e+30
rope_base = 10000.0

def product(left_side, right_side):
    return jnp.dot(left_side, right_side, precision=lax.Precision.HIGHEST)

def rms_norm(hidden, gain_vec):
    return hidden * lax.rsqrt(lax.optimization_barrier(jnp.mean(hidden * hidden, axis=-1, keepdims=True)) + epsilon) * gain_vec

def tree_layout(parents):
    length = parents.shape[0]
    token_index = jnp.arange(length, dtype=jnp.int32)
    trunk_len = 2 * SEG
    in_trunk = token_index < trunk_len
    block_of = jnp.where(in_trunk, 0, (token_index - trunk_len) // SEG + 1).astype(jnp.int32)
    offset = jnp.where(in_trunk, token_index, token_index - trunk_len - (block_of - 1) * SEG)
    position_base = jnp.where(in_trunk, 0, jnp.where(parents == 0, 2 * SEG, 3 * SEG))
    return (block_of, (position_base + offset).astype(jnp.int32), token_index)

def rotary_tables(position):
    half_dim = HD // 2
    frequency = rope_base ** (-(jnp.arange(half_dim, dtype=jnp.float32) * 2.0 / HD))
    angles = position.astype(jnp.float32)[:, None] * frequency[None, :]
    return (jnp.cos(angles), jnp.sin(angles))

def rotate(values, cosine, sine_tab):
    rows_count = values.shape[0]
    shaped = values.reshape(rows_count, -1, HD)
    half_dim = HD // 2
    first_half = shaped[..., :half_dim]
    second_half = shaped[..., half_dim:]
    cosine_wide = cosine[:, None, :]
    sine_wide = sine_tab[:, None, :]
    turned = jnp.concatenate([first_half * cosine_wide - second_half * sine_wide, first_half * sine_wide + second_half * cosine_wide], axis=-1)
    return turned.reshape(rows_count, -1)

def allowed_keys(block_query, parent_query, index_query, block_of, token_index):
    same_block = block_of[None, :] == block_query[:, None]
    causal = token_index[None, :] <= index_query[:, None]
    ancestor = (block_of[None, :] == parent_query[:, None]) | (block_of[None, :] == 0)
    return same_block & causal | jnp.logical_not(same_block) & ancestor

def forward(embed_rows, weight_set, ids_first, ids_second, parents):
    table_two, table_three, w_two, w_three, norm_attn, w_query, w_key, w_value, w_output, norm_ffn, w_gate, w_up, w_down = weight_set
    rows_two = jnp.take(low(table_two), ids_first, axis=0)
    rows_three = jnp.take(low(table_three), ids_second, axis=0)
    ngram = low_back(product(rows_two, low(w_two)) + product(rows_three, low(w_three)))
    resid_one = embed_rows + ngram
    normed = low(rms_norm(resid_one, norm_attn))
    block_of, position, token_index = tree_layout(parents)
    cosine, sine_tab = rotary_tables(position)
    query = low(rotate(low_back(product(normed, low(w_query))), cosine, sine_tab))
    keys_all = low(rotate(low_back(product(normed, low(w_key))), cosine, sine_tab))
    values = low(low_back(product(normed, low(w_value))))
    length = embed_rows.shape[0]
    heads_count = query.shape[1] // HD
    keys3 = keys_all.reshape(length, heads_count, HD)
    values3 = values.reshape(length, heads_count, HD)
    blocks = length // min(512, length)
    block_rows = length // blocks
    score_scale = HD ** (-0.5)

    def attend(block):
        query_block, block_query, parent_query, index_query = block
        scores = low_back(jnp.einsum('qhd,khd->hqk', query_block, keys3, precision=lax.Precision.HIGHEST) * score_scale)
        allowed = allowed_keys(block_query, parent_query, index_query, block_of, token_index)
        scores = jnp.where(allowed[None], scores, masked_score)
        probs = jnp.exp(scores - jax.nn.logsumexp(scores, axis=-1, keepdims=True))
        return jnp.einsum('hqk,khd->qhd', low(probs), values3, precision=lax.Precision.HIGHEST)
    mixed_blocks = lax.map(jax.checkpoint(attend), (query.reshape(blocks, block_rows, heads_count, HD), block_of.reshape(blocks, block_rows), parents.reshape(blocks, block_rows), token_index.reshape(blocks, block_rows)))
    mixed = low(low_back(mixed_blocks.reshape(length, -1)))
    resid_two = resid_one + low_back(product(mixed, low(w_output)))
    normed_two = low(rms_norm(resid_two, norm_ffn))
    gate = low_back(product(normed_two, low(w_gate)))
    upward = low_back(product(normed_two, low(w_up)))
    hidden = low(jax.nn.silu(gate) * upward)
    return resid_two + low_back(product(hidden, low(w_down)))

def reference(embedded, ids_two, ids_three, parents, table_two, table_three, w_two, w_three, norm_attn, w_query, w_key, w_value, w_output, norm_ffn, w_gate, w_up, w_down, cotangent):
    trees = embedded.shape[0] // TREE
    weight_set = (table_two, table_three, w_two, w_three, norm_attn, w_query, w_key, w_value, w_output, norm_ffn, w_gate, w_up, w_down)

    def per_tree(totals, item):
        embed_tree, ids_first, ids_second, parent_tree, cot_tree = item

        def local_forward(embed_rows, weights_in):
            return forward(embed_rows, weights_in, ids_first, ids_second, parent_tree)
        result, pullback = jax.vjp(local_forward, embed_tree.astype(jnp.float32), weight_set)
        grad_embed, grad_weights = pullback(cot_tree.astype(jnp.float32))
        totals = jax.tree.map(lambda running, update: running + update, totals, grad_weights)
        return (totals, (result.astype(jnp.bfloat16), grad_embed.astype(jnp.bfloat16)))
    start_totals = jax.tree.map(jnp.zeros_like, weight_set)
    totals, (outputs, grads) = lax.scan(per_tree, start_totals, (embedded.reshape(trees, TREE, -1), ids_two.reshape(trees, TREE), ids_three.reshape(trees, TREE), parents.reshape(trees, TREE), cotangent.reshape(trees, TREE, -1)))
    g_table_two, g_table_three, g_two, g_three, g_norm_attn, g_query, g_key, g_value, g_output, g_norm_ffn, g_gate, g_up, g_down = totals
    return (outputs.reshape(-1, D), grads.reshape(-1, D), g_table_two, g_table_three, g_two, g_three, g_norm_attn, g_query, g_key, g_value, g_output, g_norm_ffn, g_gate, g_up, g_down)
```

```python
import functools

import jax
import jax.numpy as jnp
from jax import lax
from jax.experimental import pallas as pl
from jax.experimental.pallas import tpu as pltpu
from jax.sharding import PartitionSpec as P

HD = 64
SEG = 128
TILE = 2 * SEG
EPS = 1e-05
MASKED = -1e30
ROPE_BASE = 10000.0
F32 = jnp.float32
BF16 = jnp.bfloat16
VMEM = pltpu.VMEM


def xor_tensor(value, step):
    return lax.ppermute(value, "tensor", [(i, i ^ step) for i in range(4)])


def xor_dp(value, step, count):
    return lax.ppermute(value, "dp", [(i, i ^ step) for i in range(count)])


def gather_tensor(value):
    far = xor_tensor(value, 2)
    near = xor_tensor(value, 1)
    return [value, near, far, xor_tensor(far, 1)]


def add_round(one, two):
    return (one.astype(F32) + two.astype(F32)).astype(BF16)


def scatter_tensor(slots):
    three = xor_tensor(slots[3], 1)
    one = xor_tensor(slots[1], 1)
    far = xor_tensor(add_round(slots[2], three), 2)
    return slots[0].astype(F32) + one.astype(F32) + far.astype(F32)


def gather_dp(value, count, gate=None):
    if gate is not None:
        value, _ = lax.optimization_barrier((value, gate))
    zs = [value] + [xor_dp(value, step, count) for step in (2, 4, 6)]
    pieces = []
    for piece in zs:
        pieces += [piece, xor_dp(piece, 1, count)]
    return pieces


def scatter_dp(value, count):
    if count != 8:
        return lax.psum_scatter(
            value.astype(F32), "dp", scatter_dimension=0, tiled=True
        ).reshape(value.shape[1:])
    own = lax.axis_index("dp")
    y, z = own % 2, own // 2
    pairs = value.reshape((4, 2) + value.shape[1:])
    away = lax.dynamic_index_in_dim(pairs, 1 - y, 1, keepdims=False)
    keep = lax.dynamic_index_in_dim(pairs, y, 1, keepdims=False)
    both = add_round(keep, xor_dp(away, 1, count))
    total = lax.dynamic_index_in_dim(both, z, 0, keepdims=False).astype(F32)
    for j in (1, 2, 3):
        part = lax.dynamic_index_in_dim(both, z ^ j, 0, keepdims=False)
        total = total + xor_dp(part, 2 * j, count).astype(F32)
    return total


def assemble_kernel(count, turn, keep, info, *refs):
    pieces, out = refs[:count], refs[count]
    rows = pieces[0].shape[0]
    whole_ref = refs[count + 1] if turn else out
    for i in range(count):
        place = pl.ds(pl.multiple_of((info[1] ^ i) * rows, 16), rows)
        whole_ref[place, :] = pieces[i][...]
    if turn:
        out[...] = whole_ref[...].T[:keep, :]


def assemble(info, pieces, turn, block=0, keep=None):
    count = len(pieces)
    rows, lanes = pieces[0].shape
    if keep is None:
        keep, width = lanes, lanes
    else:
        width = SEG
    shape = (keep, count * rows) if turn else (count * rows, width)
    return pl.pallas_call(
        functools.partial(assemble_kernel, count, turn, keep),
        grid_spec=pltpu.PrefetchScalarGridSpec(
            num_scalar_prefetch=1,
            grid=(1,),
            in_specs=[pl.BlockSpec((rows, width), lambda *_: (0, block))] * count,
            out_specs=pl.BlockSpec(shape, lambda *_: (0, 0)),
            scratch_shapes=[VMEM((count * rows, width), BF16)] if turn else [],
        ),
        out_shape=jax.ShapeDtypeStruct(shape, BF16),
        name="assemble",
    )(info, *pieces)


def nn(a, b):
    return lax.dot_general(a, b, (((1,), (0,)), ((), ())), preferred_element_type=F32)


def nt(a, b):
    return lax.dot_general(a, b, (((1,), (1,)), ((), ())), preferred_element_type=F32)


def tn(a, b):
    return lax.dot_general(a, b, (((0,), (0,)), ((), ())), preferred_element_type=F32)


def lookup_kernel(owners, width, own_rows, start, *refs):
    info, ids = refs[0], refs[1]
    count = len(owners)
    pieces = refs[2 : 2 + count]
    prior = None if start else refs[2 + count]
    out = refs[-1]
    for half in range(2):
        lanes = slice(half * width, (half + 1) * width)
        if start:
            out[lanes, :] = jnp.zeros((width, out.shape[1]), BF16)
        else:
            out[lanes, :] = prior[lanes, :]
    for which in range(count):
        for half in range(2):
            wanted = ids[half : half + 1, :] - (info[1] ^ owners[which]) * own_rows

            def chunk(c, total):
                first = pl.multiple_of(c * TILE, TILE)
                rows = lax.broadcasted_iota(jnp.int32, (TILE, wanted.shape[1]), 0) + first
                hot = (rows == wanted).astype(F32).astype(BF16)
                part = pieces[which][half * width : (half + 1) * width, pl.ds(first, TILE)]
                return total + nn(part, hot)

            total = lax.fori_loop(
                0, own_rows // TILE, chunk, jnp.zeros((width, wanted.shape[1]), F32)
            )
            rows = slice(half * width, (half + 1) * width)
            out[rows, :] = (out[rows, :].astype(F32) + total).astype(BF16)


def lookup(info, pieces, owners, own_rows, ids, prior):
    count = len(pieces)
    width = pieces[0].shape[0] // 2
    operands = [info, ids, *pieces]
    specs = [pl.BlockSpec(memory_space=pltpu.SMEM)] + [pl.BlockSpec(memory_space=VMEM)] * (
        1 + count
    )
    if prior is not None:
        operands.append(prior)
        specs.append(pl.BlockSpec(memory_space=VMEM))
    return pl.pallas_call(
        functools.partial(lookup_kernel, tuple(owners), width, own_rows, prior is None),
        out_shape=jax.ShapeDtypeStruct((2 * width, ids.shape[1]), BF16),
        in_specs=specs,
        out_specs=pl.BlockSpec(memory_space=VMEM),
        name="lookup",
    )(*operands)


def spread_kernel(count, width, start, *refs):
    base = (refs[0][1] * refs[-1].shape[1]).astype(F32)
    pieces = refs[1 : 1 + count]
    prior = None if start else refs[1 + count]
    out = refs[-1]
    own_rows = out.shape[1]

    def chunk(c, carry):
        first = pl.multiple_of(c * TILE, TILE)
        rows = (
            lax.broadcasted_iota(jnp.int32, (TILE, pieces[0].shape[1]), 0).astype(F32)
            + base
            + first.astype(F32)
        )
        for half in range(2):
            lanes = slice(half * width, (half + 1) * width)
            total = (
                jnp.zeros((width, TILE), F32) if start else prior[lanes, pl.ds(first, TILE)]
            )
            for piece in pieces:
                digits = piece[2 * width : 2 * width + 16, :].astype(F32)
                ids = digits[2 * half : 2 * half + 1] * 256.0 + digits[2 * half + 1 : 2 * half + 2]
                hot = (rows == ids).astype(F32).astype(BF16)
                total = total + nt(piece[lanes, :], hot)
            out[lanes, pl.ds(first, TILE)] = total
        return carry

    lax.fori_loop(0, own_rows // TILE, chunk, 0)


def spread(info, pieces, own_rows, width, prior):
    count = len(pieces)
    operands = [info, *pieces]
    specs = [pl.BlockSpec(memory_space=pltpu.SMEM)] + [pl.BlockSpec(memory_space=VMEM)] * count
    if prior is not None:
        operands.append(prior)
        specs.append(pl.BlockSpec(memory_space=VMEM))
    return pl.pallas_call(
        functools.partial(spread_kernel, count, width, prior is None),
        out_shape=jax.ShapeDtypeStruct((2 * width, own_rows), F32),
        in_specs=specs,
        out_specs=pl.BlockSpec(memory_space=VMEM),
        name="spread",
    )(*operands)


def rope_into(out, row, values, cosine, sine, scale):
    half = HD // 2
    one, two = values[:half], values[half:]
    out[row : row + half, :] = (one * cosine - two * sine).astype(BF16) * scale
    out[row + half : row + HD, :] = (one * sine + two * cosine).astype(BF16) * scale


def key_offset(parent):
    return pl.multiple_of(jnp.where(parent > 0, parent + 1, 0) * SEG, SEG)


def front_kernel(
    par,
    row0,
    row1,
    row2,
    row3,
    up0,
    up1,
    up2,
    up3,
    emb,
    wqkv,
    gain,
    cos_ref,
    sin_ref,
    resid,
    normed,
    qkv,
    mixed,
    lse,
    keys,
    vals,
):
    tile = pl.program_id(0)
    rows = jnp.concatenate([row0[...], row1[...], row2[...], row3[...]], axis=0)
    ups = jnp.concatenate([up0[...], up1[...], up2[...], up3[...]], axis=0)
    hidden = emb[...].astype(F32) + tn(rows, ups)
    resid[...] = hidden
    rate = lax.rsqrt(jnp.mean(hidden * hidden, axis=-1, keepdims=True) + EPS)
    norm = (hidden * rate * gain[...]).astype(BF16)
    normed[...] = norm
    proj = nt(wqkv[...], norm)
    cosine, sine = cos_ref[...], sin_ref[...]
    width = keys.shape[0]
    heads = width // HD
    for h in range(heads):
        rope_into(qkv, h * HD, proj[h * HD : (h + 1) * HD], cosine, sine, BF16(HD**-0.5))
        low = width + h * HD
        rope_into(qkv, low, proj[low : low + HD], cosine, sine, BF16(1.0))
    qkv[2 * width :, :] = proj[2 * width :].astype(BF16)
    place = pl.ds(pl.multiple_of(tile * TILE, TILE), TILE)
    keys[:, place] = qkv[width : 2 * width, :]
    vals[:, place] = qkv[2 * width :, :]

    def finish(h, lanes, scores, value):
        top = jnp.max(scores, axis=0, keepdims=True)
        weights = jnp.exp(scores - top)
        total = jnp.sum(weights, axis=0, keepdims=True)
        got = nn(value, weights.astype(BF16))
        mixed[h * HD : (h + 1) * HD, lanes] = (got * (1.0 / total)).astype(BF16)
        lse[h : h + 1, lanes] = top + jnp.log(total)

    @pl.when(tile == 0)
    def _():
        key_at = lax.broadcasted_iota(jnp.int32, (TILE, TILE), 0)
        query_at = lax.broadcasted_iota(jnp.int32, (TILE, TILE), 1)
        for h in range(heads):
            hs = slice(h * HD, (h + 1) * HD)
            scores = tn(keys[hs, 0:TILE], qkv[hs, :])
            scores = jnp.where(key_at <= query_at, scores, MASKED)
            finish(h, slice(0, TILE), scores, vals[hs, 0:TILE])

    @pl.when(tile > 0)
    def _():
        key_at = lax.broadcasted_iota(jnp.int32, (4 * SEG, SEG), 0)
        query_at = lax.broadcasted_iota(jnp.int32, (4 * SEG, SEG), 1)
        for half in range(2):
            parent = par[2 + 2 * tile + half]
            mine = pl.ds(pl.multiple_of(tile * TILE + half * SEG, SEG), SEG)
            theirs = pl.ds(key_offset(parent), SEG)
            limit = jnp.where(parent > 0, 4 * SEG, 3 * SEG)
            seen = (key_at < TILE) | ((key_at - TILE <= query_at) & (key_at < 3 * SEG))
            seen = seen | ((key_at >= 3 * SEG) & (key_at < limit))
            lanes = slice(half * SEG, (half + 1) * SEG)
            for h in range(heads):
                hs = slice(h * HD, (h + 1) * HD)
                key = jnp.concatenate([keys[hs, 0:TILE], keys[hs, mine], keys[hs, theirs]], axis=1)
                value = jnp.concatenate(
                    [vals[hs, 0:TILE], vals[hs, mine], vals[hs, theirs]], axis=1
                )
                scores = jnp.where(seen, tn(key, qkv[hs, lanes]), MASKED)
                finish(h, lanes, scores, value)


def whole(shape):
    return pl.BlockSpec(shape, lambda *_: (0,) * len(shape))


def front(par, rows, ups, emb, wqkvo, gain, cosine, sine):
    length, dim = emb.shape
    width = wqkvo.shape[0] // 4
    ng = rows[0].shape[0]
    tall = lambda r, _: (r, 0)
    wide = lambda r, _: (0, r)
    return pl.pallas_call(
        front_kernel,
        grid_spec=pltpu.PrefetchScalarGridSpec(
            num_scalar_prefetch=1,
            grid=(length // TILE,),
            in_specs=[pl.BlockSpec((ng, TILE), wide)] * 4
            + [whole((ng, dim))] * 4
            + [
                pl.BlockSpec((TILE, dim), tall),
                whole((3 * width, dim)),
                whole((1, dim)),
                pl.BlockSpec((HD // 2, TILE), wide),
                pl.BlockSpec((HD // 2, TILE), wide),
            ],
            out_specs=[
                pl.BlockSpec((TILE, dim), tall),
                pl.BlockSpec((TILE, dim), tall),
                pl.BlockSpec((3 * width, TILE), wide),
                pl.BlockSpec((width, TILE), wide),
                pl.BlockSpec((8, TILE), wide),
            ],
            scratch_shapes=[VMEM((width, length), BF16), VMEM((width, length), BF16)],
        ),
        out_shape=[
            jax.ShapeDtypeStruct((length, dim), F32),
            jax.ShapeDtypeStruct((length, dim), BF16),
            jax.ShapeDtypeStruct((3 * width, length), BF16),
            jax.ShapeDtypeStruct((width, length), BF16),
            jax.ShapeDtypeStruct((8, length), F32),
        ],
        name="front",
    )(par, *rows, *ups, emb, wqkvo, gain, cosine, sine)


def middle_kernel(
    who,
    mix0,
    mix1,
    mix2,
    mix3,
    out0,
    out1,
    out2,
    out3,
    resid,
    gain,
    ffn,
    cot,
    feed,
    resid_own,
    normed,
    hidden,
    grads,
    grad_res,
    grad_mix,
    grad_gain,
):
    tile = pl.program_id(0)
    units = hidden.shape[1]
    outs = jnp.concatenate([out0[...], out1[...], out2[...], out3[...]], axis=0)
    mix = jnp.concatenate([mix0[...], mix1[...], mix2[...], mix3[...]], axis=0)
    res = resid[...] + tn(mix, outs)

    @pl.when(tile == who[0])
    def _():
        resid_own[...] = res

    rate = lax.rsqrt(jnp.mean(res * res, axis=-1, keepdims=True) + EPS)
    norm = (res * rate * gain[...]).astype(BF16)
    normed[...] = norm
    gate = nn(norm, ffn[:, :units])
    upward = nn(norm, ffn[:, units : 2 * units])
    sig = 1.0 / (1.0 + jnp.exp(-gate))
    silu = gate * sig
    hid = (silu * upward).astype(BF16)
    hidden[...] = hid
    feed[0] = nt(hid, ffn[:, 2 * units :]).astype(BF16)
    back = nn(cot[...], ffn[:, 2 * units :])
    grad_gate = (back * upward * sig * (1.0 + gate * (1.0 - sig))).astype(BF16)
    grad_up = (back * silu).astype(BF16)
    grads[:, :units] = grad_gate
    grads[:, units:] = grad_up
    pulled = nt(grad_gate, ffn[:, :units]) + nt(grad_up, ffn[:, units : 2 * units])
    scaled = pulled * gain[...]
    dots = jnp.mean(scaled * res, axis=-1, keepdims=True)
    part = rate * scaled - res * (rate * rate * rate * dots) + 0.25 * cot[...].astype(F32)
    part = part.astype(BF16)
    grad_res[...] = part
    grad_mix[...] = nt(outs, part).astype(BF16)
    gained = jnp.sum(pulled * res * rate, axis=0, keepdims=True)

    @pl.when(tile == 0)
    def _():
        grad_gain[...] = gained

    @pl.when(tile > 0)
    def _():
        grad_gain[...] += gained


def middle(who, mixes, outs, resid, gain, ffn, cot):
    length, dim = resid.shape
    width = mixes[0].shape[0]
    units = ffn.shape[1] // 3
    tiles = length // TILE
    tall = lambda r, _: (r, 0)
    wide = lambda r, _: (0, r)
    return pl.pallas_call(
        middle_kernel,
        grid_spec=pltpu.PrefetchScalarGridSpec(
            num_scalar_prefetch=1,
            grid=(tiles,),
            in_specs=[pl.BlockSpec((width, TILE), wide)] * 4
            + [whole((width, dim))] * 4
            + [
                pl.BlockSpec((TILE, dim), tall),
                whole((1, dim)),
                whole((dim, 3 * units)),
                pl.BlockSpec((TILE, dim), tall),
            ],
            out_specs=[
                pl.BlockSpec((1, TILE, dim), lambda r, who: (r ^ who[0], 0, 0)),
                whole((TILE, dim)),
                pl.BlockSpec((TILE, dim), tall),
                pl.BlockSpec((TILE, units), tall),
                pl.BlockSpec((TILE, 2 * units), tall),
                pl.BlockSpec((TILE, dim), tall),
                pl.BlockSpec((4 * width, TILE), wide),
                whole((1, dim)),
            ],
        ),
        out_shape=[
            jax.ShapeDtypeStruct((tiles, TILE, dim), BF16),
            jax.ShapeDtypeStruct((TILE, dim), F32),
            jax.ShapeDtypeStruct((length, dim), BF16),
            jax.ShapeDtypeStruct((length, units), BF16),
            jax.ShapeDtypeStruct((length, 2 * units), BF16),
            jax.ShapeDtypeStruct((length, dim), BF16),
            jax.ShapeDtypeStruct((4 * width, length), BF16),
            jax.ShapeDtypeStruct((1, dim), F32),
        ],
        name="middle",
    )(who, *mixes, *outs, resid, gain, ffn, cot)


def unrope_into(out, row, values, cosine, sine):
    half = HD // 2
    one, two = values[:half], values[half:]
    out[row : row + half, :] = (one * cosine + two * sine).astype(BF16)
    out[row + half : row + HD, :] = (two * cosine - one * sine).astype(BF16)


def back_kernel(
    info,
    qkv,
    gmix,
    mixed,
    lse,
    grad_res,
    resid,
    gain,
    wqkv,
    up0,
    up1,
    up2,
    up3,
    cos_ref,
    sin_ref,
    gproj,
    grad_slots,
    grad_emb,
    grad_rows,
    grad_gain,
    keys_sum,
    vals_sum,
    query_sum,
):
    step = pl.program_id(0)
    tile = pl.num_programs(0) - 1 - step
    width = gmix.shape[0]
    heads = width // HD

    @pl.when(step == 0)
    def _():
        keys_sum[...] = jnp.zeros_like(keys_sum)
        vals_sum[...] = jnp.zeros_like(vals_sum)

    base = pl.multiple_of(tile * TILE, TILE)

    def pull(h, lanes, query, key, value, seen):
        hs = slice(h * HD, (h + 1) * HD)
        grad = gmix[hs, lanes]
        delta = jnp.sum(grad.astype(F32) * mixed[hs, lanes].astype(F32), axis=0, keepdims=True)
        scores = jnp.where(seen, tn(key, query), MASKED)
        probs = jnp.exp(scores - lse[h : h + 1, lanes])
        dval = nt(grad, probs.astype(BF16))
        dscore = (probs * (tn(value, grad) - delta)).astype(BF16)
        query_sum[hs, lanes] = nn(key, dscore) * HD**-0.5
        return nt(query, dscore), dval

    @pl.when(tile == 0)
    def _():
        key_at = lax.broadcasted_iota(jnp.int32, (TILE, TILE), 0)
        query_at = lax.broadcasted_iota(jnp.int32, (TILE, TILE), 1)
        seen = key_at <= query_at
        for h in range(heads):
            hs = slice(h * HD, (h + 1) * HD)
            key = qkv[width + h * HD : width + (h + 1) * HD, 0:TILE]
            value = qkv[2 * width + h * HD : 2 * width + (h + 1) * HD, 0:TILE]
            dkey, dval = pull(h, slice(0, TILE), qkv[hs, 0:TILE], key, value, seen)
            keys_sum[hs, 0:TILE] += dkey
            vals_sum[hs, 0:TILE] += dval

    @pl.when(tile > 0)
    def _():
        key_at = lax.broadcasted_iota(jnp.int32, (4 * SEG, SEG), 0)
        query_at = lax.broadcasted_iota(jnp.int32, (4 * SEG, SEG), 1)
        for half in range(2):
            parent = info[2 + 2 * tile + half]
            mine = pl.ds(pl.multiple_of(base + half * SEG, SEG), SEG)
            theirs = pl.ds(key_offset(parent), SEG)
            limit = jnp.where(parent > 0, 4 * SEG, 3 * SEG)
            seen = (key_at < TILE) | ((key_at - TILE <= query_at) & (key_at < 3 * SEG))
            seen = seen | ((key_at >= 3 * SEG) & (key_at < limit))
            lanes = slice(half * SEG, (half + 1) * SEG)
            for h in range(heads):
                hs = slice(h * HD, (h + 1) * HD)
                ks = slice(width + h * HD, width + (h + 1) * HD)
                vs = slice(2 * width + h * HD, 2 * width + (h + 1) * HD)
                key = jnp.concatenate([qkv[ks, 0:TILE], qkv[ks, mine], qkv[ks, theirs]], axis=1)
                value = jnp.concatenate([qkv[vs, 0:TILE], qkv[vs, mine], qkv[vs, theirs]], axis=1)
                dkey, dval = pull(h, lanes, qkv[hs, mine], key, value, seen)
                for total, part in ((keys_sum, dkey), (vals_sum, dval)):
                    total[hs, 0:TILE] += part[:, 0:TILE]
                    total[hs, mine] += part[:, TILE : 3 * SEG]
                    total[hs, theirs] += part[:, 3 * SEG :]

    cosine, sine = cos_ref[...], sin_ref[...]
    place = pl.ds(base, TILE)
    for h in range(heads):
        hs = slice(h * HD, (h + 1) * HD)
        unrope_into(gproj, h * HD, query_sum[hs, :], cosine, sine)
        unrope_into(gproj, width + h * HD, keys_sum[hs, place], cosine, sine)
    gproj[2 * width :, :] = vals_sum[:, place].astype(BF16)
    pulled = tn(gproj[...], wqkv[...])
    hidden = resid[...]
    rate = lax.rsqrt(jnp.mean(hidden * hidden, axis=-1, keepdims=True) + EPS)
    scaled = pulled * gain[...]
    dots = jnp.mean(scaled * hidden, axis=-1, keepdims=True)
    part = grad_res[...].astype(F32) + rate * scaled - hidden * (rate * rate * rate * dots)
    part = part.astype(BF16)
    grad_slots[0] = part
    grad_emb[...] = part
    ups = jnp.concatenate([up0[...], up1[...], up2[...], up3[...]], axis=0)
    grad_rows[...] = nt(ups, part).astype(BF16)
    gained = jnp.sum(pulled * hidden * rate, axis=0, keepdims=True)

    @pl.when(step == 0)
    def _():
        grad_gain[...] = gained

    @pl.when(step > 0)
    def _():
        grad_gain[...] += gained


def back(info, qkv, gmix, mixed, lse, grad_res, resid, gain, wqkvo, ups, cosine, sine):
    length, dim = resid.shape
    width = gmix.shape[0]
    ng = ups[0].shape[0]
    tiles = length // TILE
    last = tiles - 1
    tall = lambda r, _: (last - r, 0)
    wide = lambda r, _: (0, last - r)
    return pl.pallas_call(
        back_kernel,
        grid_spec=pltpu.PrefetchScalarGridSpec(
            num_scalar_prefetch=1,
            grid=(tiles,),
            in_specs=[
                whole((3 * width, length)),
                pl.BlockSpec((width, TILE), wide),
                pl.BlockSpec((width, TILE), wide),
                pl.BlockSpec((8, TILE), wide),
                pl.BlockSpec((TILE, dim), tall),
                pl.BlockSpec((TILE, dim), tall),
                whole((1, dim)),
                whole((3 * width, dim)),
            ]
            + [whole((ng, dim))] * 4
            + [
                pl.BlockSpec((HD // 2, TILE), wide),
                pl.BlockSpec((HD // 2, TILE), wide),
            ],
            out_specs=[
                pl.BlockSpec((3 * width, TILE), wide),
                pl.BlockSpec((1, TILE, dim), lambda r, info: ((last - r) ^ info[0], 0, 0)),
                pl.BlockSpec((TILE, dim), tall),
                pl.BlockSpec((4 * ng, TILE), wide),
                whole((1, dim)),
            ],
            scratch_shapes=[
                VMEM((width, length), F32),
                VMEM((width, length), F32),
                VMEM((width, TILE), F32),
            ],
        ),
        out_shape=[
            jax.ShapeDtypeStruct((3 * width, length), BF16),
            jax.ShapeDtypeStruct((tiles, TILE, dim), BF16),
            jax.ShapeDtypeStruct((length, dim), BF16),
            jax.ShapeDtypeStruct((4 * ng, length), BF16),
            jax.ShapeDtypeStruct((1, dim), F32),
        ],
        name="back",
    )(info, qkv, gmix, mixed, lse, grad_res, resid, gain, wqkvo, *ups, cosine, sine)


def rotary(parents):
    length = parents.shape[0]
    token = jnp.arange(length, dtype=jnp.int32)
    trunk = 2 * SEG
    inside = token < trunk
    block = jnp.where(inside, 0, (token - trunk) // SEG + 1)
    offset = jnp.where(inside, token, token - trunk - (block - 1) * SEG)
    position = jnp.where(inside, 0, jnp.where(parents == 0, 2 * SEG, 3 * SEG)) + offset
    half = HD // 2
    frequency = ROPE_BASE ** (-(jnp.arange(half, dtype=F32) * 2.0 / HD))
    angles = frequency[:, None] * position.astype(F32)[None, :]
    return jnp.cos(angles), jnp.sin(angles)


def natural(slots, index):
    count = slots.shape[0]
    return jnp.concatenate(
        [lax.dynamic_index_in_dim(slots, r ^ index, 0, keepdims=False) for r in range(count)],
        axis=0,
    )


def shards(
    dp,
    embedded,
    ids_two,
    ids_three,
    parents,
    table_two,
    table_three,
    w_two,
    w_three,
    norm_attn,
    w_query,
    w_key,
    w_value,
    w_output,
    norm_ffn,
    w_gate,
    w_up,
    w_down,
    cotangent,
):
    own_d = lax.axis_index("dp")
    own_t = lax.axis_index("tensor")
    own_rows, ng = table_two.shape
    rows, dim = embedded.shape
    width = w_query.shape[1]
    units = w_gate.shape[1]
    own_dim = w_query.shape[0]
    gain_one = norm_attn.reshape(1, dim)
    gain_two = norm_ffn.reshape(1, dim)

    tables = jnp.concatenate([table_two.astype(BF16).T, table_three.astype(BF16).T], axis=0)
    small = jnp.concatenate([w_two.astype(BF16).T, w_three.astype(BF16).T], axis=1)
    attn_pack = jnp.concatenate(
        [
            w_query.astype(BF16),
            w_key.astype(BF16),
            w_value.astype(BF16),
            w_output.astype(BF16).T,
        ],
        axis=1,
    )
    ffn_pack = jnp.concatenate(
        [w_gate.astype(BF16), w_up.astype(BF16), w_down.astype(BF16).T], axis=1
    )
    ids = jnp.stack([ids_two, ids_three])
    info = jnp.concatenate(
        [jnp.stack([own_t, own_d]).astype(jnp.int32), parents.reshape(-1, SEG)[:, 0]]
    )

    token_slots = gather_tensor(jnp.stack([embedded, cotangent]))
    token_slots = jnp.stack(token_slots)
    emb_all = natural(token_slots[:, 0], own_t)
    cot_all = natural(token_slots[:, 1], own_t)

    if dp == 8:
        pad = jnp.zeros((own_dim, SEG - 2 * ng), BF16)
        first = jnp.concatenate([tables, small, pad], axis=1)
        pieces = gather_dp(first, dp)
        attn_pieces = gather_dp(attn_pack, dp, tuple(pieces[0::2]))
        ffn_pieces = gather_dp(ffn_pack, dp, tuple(attn_pieces[0::2]))
        got = None
        for j in range(0, dp, 2):
            got = lookup(info, pieces[j : j + 2], (j, j + 1), own_rows, ids, got)
        ups = assemble(info, pieces, True, own_rows // SEG, 2 * ng)
        wqkvo = assemble(info, attn_pieces, True)
        ffn_w = assemble(info, ffn_pieces, False)
    else:
        every = lax.all_gather(tables, "dp", axis=0)
        ups = lax.all_gather(small, "dp", axis=0, tiled=True).T
        wqkvo = lax.all_gather(attn_pack, "dp", axis=0, tiled=True).T
        ffn_w = lax.all_gather(ffn_pack, "dp", axis=0, tiled=True)

        def take(i, so_far):
            piece = lax.dynamic_index_in_dim(every, i, 0, keepdims=False)
            at = jnp.stack([own_t, i]).astype(jnp.int32)
            return lookup(at, [piece], (0,), own_rows, ids, so_far)

        got = lax.fori_loop(0, dp, take, jnp.zeros((2 * ng, ids.shape[1]), BF16))

    ups = gather_tensor(ups)
    outs = gather_tensor(wqkvo[3 * width :])
    row_sets = gather_tensor(got)

    cosine, sine = rotary(parents)
    resid, normed, qkv, mixed, lse = front(
        info, row_sets, ups, emb_all, wqkvo, gain_one, cosine, sine
    )
    mixes = gather_tensor(mixed)
    feed, resid_own, normed_two, hidden, grads, grad_res, grad_mix, gain_part_two = middle(
        info, mixes, outs, resid, gain_two, ffn_w, cot_all
    )
    gmix = scatter_tensor([grad_mix[k * width : (k + 1) * width] for k in range(4)]).astype(BF16)
    feed, grad_res_late, _ = lax.optimization_barrier((feed, grad_res, gmix))
    output = (resid_own + scatter_tensor([feed[k] for k in range(4)])).astype(BF16)
    out_parts = [nn(mixes[k], grad_res_late).astype(BF16) for k in range(4)]
    out_grad = scatter_tensor(out_parts).astype(BF16)

    gate_up = tn(normed_two, grads).astype(BF16)
    down = tn(cot_all, hidden).astype(BF16)
    ffn_grads = jnp.concatenate([gate_up, down], axis=1).reshape(dp, own_dim, 3 * units)
    ffn_total = scatter_dp(ffn_grads, dp)

    gproj, slots, grad_emb, grad_rows, gain_part_one = back(
        info, qkv, gmix, mixed, lse, grad_res, resid, gain_one, wqkvo, ups, cosine, sine
    )
    row_total = scatter_tensor([grad_rows[k * 2 * ng : (k + 1) * 2 * ng] for k in range(4)])
    slots, grad_emb, _ = lax.optimization_barrier((slots, grad_emb, row_total))
    embed_grad = scatter_tensor([slots[k] for k in range(4)]).astype(BF16)

    digits = jnp.stack([ids_two // 256, ids_two % 256, ids_three // 256, ids_three % 256])
    digits = jnp.concatenate([digits.astype(BF16), jnp.zeros((12, digits.shape[1]), BF16)])
    row_pack = jnp.concatenate([row_total.astype(BF16), digits], axis=0)
    if dp == 8:
        row_pieces = gather_dp(row_pack, dp)
        table_grad = None
        for j in range(0, dp, 2):
            table_grad = spread(info, row_pieces[j : j + 2], own_rows, ng, table_grad)
    else:
        every = lax.all_gather(row_pack, "dp", axis=0)

        def put(i, so_far):
            piece = lax.dynamic_index_in_dim(every, i, 0, keepdims=False)
            return spread(info, [piece], own_rows, ng, so_far)

        table_grad = lax.fori_loop(0, dp, put, jnp.zeros((2 * ng, own_rows), F32))

    up_parts = [nn(row_sets[k], grad_emb).astype(BF16) for k in range(4)]
    up_grad = scatter_tensor(up_parts).astype(BF16)
    proj_grad = lax.dot_general(
        normed, gproj, (((0,), (1,)), ((), ())), preferred_element_type=F32
    ).astype(BF16)
    attn_grads = jnp.concatenate([proj_grad, out_grad.T, up_grad.T], axis=1)
    attn_total = scatter_dp(attn_grads.reshape(dp, own_dim, attn_grads.shape[1]), dp)

    gains = jnp.concatenate([gain_part_one, gain_part_two], axis=0)
    gains = gains + xor_tensor(gains, 1)
    gains = gains + xor_tensor(gains, 2)
    step = 1
    while step < dp:
        gains = gains + xor_dp(gains, step, dp)
        step *= 2

    return (
        output,
        embed_grad,
        table_grad[:ng].T,
        table_grad[ng:].T,
        attn_total[:, 4 * width : 4 * width + ng].T,
        attn_total[:, 4 * width + ng :].T,
        gains[0],
        attn_total[:, :width],
        attn_total[:, width : 2 * width],
        attn_total[:, 2 * width : 3 * width],
        attn_total[:, 3 * width : 4 * width].T,
        gains[1],
        ffn_total[:, :units],
        ffn_total[:, units : 2 * units],
        ffn_total[:, 2 * units :].T,
    )


def solution(mesh):
    tokens = P(("dp", "tensor"), None)
    down, across = P("dp", "tensor"), P("tensor", "dp")
    in_specs = (
        (tokens, P("dp"), P("dp"), P("dp"), down, down, across, across, P())
        + (down, down, down, across, P(), down, down, across, tokens)
    )
    out_specs = (
        (tokens, tokens, down, down, across, across, P())
        + (down, down, down, across, P(), down, down, across)
    )
    body = functools.partial(shards, mesh.shape["dp"])
    return jax.shard_map(body, mesh=mesh, in_specs=in_specs, out_specs=out_specs, check_vma=False)
```

```python
import functools

import jax
import jax.numpy as jnp
from jax import lax
from jax.experimental import pallas as pl
from jax.experimental.pallas import tpu as pltpu
from jax.sharding import PartitionSpec as P

HD = 64
SEG = 128
TILE = 2 * SEG
EPS = 1e-05
MASKED = -1e30
ROPE_BASE = 10000.0
F32 = jnp.float32
BF16 = jnp.bfloat16
VMEM = pltpu.VMEM


def xor_tensor(value, step):
    return lax.ppermute(value, "tensor", [(i, i ^ step) for i in range(4)])


def xor_dp(value, step, count):
    return lax.ppermute(value, "dp", [(i, i ^ step) for i in range(count)])


def after(value, *others):
    return lax.optimization_barrier((value,) + others)[0]


def gather_tensor(value):
    far = xor_tensor(value, 2)
    near = xor_tensor(value, 1)
    return [value, near, far, xor_tensor(far, 1)]


def add_round(one, two):
    return (one.astype(F32) + two.astype(F32)).astype(BF16)


def scatter_tensor(stay, leave):
    come = xor_tensor(leave, 1)
    far = xor_tensor(add_round(stay[1], come[1]), 2)
    return stay[0], come[0], far


def total(terms):
    return terms[0].astype(F32) + terms[1].astype(F32) + terms[2].astype(F32)


def double_dp(value):
    zero = jnp.stack([value, xor_dp(value, 4, 8)])
    two = xor_dp(zero, 2, 8)
    return zero, two, xor_dp(zero, 1, 8), xor_dp(two, 1, 8)


DOUBLED = (0, 4, 2, 6, 1, 5, 3, 7)
HALVED = (0, 2, 1, 3)


def halve_first(keep, come):
    return add_round(keep[:2], come[:2]), add_round(keep[2:], come[2:])


def halve_second(stay, come):
    return add_round(stay[0], come[0]), add_round(stay[1], come[1])


def sum_dp(halves, count):
    if count != 8:
        return lax.psum_scatter(halves[0].astype(F32), "dp", scatter_dimension=0, tiled=True)[0]
    away, keep = halves
    stay, leave = halve_first(keep, xor_dp(away, 1, count))
    ours, leave = halve_second(stay, xor_dp(leave, 2, count))
    return ours.astype(F32) + xor_dp(leave, 4, count).astype(F32)


def entries(refs):
    out = []
    for ref in refs:
        out += [ref] if len(ref.shape) == 2 else [ref.at[i] for i in range(ref.shape[0])]
    return out


def place_rows(info, refs, lane, whole_ref):
    for piece, xor in zip(entries(refs), DOUBLED):
        rows = piece.shape[0]
        at = pl.ds(pl.multiple_of((info[1] ^ xor) * rows, 16), rows)
        whole_ref[at, :] = piece[:, lane : lane + whole_ref.shape[1]]


def assemble_kernel(turn, info, *refs):
    pieces, out = refs[:4], refs[4]
    whole_ref = refs[-1] if turn else out
    place_rows(info, pieces, 0, whole_ref)
    if turn:
        out[...] = whole_ref[...].T


def assemble(info, arrays, turn):
    rows, cols = arrays[0].shape[1:]
    shape = (cols, 8 * rows) if turn else (8 * rows, cols)
    return pl.pallas_call(
        functools.partial(assemble_kernel, turn),
        out_shape=jax.ShapeDtypeStruct(shape, BF16),
        in_specs=[pl.BlockSpec(memory_space=pltpu.SMEM)] + [pl.BlockSpec(memory_space=VMEM)] * 4,
        out_specs=pl.BlockSpec(memory_space=VMEM),
        scratch_shapes=[VMEM((8 * rows, cols), BF16)] if turn else [],
        name="assemble",
    )(info, *arrays)


def whole(shape):
    return pl.BlockSpec(shape, lambda *_: (0,) * len(shape))


def nn(a, b):
    return lax.dot_general(a, b, (((1,), (0,)), ((), ())), preferred_element_type=F32)


def nt(a, b):
    return lax.dot_general(a, b, (((1,), (1,)), ((), ())), preferred_element_type=F32)


def tn(a, b):
    return lax.dot_general(a, b, (((0,), (0,)), ((), ())), preferred_element_type=F32)


def pack_first_kernel(two, three, up_two, up_three, out):
    ng, rows = two.shape
    out[:ng, :rows] = two[...].astype(BF16)
    out[ng:, :rows] = three[...].astype(BF16)
    out[:, rows:] = jnp.zeros((2 * ng, SEG), BF16)
    if up_two.shape[1] == 2 * ng:
        small = jnp.concatenate([up_two[...], up_three[...]], axis=0)
        out[:, rows : rows + 2 * ng] = small.T.astype(BF16)


def pack_first(two, three, up_two, up_three):
    ng, rows = two.shape
    return pl.pallas_call(
        pack_first_kernel,
        out_shape=jax.ShapeDtypeStruct((2 * ng, rows + SEG), BF16),
        name="pack_first",
    )(two, three, up_two, up_three)


def pack_kernel(query, key, value, output, gate, up, down, attn, ffn):
    width, units = query.shape[1], gate.shape[1]
    for i, ref in enumerate((query, key, value)):
        attn[:, i * width : (i + 1) * width] = ref[...].astype(BF16)
    attn[:, 3 * width :] = output[...].T.astype(BF16)
    for i, ref in enumerate((gate, up, down)):
        ffn[:, i * units : (i + 1) * units] = ref[...].astype(BF16)


def pack(query, key, value, output, gate, up, down):
    rows, width = query.shape
    return pl.pallas_call(
        pack_kernel,
        out_shape=[
            jax.ShapeDtypeStruct((rows, 4 * width), BF16),
            jax.ShapeDtypeStruct((rows, 3 * gate.shape[1]), BF16),
        ],
        name="pack",
    )(query, key, value, output, gate, up, down)


def split_rows(info, whole_ref, outs, rows):
    if len(outs) == 1:
        for i in range(outs[0].shape[0]):
            outs[0][i] = whole_ref[i * rows : (i + 1) * rows, :]
        return
    for entry, xor in enumerate(HALVED):
        for out, other in zip(outs, (1, 0)):
            at = info[1] ^ (2 * xor + other)
            out[entry] = whole_ref[pl.ds(pl.multiple_of(at * rows, 16), rows), :]


def weigh_kernel(rows, halves, info, cot, hidden, norm, grads, *refs):
    mixes, grad, feed = refs[:4], refs[4], refs[5]
    downs, gates = refs[6 : 6 + halves], refs[6 + halves : 6 + 2 * halves]
    stay, leave, turned, down_whole, gate_whole = refs[6 + 2 * halves :]
    units = hidden.shape[1]
    turned[...] = cot[...].T
    down_whole[:, units:] = nn(turned[...], hidden[...]).astype(BF16)
    turned[...] = norm[...].T
    down_whole[:, :units] = nn(turned[...], grads[:, :units]).astype(BF16)
    split_rows(info, down_whole, downs, rows)
    gate_whole[...] = nn(turned[...], grads[:, units:]).astype(BF16)
    split_rows(info, gate_whole, gates, rows)
    for xor in range(4):
        out, at = (stay, leave)[xor % 2], xor // 2
        out[at, : feed.shape[1]] = feed[2 * (xor % 2) + at]
        out[at, feed.shape[1] :] = nn(mixes[xor][...], grad[...]).astype(BF16)


def weigh(info, cot, hidden, norm, grads, mixes, grad, feed, count, own_dim):
    vm = pl.BlockSpec(memory_space=VMEM)
    dim, length = cot.shape[1], cot.shape[0]
    lead = [4, 4] if count == 8 else [count]
    units = hidden.shape[1]
    shapes = [(n, own_dim, 2 * units) for n in lead]
    shapes += [(n, own_dim, units) for n in lead]
    shapes += [(2, feed.shape[1] + mixes[0].shape[0], dim)] * 2
    got = pl.pallas_call(
        functools.partial(weigh_kernel, own_dim, len(lead)),
        out_shape=[jax.ShapeDtypeStruct(shape, BF16) for shape in shapes],
        in_specs=[pl.BlockSpec(memory_space=pltpu.SMEM)] + [vm] * 10,
        out_specs=[vm] * len(shapes),
        scratch_shapes=[
            VMEM((dim, length), BF16),
            VMEM((dim, 2 * units), BF16),
            VMEM((dim, units), BF16),
        ],
        name="weigh",
    )(info, cot, hidden, norm, grads, *mixes, grad, feed)
    return got[: len(lead)], got[len(lead) : 2 * len(lead)], got[2 * len(lead) :]


def weigh_turned_kernel(rows, info, left, right, extra, *refs):
    outs, whole_ref = refs[:-1], refs[-1]
    wide = nn(right[...], left[...]).astype(BF16)
    whole_ref[...] = jnp.concatenate([wide, extra[...]], axis=0).T
    split_rows(info, whole_ref, outs, rows)


def turn_kernel(rows, info, extra, below, *refs):
    outs, whole_ref = refs[:-1], refs[-1]
    whole_ref[...] = extra[...].T
    split_rows(info, whole_ref, [out.at[:, :rows] for out in outs], rows)
    for out in outs:
        for z in range(out.shape[0]):
            out[z, rows:] = below[...]


def split_call(body, info, operands, count, own_dim, cols, below=0):
    vm = pl.BlockSpec(memory_space=VMEM)
    lead = [4, 4] if count == 8 else [count]
    shapes = [jax.ShapeDtypeStruct((n, own_dim + below, cols), BF16) for n in lead]
    return pl.pallas_call(
        functools.partial(body, own_dim),
        out_shape=shapes,
        in_specs=[pl.BlockSpec(memory_space=pltpu.SMEM)] + [vm] * len(operands),
        out_specs=[vm] * len(shapes),
        scratch_shapes=[VMEM((count * own_dim, cols), BF16)],
        name="split",
    )(info, *operands)


def weigh_turned(info, left, right, extra, count, own_dim):
    cols = right.shape[0] + extra.shape[0]
    return split_call(weigh_turned_kernel, info, [left, right, extra], count, own_dim, cols)


def turn(info, extra, below, count, own_dim):
    return split_call(
        turn_kernel, info, [extra, below], count, own_dim, extra.shape[0], below.shape[0]
    )


def steps(length):
    return lax.broadcasted_iota(jnp.int32, (TILE, SEG), 0).astype(F32).astype(BF16)


def one_hot(places, wanted):
    near = jnp.clip(wanted, -1.0, float(TILE)).astype(BF16)
    parts = [
        jnp.where(places == near[:, c : c + SEG], BF16(1.0), BF16(0.0))
        for c in range(0, wanted.shape[1], SEG)
    ]
    return jnp.concatenate(parts, axis=1)


def lookup_kernel(owners, arrays, width, own_rows, start, end, *refs):
    info, ids = refs[0], refs[1]
    arrays, refs = refs[2 : 2 + arrays], refs[2 + arrays :]
    pieces = entries(arrays)
    count = len(owners)
    at = 0
    if end:
        ups, refs, out, whole_ref = refs[:4], refs[4:-2], refs[-2], refs[-1]
        at = out.shape[1] - ids.shape[1]
        place_rows(info, ups, own_rows, whole_ref)
        out[:, :at] = whole_ref[...].T[: 2 * width]
    else:
        out = refs[-1]
    prior = None if start else refs[0]
    places = steps(TILE)
    for half in range(2):
        lanes = slice(half * width, (half + 1) * width)
        wanted = [
            (ids[half : half + 1, :] - (info[1] ^ owner) * own_rows).astype(F32) for owner in owners
        ]

        def chunk(c, sofar):
            first = pl.multiple_of(c * TILE, TILE)
            for which in range(count):
                hot = one_hot(places, wanted[which] - first.astype(F32))
                sofar = sofar + nn(pieces[which][lanes, pl.ds(first, TILE)], hot)
            return sofar

        empty = jnp.zeros((width, ids.shape[1]), F32) if start else prior[lanes, :].astype(F32)
        out[lanes, at:] = lax.fori_loop(0, own_rows // TILE, chunk, empty).astype(BF16)


def lookup(info, pieces, owners, own_rows, ids, prior, ups=()):
    width = pieces[0].shape[-2] // 2
    vm = pl.BlockSpec(memory_space=VMEM)
    operands = [info, ids, *pieces, *ups] + ([] if prior is None else [prior])
    at = 8 * ups[0].shape[1] if ups else 0
    return pl.pallas_call(
        functools.partial(
            lookup_kernel, owners, len(pieces), width, own_rows, prior is None, bool(ups)
        ),
        out_shape=jax.ShapeDtypeStruct((2 * width, at + ids.shape[1]), BF16),
        in_specs=[pl.BlockSpec(memory_space=pltpu.SMEM)] + [vm] * (len(operands) - 1),
        out_specs=vm,
        scratch_shapes=[VMEM((at, SEG), BF16)] if ups else [],
        name="lookup",
    )(*operands)


def spread_kernel(arrays, width, start, end, *refs):
    outs = refs[-3:-1] if end else refs[-2:-1]
    turned = refs[-1]
    info, pieces = refs[0], entries(refs[1 : 1 + arrays])
    own_rows = outs[0].shape[-1] if end else outs[0].shape[1]
    length = pieces[0].shape[1]
    places = steps(TILE)
    wanted = []
    for i, piece in enumerate(pieces):
        turned[i * length : (i + 1) * length, :] = piece[: 2 * width, :].T
        digits = piece[2 * width :, :].astype(F32)
        wanted.append(
            [
                digits[d : d + 1] * 256.0 + digits[d + 1 : d + 2] - (info[1] * own_rows).astype(F32)
                for d in (0, 2)
            ]
        )

    def chunk(c, carry):
        first = pl.multiple_of(c * TILE, TILE)
        for half in range(2):
            hot = [one_hot(places, want[half] - first.astype(F32)) for want in wanted]
            hot = jnp.concatenate(hot, axis=1) if len(hot) > 1 else hot[0]
            part = nn(hot, turned[: len(pieces) * length, half * width : (half + 1) * width])
            cut = pl.ds(first, TILE)
            if not start:
                part = part + refs[1 + arrays][half, cut, :]
            if end:
                outs[half][:, cut] = part.T
            else:
                outs[0][half, cut, :] = part
        return carry

    lax.fori_loop(0, own_rows // TILE, chunk, 0)


def spread(info, pieces, own_rows, width, prior, end):
    operands = [info, *pieces] + ([] if prior is None else [prior])
    vm = pl.BlockSpec(memory_space=VMEM)
    shapes = [(width, own_rows)] * 2 if end else [(2, own_rows, width)]
    length = pieces[0].shape[-1]
    count = sum(1 if piece.ndim == 2 else piece.shape[0] for piece in pieces)
    got = pl.pallas_call(
        functools.partial(spread_kernel, len(pieces), width, prior is None, end),
        out_shape=[jax.ShapeDtypeStruct(shape, F32) for shape in shapes],
        in_specs=[pl.BlockSpec(memory_space=pltpu.SMEM)] + [vm] * (len(operands) - 1),
        out_specs=[vm] * len(shapes),
        scratch_shapes=[VMEM((count * length, 2 * width), BF16)],
        name="spread",
    )(*operands)
    return got if end else got[0]


def rope_into(out, row, values, cosine, sine, scale):
    half = HD // 2
    one, two = values[:half], values[half:]
    out[row : row + half, :] = (one * cosine - two * sine).astype(BF16) * scale
    out[row + half : row + HD, :] = (one * sine + two * cosine).astype(BF16) * scale


def key_offset(parent):
    return pl.multiple_of(jnp.where(parent > 0, parent + 1, 0) * SEG, SEG)


def pick(refs, which):
    value = refs[3][0]
    for k in range(3):
        value = jnp.where(which == k, refs[k][0], value)
    return value


def front_kernel(
    par,
    row0,
    row1,
    row2,
    row3,
    up0,
    up1,
    up2,
    up3,
    emb0,
    emb1,
    emb2,
    emb3,
    wqkv,
    gain,
    cos_ref,
    sin_ref,
    resid,
    normed,
    qkv,
    mixed,
    lse,
    keys,
    vals,
):
    tile = pl.program_id(0)
    rows = jnp.concatenate([row0[...], row1[...], row2[...], row3[...]], axis=0)
    ups = jnp.concatenate([up0[...], up1[...], up2[...], up3[...]], axis=0)
    own = pick((emb0, emb1, emb2, emb3), tile ^ par[0])
    hidden = own.astype(F32) + tn(rows, ups)
    resid[...] = hidden
    rate = lax.rsqrt(jnp.mean(hidden * hidden, axis=-1, keepdims=True) + EPS)
    norm = (hidden * rate * gain[...]).astype(BF16)
    normed[...] = norm
    proj = nt(wqkv[...], norm)
    cosine, sine = cos_ref[...], sin_ref[...]
    width = keys.shape[0]
    heads = width // HD
    for h in range(heads):
        rope_into(qkv, h * HD, proj[h * HD : (h + 1) * HD], cosine, sine, BF16(HD**-0.5))
        low = width + h * HD
        rope_into(qkv, low, proj[low : low + HD], cosine, sine, BF16(1.0))
    qkv[2 * width :, :] = proj[2 * width :].astype(BF16)
    place = pl.ds(pl.multiple_of(tile * TILE, TILE), TILE)
    keys[:, place] = qkv[width : 2 * width, :]
    vals[:, place] = qkv[2 * width :, :]

    def finish(h, lanes, scores, value):
        top = jnp.max(scores, axis=0, keepdims=True)
        weights = jnp.exp(scores - top)
        total = jnp.sum(weights, axis=0, keepdims=True)
        got = nn(value, weights.astype(BF16))
        mixed[h * HD : (h + 1) * HD, lanes] = (got * (1.0 / total)).astype(BF16)
        lse[h : h + 1, lanes] = top + jnp.log(total)

    @pl.when(tile == 0)
    def _():
        key_at = lax.broadcasted_iota(jnp.int32, (TILE, TILE), 0)
        query_at = lax.broadcasted_iota(jnp.int32, (TILE, TILE), 1)
        for h in range(heads):
            hs = slice(h * HD, (h + 1) * HD)
            scores = tn(keys[hs, 0:TILE], qkv[hs, :])
            scores = jnp.where(key_at <= query_at, scores, MASKED)
            finish(h, slice(0, TILE), scores, vals[hs, 0:TILE])

    @pl.when(tile > 0)
    def _():
        key_at = lax.broadcasted_iota(jnp.int32, (4 * SEG, SEG), 0)
        query_at = lax.broadcasted_iota(jnp.int32, (4 * SEG, SEG), 1)
        for half in range(2):
            parent = par[2 + 2 * tile + half]
            mine = pl.ds(pl.multiple_of(tile * TILE + half * SEG, SEG), SEG)
            theirs = pl.ds(key_offset(parent), SEG)
            limit = jnp.where(parent > 0, 4 * SEG, 3 * SEG)
            seen = (key_at < TILE) | ((key_at - TILE <= query_at) & (key_at < 3 * SEG))
            seen = seen | ((key_at >= 3 * SEG) & (key_at < limit))
            lanes = slice(half * SEG, (half + 1) * SEG)
            for h in range(heads):
                hs = slice(h * HD, (h + 1) * HD)
                key = jnp.concatenate([keys[hs, 0:TILE], keys[hs, mine], keys[hs, theirs]], axis=1)
                value = jnp.concatenate(
                    [vals[hs, 0:TILE], vals[hs, mine], vals[hs, theirs]], axis=1
                )
                scores = jnp.where(seen, tn(key, qkv[hs, lanes]), MASKED)
                finish(h, lanes, scores, value)


def front(par, sets, tokens, wqkvo, gain, cosine, sine):
    dim = tokens[0].shape[2]
    length = sets[0].shape[1] - dim
    width = wqkvo.shape[0] // 4
    ng = sets[0].shape[0]
    tall = lambda r, _: (r, 0)
    wide = lambda r, _: (0, r)
    return pl.pallas_call(
        front_kernel,
        grid_spec=pltpu.PrefetchScalarGridSpec(
            num_scalar_prefetch=1,
            grid=(length // TILE,),
            in_specs=[pl.BlockSpec((ng, TILE), lambda r, _: (0, r + dim // TILE))] * 4
            + [whole((ng, dim))] * 4
            + [whole((1, TILE, dim))] * 4
            + [
                whole((3 * width, dim)),
                whole((1, dim)),
                pl.BlockSpec((HD // 2, TILE), wide),
                pl.BlockSpec((HD // 2, TILE), wide),
            ],
            out_specs=[
                pl.BlockSpec((TILE, dim), tall),
                pl.BlockSpec((TILE, dim), tall),
                pl.BlockSpec((3 * width, TILE), wide),
                pl.BlockSpec((width, TILE), wide),
                pl.BlockSpec((8, TILE), wide),
            ],
            scratch_shapes=[VMEM((width, length), BF16), VMEM((width, length), BF16)],
        ),
        out_shape=[
            jax.ShapeDtypeStruct((length, dim), F32),
            jax.ShapeDtypeStruct((length, dim), BF16),
            jax.ShapeDtypeStruct((3 * width, length), BF16),
            jax.ShapeDtypeStruct((width, length), BF16),
            jax.ShapeDtypeStruct((8, length), F32),
        ],
        name="front",
    )(par, *sets, *sets, *tokens, wqkvo, gain, cosine, sine)


def middle_kernel(
    who,
    mix0,
    mix1,
    mix2,
    mix3,
    out0,
    out1,
    out2,
    out3,
    resid,
    gain,
    ffn,
    cot0,
    cot1,
    cot2,
    cot3,
    feed,
    resid_own,
    normed,
    hidden,
    grads,
    grad_res,
    mix_stay,
    mix_leave,
    grad_gain,
    cot_all,
):
    tile = pl.program_id(0)
    units = hidden.shape[1]
    outs = jnp.concatenate([out0[...], out1[...], out2[...], out3[...]], axis=0)
    mix = jnp.concatenate([mix0[...], mix1[...], mix2[...], mix3[...]], axis=0)
    res = resid[...] + tn(mix, outs)

    @pl.when(tile == who[0])
    def _():
        resid_own[...] = res

    rate = lax.rsqrt(jnp.mean(res * res, axis=-1, keepdims=True) + EPS)
    norm = (res * rate * gain[...]).astype(BF16)
    normed[...] = norm
    gate = nn(norm, ffn[:, :units])
    upward = nn(norm, ffn[:, units : 2 * units])
    sig = 1.0 / (1.0 + jnp.exp(-gate))
    silu = gate * sig
    hid = (silu * upward).astype(BF16)
    hidden[...] = hid
    feed[0] = nt(hid, ffn[:, 2 * units :]).astype(BF16)
    cot = pick((cot0, cot1, cot2, cot3), tile ^ who[0])
    cot_all[...] = cot
    back = nn(cot, ffn[:, 2 * units :])
    grad_gate = (back * upward * sig * (1.0 + gate * (1.0 - sig))).astype(BF16)
    grad_up = (back * silu).astype(BF16)
    grads[:, :units] = grad_gate
    grads[:, units:] = grad_up
    pulled = nt(grad_gate, ffn[:, :units]) + nt(grad_up, ffn[:, units : 2 * units])
    scaled = pulled * gain[...]
    dots = jnp.mean(scaled * res, axis=-1, keepdims=True)
    part = rate * scaled - res * (rate * rate * rate * dots) + 0.25 * cot.astype(F32)
    part = part.astype(BF16)
    grad_res[...] = part
    by_head = nt(outs, part).astype(BF16)
    width = out0.shape[0]
    for k in range(4):
        out = (mix_stay, mix_leave)[k % 2]
        out[k // 2] = by_head[k * width : (k + 1) * width]
    gained = jnp.sum(pulled * res * rate, axis=0, keepdims=True)

    @pl.when(tile == 0)
    def _():
        grad_gain[...] = gained

    @pl.when(tile > 0)
    def _():
        grad_gain[...] += gained


def slot_of(xor):
    return (xor & 1) * 2 + (xor >> 1)


def middle(who, mixes, outs, resid, gain, ffn, tokens):
    length, dim = resid.shape
    width = mixes[0].shape[0]
    units = ffn.shape[1] // 3
    tiles = length // TILE
    tall = lambda r, _: (r, 0)
    wide = lambda r, _: (0, r)
    return pl.pallas_call(
        middle_kernel,
        grid_spec=pltpu.PrefetchScalarGridSpec(
            num_scalar_prefetch=1,
            grid=(tiles,),
            in_specs=[pl.BlockSpec((width, TILE), wide)] * 4
            + [whole((width, dim))] * 4
            + [
                pl.BlockSpec((TILE, dim), tall),
                whole((1, dim)),
                whole((dim, 3 * units)),
            ]
            + [pl.BlockSpec((1, TILE, dim), lambda *_: (1, 0, 0))] * 4,
            out_specs=[
                pl.BlockSpec((1, TILE, dim), lambda r, who: (slot_of(r ^ who[0]), 0, 0)),
                whole((TILE, dim)),
                pl.BlockSpec((TILE, dim), tall),
                pl.BlockSpec((TILE, units), tall),
                pl.BlockSpec((TILE, 2 * units), tall),
                pl.BlockSpec((TILE, dim), tall),
                pl.BlockSpec((2, width, TILE), lambda r, _: (0, 0, r)),
                pl.BlockSpec((2, width, TILE), lambda r, _: (0, 0, r)),
                whole((1, dim)),
                pl.BlockSpec((TILE, dim), tall),
            ],
        ),
        out_shape=[
            jax.ShapeDtypeStruct((tiles, TILE, dim), BF16),
            jax.ShapeDtypeStruct((TILE, dim), F32),
            jax.ShapeDtypeStruct((length, dim), BF16),
            jax.ShapeDtypeStruct((length, units), BF16),
            jax.ShapeDtypeStruct((length, 2 * units), BF16),
            jax.ShapeDtypeStruct((length, dim), BF16),
            jax.ShapeDtypeStruct((2, width, length), BF16),
            jax.ShapeDtypeStruct((2, width, length), BF16),
            jax.ShapeDtypeStruct((1, dim), F32),
            jax.ShapeDtypeStruct((length, dim), BF16),
        ],
        name="middle",
    )(who, *mixes, *outs, resid, gain, ffn, *tokens)


def unrope_into(out, row, values, cosine, sine):
    half = HD // 2
    one, two = values[:half], values[half:]
    out[row : row + half, :] = (one * cosine + two * sine).astype(BF16)
    out[row + half : row + HD, :] = (two * cosine - one * sine).astype(BF16)


def back_kernel(
    info,
    qkv,
    gmix,
    mixed,
    lse,
    grad_res,
    resid,
    gain,
    gain_two,
    wqkv,
    up0,
    up1,
    up2,
    up3,
    row0,
    row1,
    row2,
    row3,
    cos_ref,
    sin_ref,
    gproj,
    stay,
    leave,
    row_stay,
    row_leave,
    keys_sum,
    vals_sum,
    query_sum,
    grad_gain,
    grad_ups,
):
    step = pl.program_id(0)
    tile = pl.num_programs(0) - 1 - step
    width = gmix.shape[0]
    heads = width // HD

    @pl.when(step == 0)
    def _():
        keys_sum[...] = jnp.zeros_like(keys_sum)
        vals_sum[...] = jnp.zeros_like(vals_sum)

    base = pl.multiple_of(tile * TILE, TILE)

    def pull(h, lanes, query, key, value, seen):
        hs = slice(h * HD, (h + 1) * HD)
        grad = gmix[hs, lanes]
        delta = jnp.sum(grad.astype(F32) * mixed[hs, lanes].astype(F32), axis=0, keepdims=True)
        scores = jnp.where(seen, tn(key, query), MASKED)
        probs = jnp.exp(scores - lse[h : h + 1, lanes])
        dval = nt(grad, probs.astype(BF16))
        dscore = (probs * (tn(value, grad) - delta)).astype(BF16)
        query_sum[hs, lanes] = nn(key, dscore) * HD**-0.5
        return nt(query, dscore), dval

    @pl.when(tile == 0)
    def _():
        key_at = lax.broadcasted_iota(jnp.int32, (TILE, TILE), 0)
        query_at = lax.broadcasted_iota(jnp.int32, (TILE, TILE), 1)
        seen = key_at <= query_at
        for h in range(heads):
            hs = slice(h * HD, (h + 1) * HD)
            key = qkv[width + h * HD : width + (h + 1) * HD, 0:TILE]
            value = qkv[2 * width + h * HD : 2 * width + (h + 1) * HD, 0:TILE]
            dkey, dval = pull(h, slice(0, TILE), qkv[hs, 0:TILE], key, value, seen)
            keys_sum[hs, 0:TILE] += dkey
            vals_sum[hs, 0:TILE] += dval

    @pl.when(tile > 0)
    def _():
        key_at = lax.broadcasted_iota(jnp.int32, (4 * SEG, SEG), 0)
        query_at = lax.broadcasted_iota(jnp.int32, (4 * SEG, SEG), 1)
        for half in range(2):
            parent = info[2 + 2 * tile + half]
            mine = pl.ds(pl.multiple_of(base + half * SEG, SEG), SEG)
            theirs = pl.ds(key_offset(parent), SEG)
            limit = jnp.where(parent > 0, 4 * SEG, 3 * SEG)
            seen = (key_at < TILE) | ((key_at - TILE <= query_at) & (key_at < 3 * SEG))
            seen = seen | ((key_at >= 3 * SEG) & (key_at < limit))
            lanes = slice(half * SEG, (half + 1) * SEG)
            for h in range(heads):
                hs = slice(h * HD, (h + 1) * HD)
                ks = slice(width + h * HD, width + (h + 1) * HD)
                vs = slice(2 * width + h * HD, 2 * width + (h + 1) * HD)
                key = jnp.concatenate([qkv[ks, 0:TILE], qkv[ks, mine], qkv[ks, theirs]], axis=1)
                value = jnp.concatenate([qkv[vs, 0:TILE], qkv[vs, mine], qkv[vs, theirs]], axis=1)
                dkey, dval = pull(h, lanes, qkv[hs, mine], key, value, seen)
                for total, part in ((keys_sum, dkey), (vals_sum, dval)):
                    total[hs, 0:TILE] += part[:, 0:TILE]
                    total[hs, mine] += part[:, TILE : 3 * SEG]
                    total[hs, theirs] += part[:, 3 * SEG :]

    cosine, sine = cos_ref[...], sin_ref[...]
    place = pl.ds(base, TILE)
    for h in range(heads):
        hs = slice(h * HD, (h + 1) * HD)
        unrope_into(gproj, h * HD, query_sum[hs, :], cosine, sine)
        unrope_into(gproj, width + h * HD, keys_sum[hs, place], cosine, sine)
    gproj[2 * width :, :] = vals_sum[:, place].astype(BF16)
    pulled = tn(gproj[...], wqkv[...])
    hidden = resid[...]
    rate = lax.rsqrt(jnp.mean(hidden * hidden, axis=-1, keepdims=True) + EPS)
    scaled = pulled * gain[...]
    dots = jnp.mean(scaled * hidden, axis=-1, keepdims=True)
    part = grad_res[...].astype(F32) + rate * scaled - hidden * (rate * rate * rate * dots)
    part = part.astype(BF16)
    slot = slot_of(tile ^ info[0])

    @pl.when(slot < 2)
    def _():
        stay[slot, :TILE, :] = part

    @pl.when(slot >= 2)
    def _():
        leave[slot - 2, :TILE, :] = part

    rows = jnp.concatenate([row0[...], row1[...], row2[...], row3[...]], axis=0)
    up_part = nn(rows, part)
    ups = jnp.concatenate([up0[...], up1[...], up2[...], up3[...]], axis=0)
    by_column = nt(ups, part).astype(BF16)
    wide = up0.shape[0]
    for k in range(4):
        (row_stay, row_leave)[k % 2][k // 2] = by_column[k * wide : (k + 1) * wide]
    gained = jnp.sum(pulled * hidden * rate, axis=0, keepdims=True)

    @pl.when(step == 0)
    def _():
        grad_gain[...] = gained
        grad_ups[...] = up_part

    @pl.when(step > 0)
    def _():
        grad_gain[...] += gained
        grad_ups[...] += up_part

    @pl.when(tile == 0)
    def _():
        dim = grad_gain.shape[1]
        gains = jnp.concatenate(
            [grad_gain[...], gain_two[...], jnp.zeros((14, dim), F32)], axis=0
        ).astype(BF16)
        for k in range(4):
            out = (stay, leave)[k % 2]
            out[k // 2, TILE : TILE + wide, :] = grad_ups[k * wide : (k + 1) * wide, :].astype(BF16)
            out[k // 2, TILE + wide :, :] = gains


def back(info, qkv, gmix, mixed, lse, grad_res, resid, gain, gain_part, wqkvo, sets, cosine, sine):
    length, dim = resid.shape
    width = gmix.shape[0]
    ng = sets[0].shape[0]
    tiles = length // TILE
    last = tiles - 1
    tall = lambda r, _: (last - r, 0)
    wide = lambda r, _: (0, last - r)
    return pl.pallas_call(
        back_kernel,
        grid_spec=pltpu.PrefetchScalarGridSpec(
            num_scalar_prefetch=1,
            grid=(tiles,),
            in_specs=[
                whole((3 * width, length)),
                pl.BlockSpec((width, TILE), wide),
                pl.BlockSpec((width, TILE), wide),
                pl.BlockSpec((8, TILE), wide),
                pl.BlockSpec((TILE, dim), tall),
                pl.BlockSpec((TILE, dim), tall),
                whole((1, dim)),
                whole((1, dim)),
                whole((3 * width, dim)),
            ]
            + [whole((ng, dim))] * 4
            + [pl.BlockSpec((ng, TILE), lambda r, _: (0, last - r + dim // TILE))] * 4
            + [
                pl.BlockSpec((HD // 2, TILE), wide),
                pl.BlockSpec((HD // 2, TILE), wide),
            ],
            out_specs=[
                pl.BlockSpec((3 * width, TILE), wide),
                whole((2, TILE + ng + 16, dim)),
                whole((2, TILE + ng + 16, dim)),
                pl.BlockSpec((2, ng, TILE), lambda r, _: (0, 0, last - r)),
                pl.BlockSpec((2, ng, TILE), lambda r, _: (0, 0, last - r)),
            ],
            scratch_shapes=[
                VMEM((width, length), F32),
                VMEM((width, length), F32),
                VMEM((width, TILE), F32),
                VMEM((1, dim), F32),
                VMEM((4 * ng, dim), F32),
            ],
        ),
        out_shape=[
            jax.ShapeDtypeStruct((3 * width, length), BF16),
            jax.ShapeDtypeStruct((2, TILE + ng + 16, dim), BF16),
            jax.ShapeDtypeStruct((2, TILE + ng + 16, dim), BF16),
            jax.ShapeDtypeStruct((2, ng, length), BF16),
            jax.ShapeDtypeStruct((2, ng, length), BF16),
        ],
        name="back",
    )(info, qkv, gmix, mixed, lse, grad_res, resid, gain, gain_part, wqkvo, *sets, *sets, cosine, sine)


def rotary(parents):
    length = parents.shape[0]
    token = jnp.arange(length, dtype=jnp.int32)
    trunk = 2 * SEG
    inside = token < trunk
    block = jnp.where(inside, 0, (token - trunk) // SEG + 1)
    offset = jnp.where(inside, token, token - trunk - (block - 1) * SEG)
    position = jnp.where(inside, 0, jnp.where(parents == 0, 2 * SEG, 3 * SEG)) + offset
    half = HD // 2
    frequency = ROPE_BASE ** (-(jnp.arange(half, dtype=F32) * 2.0 / HD))
    angles = frequency[:, None] * position.astype(F32)[None, :]
    return jnp.cos(angles), jnp.sin(angles)


def shards(
    dp,
    embedded,
    ids_two,
    ids_three,
    parents,
    table_two,
    table_three,
    w_two,
    w_three,
    norm_attn,
    w_query,
    w_key,
    w_value,
    w_output,
    norm_ffn,
    w_gate,
    w_up,
    w_down,
    cotangent,
):
    own_d = lax.axis_index("dp")
    own_t = lax.axis_index("tensor")
    own_rows, ng = table_two.shape
    rows, dim = embedded.shape
    width = w_query.shape[1]
    units = w_gate.shape[1]
    own_dim = w_query.shape[0]
    gain_one = norm_attn.reshape(1, dim)
    gain_two = norm_ffn.reshape(1, dim)

    ids = jnp.stack([ids_two, ids_three])
    info = jnp.concatenate(
        [jnp.stack([own_t, own_d]).astype(jnp.int32), parents.reshape(-1, SEG)[:, 0]]
    )
    cosine, sine = rotary(parents)

    first = pack_first(table_two.T, table_three.T, w_two, w_three)
    attn_pack, ffn_pack = pack(w_query, w_key, w_value, w_output, w_gate, w_up, w_down.T)
    token_pair = jnp.stack([embedded, cotangent])
    if dp == 8:
        zero, two, one, three = arrays = double_dp(first)
        got = lookup(info, [zero], (0, 4), own_rows, ids, None)
        got = lookup(info, [two, one], (2, 6, 1, 5), own_rows, ids, got)
        got = lookup(info, [three], (3, 7), own_rows, ids, got, arrays)
        token_pair = after(token_pair, zero)
        attn_arrays = double_dp(after(attn_pack, zero))
        wqkvo = assemble(info, attn_arrays, True)
        ffn_arrays = double_dp(after(ffn_pack, attn_arrays[0]))
        ffn_w = assemble(info, ffn_arrays, False)
    else:
        every = lax.all_gather(first[:, :own_rows], "dp", axis=0)
        small = jnp.concatenate([w_two.astype(BF16).T, w_three.astype(BF16).T], axis=1)
        ups = lax.all_gather(small, "dp", axis=0, tiled=True).T
        wqkvo = lax.all_gather(attn_pack, "dp", axis=0, tiled=True).T
        ffn_w = lax.all_gather(ffn_pack, "dp", axis=0, tiled=True)

        def take(i, so_far):
            piece = lax.dynamic_index_in_dim(every, i, 0, keepdims=False)
            at = jnp.stack([own_t, i]).astype(jnp.int32)
            return lookup(at, [piece], (0,), own_rows, ids, so_far)

        got = lax.fori_loop(0, dp, take, jnp.zeros((2 * ng, ids.shape[1]), BF16))
        got = jnp.concatenate([ups, got], axis=1)

    tokens = gather_tensor(token_pair)
    sets = gather_tensor(got)
    outs = gather_tensor(after(wqkvo[3 * width :], sets[2]))

    resid, normed, qkv, mixed, lse = front(info, sets, tokens, wqkvo, gain_one, cosine, sine)
    mixes = gather_tensor(mixed)
    feed, resid_own, normed_two, hidden, grads, grad_res, stay, leave, gain_part_two, cot_all = (
        middle(info, mixes, outs, resid, gain_two, ffn_w, tokens)
    )
    near, near_far = xor_tensor(leave, 1), None
    near_far = add_round(stay[1], near[1])
    gmix = total((stay[0], near[0], xor_tensor(near_far, 2))).astype(BF16)

    cot_all, _ = lax.optimization_barrier((cot_all, near_far))
    down_halves, up_halves, halves = weigh(
        info, cot_all, hidden, normed_two, grads, mixes, grad_res, feed, dp, own_dim
    )
    down_total, up_total = sum_dp(down_halves, dp), sum_dp(up_halves, dp)
    gmix, *halves = lax.optimization_barrier((gmix, *halves))
    feed_terms = scatter_tensor(*halves)
    output = (resid_own + total([term[:rows] for term in feed_terms])).astype(BF16)
    out_grad = total([term[rows:] for term in feed_terms]).astype(BF16)

    gproj, stay, leave, row_stay, row_leave = back(
        info, qkv, gmix, mixed, lse, grad_res, resid, gain_one, gain_part_two, wqkvo, sets,
        cosine, sine,
    )

    near = xor_tensor(row_leave, 1)
    near_far = add_round(row_stay[1], near[1])
    far = xor_tensor(near_far, 2)
    row_total = total((row_stay[0], near[0], far)).astype(BF16)
    digits = jnp.stack([ids_two // 256, ids_two % 256, ids_three // 256, ids_three % 256])
    digits = jnp.pad(digits.astype(BF16), ((0, 12), (0, 0)))
    row_pack = jnp.concatenate([row_total, digits], axis=0)
    if dp == 8:
        zero, two, one, three = double_dp(row_pack)
        table_grad = spread(info, [zero], own_rows, ng, None, False)
        table_grad = spread(info, [two, one], own_rows, ng, table_grad, False)
        table_grad = spread(info, [three], own_rows, ng, table_grad, True)
    else:
        every = lax.all_gather(row_pack, "dp", axis=0)

        def put(i, so_far):
            piece = lax.dynamic_index_in_dim(every, i, 0, keepdims=False)
            return spread(info, [piece], own_rows, ng, so_far, False)

        table_grad = lax.fori_loop(0, dp, put, jnp.zeros((2, own_rows, ng), F32))
        table_grad = table_grad[0].T, table_grad[1].T

    gproj, _ = lax.optimization_barrier((gproj, near_far))
    attn_total = sum_dp(weigh_turned(info, normed, gproj, out_grad, dp, own_dim), dp)

    stay, leave, _ = lax.optimization_barrier((stay, leave, far))
    terms = scatter_tensor(stay, leave)
    embed_grad = total([term[:rows] for term in terms]).astype(BF16)
    below = add_round(add_round(terms[0][rows:], terms[1][rows:]), terms[2][rows:])
    proj_up_grad, gains = below[: 2 * ng], below[2 * ng : 2 * ng + 2]
    if dp == 8:
        folded = gains.reshape(2 * dim // (2 * ng), 2 * ng)
        proj_up_total = sum_dp(turn(info, proj_up_grad, folded, dp, own_dim), dp)
        gains = proj_up_total[own_dim:].reshape(2, dim)
    else:
        empty = jnp.zeros((16, 2 * ng), BF16)
        halves = turn(info, proj_up_grad, empty, dp, own_dim)[0][:, :own_dim]
        proj_up_total = sum_dp([halves], dp)
        gains = lax.psum(gains.astype(F32), "dp")

    return (
        output,
        embed_grad,
        table_grad[0].T,
        table_grad[1].T,
        proj_up_total[:own_dim, :ng].T,
        proj_up_total[:own_dim, ng:].T,
        gains[0],
        attn_total[:, :width],
        attn_total[:, width : 2 * width],
        attn_total[:, 2 * width : 3 * width],
        attn_total[:, 3 * width :].T,
        gains[1],
        down_total[:, :units],
        up_total,
        down_total[:, units:].T,
    )


def solution(mesh):
    tokens = P(("dp", "tensor"), None)
    down, across = P("dp", "tensor"), P("tensor", "dp")
    in_specs = (
        (tokens, P("dp"), P("dp"), P("dp"), down, down, across, across, P())
        + (down, down, down, across, P(), down, down, across, tokens)
    )
    out_specs = (
        (tokens, tokens, down, down, across, across, P())
        + (down, down, down, across, P(), down, down, across)
    )
    body = functools.partial(shards, mesh.shape["dp"])
    return jax.shard_map(body, mesh=mesh, in_specs=in_specs, out_specs=out_specs, check_vma=False)
```

```python
import functools

import jax
import jax.numpy as jnp
from jax import lax
from jax.experimental import pallas as pl
from jax.experimental.pallas import tpu as pltpu
from jax.sharding import PartitionSpec as P

HD = 64
SEG = 128
TILE = 2 * SEG
EPS = 1e-05
MASKED = -1e30
ROPE_BASE = 10000.0
F32 = jnp.float32
BF16 = jnp.bfloat16
VMEM = pltpu.VMEM


def xor_tensor(value, step):
    return lax.ppermute(value, "tensor", [(i, i ^ step) for i in range(4)])


def xor_dp(value, step, count):
    return lax.ppermute(value, "dp", [(i, i ^ step) for i in range(count)])


def after(value, *others):
    return lax.optimization_barrier((value,) + others)[0]


def gather_tensor(value):
    far = xor_tensor(value, 2)
    near = xor_tensor(value, 1)
    return [value, near, far, xor_tensor(far, 1)]


def add_round(one, two):
    return (one.astype(F32) + two.astype(F32)).astype(BF16)


def scatter_tensor(stay, leave):
    come = xor_tensor(leave, 1)
    far = xor_tensor(add_round(stay[1], come[1]), 2)
    return stay[0], come[0], far


def total(terms):
    return terms[0].astype(F32) + terms[1].astype(F32) + terms[2].astype(F32)


def double_dp(value, others=(), window=lambda zero: ()):
    zero = jnp.stack([value, after(xor_dp(value, 4, 8), *others)])
    made = window(zero)
    two, one, *made = lax.optimization_barrier((xor_dp(zero, 2, 8), xor_dp(zero, 1, 8), *made))
    return (zero, two, one, xor_dp(two, 1, 8)), made


DOUBLED = (0, 4, 2, 6, 1, 5, 3, 7)
HALVED = (0, 2, 1, 3)


def halve_first(keep, come):
    return add_round(keep[:2], come[:2]), add_round(keep[2:], come[2:])


def halve_second(stay, come):
    return add_round(stay[0], come[0]), add_round(stay[1], come[1])


class SumDp:
    def __init__(self, halves, count):
        self.count, self.halves = count, halves
        if count == 8:
            away, self.keep = halves
            self.first = xor_dp(away, 1, count)

    def across(self):
        if self.count == 8:
            self.stay, leave = halve_first(self.keep, self.first)
            self.second = xor_dp(leave, 2, self.count)

    def total(self):
        if self.count != 8:
            values = self.halves[0].astype(F32)
            return lax.psum_scatter(values, "dp", scatter_dimension=0, tiled=True)[0]
        return self.ours.astype(F32) + self.third.astype(F32)

    def between(self):
        if self.count == 8:
            self.ours, leave = halve_second(self.stay, self.second)
            self.third = xor_dp(leave, 4, self.count)


def entries(refs):
    out = []
    for ref in refs:
        out += [ref] if len(ref.shape) == 2 else [ref.at[i] for i in range(ref.shape[0])]
    return out


def place_rows(info, refs, lane, whole_ref):
    for piece, xor in zip(entries(refs), DOUBLED):
        rows = piece.shape[0]
        at = pl.ds(pl.multiple_of((info[1] ^ xor) * rows, 16), rows)
        whole_ref[at, :] = piece[:, lane : lane + whole_ref.shape[1]]


def assemble_kernel(turn, info, *refs):
    pieces, out = refs[:4], refs[4]
    whole_ref = refs[-1] if turn else out
    place_rows(info, pieces, 0, whole_ref)
    if turn:
        turned = whole_ref[...].T
        out[...] = turned[: out.shape[0]]
        refs[5][...] = turned[out.shape[0] :]


def assemble(info, arrays, turn):
    rows, cols = arrays[0].shape[1:]
    shapes = [(8 * rows, cols)]
    if turn:
        shapes = [(cols - cols // 4, 8 * rows), (cols // 4, 8 * rows)]
    return pl.pallas_call(
        functools.partial(assemble_kernel, turn),
        out_shape=[jax.ShapeDtypeStruct(shape, BF16) for shape in shapes],
        in_specs=[pl.BlockSpec(memory_space=pltpu.SMEM)] + [pl.BlockSpec(memory_space=VMEM)] * 4,
        out_specs=[pl.BlockSpec(memory_space=VMEM)] * len(shapes),
        scratch_shapes=[VMEM((8 * rows, cols), BF16)] if turn else [],
        name="assemble",
    )(info, *arrays)


def whole(shape):
    return pl.BlockSpec(shape, lambda *_: (0,) * len(shape))


def nn(a, b):
    return lax.dot_general(a, b, (((1,), (0,)), ((), ())), preferred_element_type=F32)


def nt(a, b):
    return lax.dot_general(a, b, (((1,), (1,)), ((), ())), preferred_element_type=F32)


def tn(a, b):
    return lax.dot_general(a, b, (((0,), (0,)), ((), ())), preferred_element_type=F32)


def pack_first_kernel(two, three, up_two, up_three, out):
    ng, rows = two.shape
    out[:ng, :rows] = two[...].astype(BF16)
    out[ng:, :rows] = three[...].astype(BF16)
    out[:, rows:] = jnp.zeros((2 * ng, SEG), BF16)
    if up_two.shape[1] == 2 * ng:
        small = jnp.concatenate([up_two[...], up_three[...]], axis=0)
        out[:, rows : rows + 2 * ng] = small.T.astype(BF16)


def pack_first(two, three, up_two, up_three):
    ng, rows = two.shape
    return pl.pallas_call(
        pack_first_kernel,
        out_shape=jax.ShapeDtypeStruct((2 * ng, rows + SEG), BF16),
        name="pack_first",
    )(two, three, up_two, up_three)


def pack_kernel(query, key, value, output, gate, up, down, attn, ffn):
    width, units = query.shape[1], gate.shape[1]
    for i, ref in enumerate((query, key, value)):
        attn[:, i * width : (i + 1) * width] = ref[...].astype(BF16)
    attn[:, 3 * width :] = output[...].T.astype(BF16)
    for i, ref in enumerate((gate, up, down)):
        ffn[:, i * units : (i + 1) * units] = ref[...].astype(BF16)


def pack(query, key, value, output, gate, up, down):
    rows, width = query.shape
    return pl.pallas_call(
        pack_kernel,
        out_shape=[
            jax.ShapeDtypeStruct((rows, 4 * width), BF16),
            jax.ShapeDtypeStruct((rows, 3 * gate.shape[1]), BF16),
        ],
        name="pack",
    )(query, key, value, output, gate, up, down)


def split_rows(info, whole_ref, outs, rows):
    if len(outs) == 1:
        for i in range(outs[0].shape[0]):
            outs[0][i] = whole_ref[i * rows : (i + 1) * rows, :]
        return
    for entry, xor in enumerate(HALVED):
        for out, other in zip(outs, (1, 0)):
            at = info[1] ^ (2 * xor + other)
            out[entry] = whole_ref[pl.ds(pl.multiple_of(at * rows, 16), rows), :]


def weigh_kernel(rows, halves, info, cot, hidden, norm, grads, *refs):
    mixes, grad, refs = refs[:4], refs[4], refs[5:]
    outs, (stay, leave, turned, whole_ref) = refs[:halves], refs[halves:]
    at = grads.shape[1]
    turned[...] = cot[...].T
    whole_ref[:, at:] = nn(turned[...], hidden[...]).astype(BF16)
    turned[...] = norm[...].T
    whole_ref[:, :at] = nn(turned[...], grads[...]).astype(BF16)
    split_rows(info, whole_ref, outs, rows)
    for xor in range(4):
        (stay, leave)[xor % 2][xor // 2] = nn(mixes[xor][...], grad[...]).astype(BF16)


def weigh(info, cot, hidden, norm, grads, mixes, grad, count, own_dim):
    vm = pl.BlockSpec(memory_space=VMEM)
    dim, length = cot.shape[1], cot.shape[0]
    lead = [4, 4] if count == 8 else [count]
    cols = hidden.shape[1] + grads.shape[1]
    shapes = [(n, own_dim, cols) for n in lead] + [(2, mixes[0].shape[0], dim)] * 2
    got = pl.pallas_call(
        functools.partial(weigh_kernel, own_dim, len(lead)),
        out_shape=[jax.ShapeDtypeStruct(shape, BF16) for shape in shapes],
        in_specs=[pl.BlockSpec(memory_space=pltpu.SMEM)] + [vm] * 9,
        out_specs=[vm] * len(shapes),
        scratch_shapes=[VMEM((dim, length), BF16), VMEM((dim, cols), BF16)],
        name="weigh",
    )(info, cot, hidden, norm, grads, *mixes, grad)
    return got[: len(lead)], got[len(lead) :]


def weigh_turned_kernel(rows, info, left, right, *refs):
    outs, whole_ref = refs[:-1], refs[-1]
    whole_ref[...] = nn(right[...], left[...]).astype(BF16).T
    split_rows(info, whole_ref, outs, rows)


def turn_kernel(rows, info, wide, *refs):
    outs, whole_ref = refs[:-1], refs[-1]
    whole_ref[...] = wide[...].T
    split_rows(info, whole_ref, outs, rows)


def turn_below_kernel(rows, info, wide, below, *refs):
    outs = refs[:-1]
    turn_kernel(rows, info, wide, *(out.at[:, :rows] for out in outs), refs[-1])
    for out in outs:
        for z in range(out.shape[0]):
            out[z, rows:, : below.shape[1]] = below[...]


def split_call(body, info, operands, count, own_dim, cols, below=0):
    vm = pl.BlockSpec(memory_space=VMEM)
    lead = [4, 4] if count == 8 else [count]
    shapes = [jax.ShapeDtypeStruct((n, own_dim + below, cols), BF16) for n in lead]
    return pl.pallas_call(
        functools.partial(body, own_dim),
        out_shape=shapes,
        in_specs=[pl.BlockSpec(memory_space=pltpu.SMEM)] + [vm] * len(operands),
        out_specs=[vm] * len(shapes),
        scratch_shapes=[VMEM((count * own_dim, cols), BF16)],
        name="split",
    )(info, *operands)


def weigh_turned(info, left, right, count, own_dim):
    return split_call(weigh_turned_kernel, info, [left, right], count, own_dim, right.shape[0])


def turn(info, wide, below, count, own_dim):
    if below is None:
        return split_call(turn_kernel, info, [wide], count, own_dim, wide.shape[0])
    return split_call(
        turn_below_kernel, info, [wide, below], count, own_dim, wide.shape[0], below.shape[0]
    )


def steps(length):
    return lax.broadcasted_iota(jnp.int32, (TILE, SEG), 0).astype(F32).astype(BF16)


def one_hot(places, wanted):
    near = jnp.clip(wanted, -1.0, float(TILE)).astype(BF16)
    parts = [
        jnp.where(places == near[:, c : c + SEG], BF16(1.0), BF16(0.0))
        for c in range(0, wanted.shape[1], SEG)
    ]
    return jnp.concatenate(parts, axis=1)


def lookup_kernel(owners, arrays, width, own_rows, start, end, *refs):
    info, ids = refs[0], refs[1]
    arrays, refs = refs[2 : 2 + arrays], refs[2 + arrays :]
    pieces = entries(arrays)
    count = len(owners)
    at = 0
    if end:
        ups, refs, out, whole_ref = refs[:4], refs[4:-2], refs[-2], refs[-1]
        at = out.shape[1] - ids.shape[1]
        place_rows(info, ups, own_rows, whole_ref)
        out[:, :at] = whole_ref[...].T[: 2 * width]
    else:
        out = refs[-1]
    prior = None if start else refs[0]
    places = steps(TILE)
    for half in range(2):
        lanes = slice(half * width, (half + 1) * width)
        wanted = [
            (ids[half : half + 1, :] - (info[1] ^ owner) * own_rows).astype(F32) for owner in owners
        ]

        def chunk(c, sofar):
            first = pl.multiple_of(c * TILE, TILE)
            for which in range(count):
                hot = one_hot(places, wanted[which] - first.astype(F32))
                sofar = sofar + nn(pieces[which][lanes, pl.ds(first, TILE)], hot)
            return sofar

        empty = jnp.zeros((width, ids.shape[1]), F32) if start else prior[lanes, :].astype(F32)
        out[lanes, at:] = lax.fori_loop(0, own_rows // TILE, chunk, empty).astype(BF16)


def lookup(info, pieces, owners, own_rows, ids, prior, ups=()):
    width = pieces[0].shape[-2] // 2
    vm = pl.BlockSpec(memory_space=VMEM)
    operands = [info, ids, *pieces, *ups] + ([] if prior is None else [prior])
    at = 8 * ups[0].shape[1] if ups else 0
    return pl.pallas_call(
        functools.partial(
            lookup_kernel, owners, len(pieces), width, own_rows, prior is None, bool(ups)
        ),
        out_shape=jax.ShapeDtypeStruct((2 * width, at + ids.shape[1]), BF16),
        in_specs=[pl.BlockSpec(memory_space=pltpu.SMEM)] + [vm] * (len(operands) - 1),
        out_specs=vm,
        scratch_shapes=[VMEM((at, SEG), BF16)] if ups else [],
        name="lookup",
    )(*operands)


def spread_kernel(arrays, width, start, end, *refs):
    outs = refs[-2:] if end else refs[-1:]
    info, pieces = refs[0], entries(refs[1 : 1 + arrays])
    prior = None if start else refs[1 + arrays]
    own_rows = outs[0].shape[1]
    base = (info[1] * own_rows).astype(F32)
    places = steps(TILE)
    wanted = []
    for piece in pieces:
        digits = piece[2 * width :, :].astype(F32)
        wanted.append([digits[d : d + 1] * 256.0 + digits[d + 1 : d + 2] - base for d in (0, 2)])

    def chunk(c, carry):
        first = pl.multiple_of(c * TILE, TILE)
        cut = pl.ds(first, TILE)
        for half in range(2):
            lanes = slice(half * width, (half + 1) * width)
            sofar = jnp.zeros((width, TILE), F32) if start else prior[lanes, cut]
            for piece, want in zip(pieces, wanted):
                hot = one_hot(places, want[half] - first.astype(F32))
                sofar = sofar + nt(piece[lanes, :], hot)
            if end:
                outs[half][:, cut] = sofar
            else:
                outs[0][lanes, cut] = sofar
        return carry

    lax.fori_loop(0, own_rows // TILE, chunk, 0)


def spread(info, pieces, own_rows, width, prior, end):
    operands = [info, *pieces] + ([] if prior is None else [prior])
    vm = pl.BlockSpec(memory_space=VMEM)
    shapes = [(width, own_rows)] * 2 if end else [(2 * width, own_rows)]
    got = pl.pallas_call(
        functools.partial(spread_kernel, len(pieces), width, prior is None, end),
        out_shape=[jax.ShapeDtypeStruct(shape, F32) for shape in shapes],
        in_specs=[pl.BlockSpec(memory_space=pltpu.SMEM)] + [vm] * (len(operands) - 1),
        out_specs=[vm] * len(shapes),
        name="spread",
    )(*operands)
    return got if end else got[0]


def rope_into(out, row, values, cosine, sine, scale):
    half = HD // 2
    one, two = values[:half], values[half:]
    out[row : row + half, :] = (one * cosine - two * sine).astype(BF16) * scale
    out[row + half : row + HD, :] = (one * sine + two * cosine).astype(BF16) * scale


def key_offset(parent):
    return pl.multiple_of(jnp.where(parent > 0, parent + 1, 0) * SEG, SEG)


def pick(refs, which):
    value = refs[3][0]
    for k in range(3):
        value = jnp.where(which == k, refs[k][0], value)
    return value


def front_kernel(
    par,
    row0,
    row1,
    row2,
    row3,
    up0,
    up1,
    up2,
    up3,
    emb0,
    emb1,
    emb2,
    emb3,
    wqkv,
    gain,
    cos_ref,
    sin_ref,
    resid,
    normed,
    qkv,
    mixed,
    lse,
    keys,
    vals,
):
    tile = pl.program_id(0)
    rows = jnp.concatenate([row0[...], row1[...], row2[...], row3[...]], axis=0)
    ups = jnp.concatenate([up0[...], up1[...], up2[...], up3[...]], axis=0)
    own = pick((emb0, emb1, emb2, emb3), tile ^ par[0])
    hidden = own.astype(F32) + tn(rows, ups)
    resid[...] = hidden
    rate = lax.rsqrt(jnp.mean(hidden * hidden, axis=-1, keepdims=True) + EPS)
    norm = (hidden * rate * gain[...]).astype(BF16)
    normed[...] = norm
    proj = nt(wqkv[...], norm)
    cosine, sine = cos_ref[...], sin_ref[...]
    width = keys.shape[0]
    heads = width // HD
    for h in range(heads):
        rope_into(qkv, h * HD, proj[h * HD : (h + 1) * HD], cosine, sine, BF16(HD**-0.5))
        low = width + h * HD
        rope_into(qkv, low, proj[low : low + HD], cosine, sine, BF16(1.0))
    qkv[2 * width :, :] = proj[2 * width :].astype(BF16)
    place = pl.ds(pl.multiple_of(tile * TILE, TILE), TILE)
    keys[:, place] = qkv[width : 2 * width, :]
    vals[:, place] = qkv[2 * width :, :]

    def finish(h, lanes, scores, value):
        top = jnp.max(scores, axis=0, keepdims=True)
        weights = jnp.exp(scores - top)
        total = jnp.sum(weights, axis=0, keepdims=True)
        got = nn(value, weights.astype(BF16))
        mixed[h * HD : (h + 1) * HD, lanes] = (got * (1.0 / total)).astype(BF16)
        lse[h : h + 1, lanes] = top + jnp.log(total)

    @pl.when(tile == 0)
    def _():
        key_at = lax.broadcasted_iota(jnp.int32, (TILE, TILE), 0)
        query_at = lax.broadcasted_iota(jnp.int32, (TILE, TILE), 1)
        for h in range(heads):
            hs = slice(h * HD, (h + 1) * HD)
            scores = tn(keys[hs, 0:TILE], qkv[hs, :])
            scores = jnp.where(key_at <= query_at, scores, MASKED)
            finish(h, slice(0, TILE), scores, vals[hs, 0:TILE])

    @pl.when(tile > 0)
    def _():
        key_at = lax.broadcasted_iota(jnp.int32, (4 * SEG, SEG), 0)
        query_at = lax.broadcasted_iota(jnp.int32, (4 * SEG, SEG), 1)
        for half in range(2):
            parent = par[2 + 2 * tile + half]
            mine = pl.ds(pl.multiple_of(tile * TILE + half * SEG, SEG), SEG)
            theirs = pl.ds(key_offset(parent), SEG)
            limit = jnp.where(parent > 0, 4 * SEG, 3 * SEG)
            seen = (key_at < TILE) | ((key_at - TILE <= query_at) & (key_at < 3 * SEG))
            seen = seen | ((key_at >= 3 * SEG) & (key_at < limit))
            lanes = slice(half * SEG, (half + 1) * SEG)
            for h in range(heads):
                hs = slice(h * HD, (h + 1) * HD)
                key = jnp.concatenate([keys[hs, 0:TILE], keys[hs, mine], keys[hs, theirs]], axis=1)
                value = jnp.concatenate(
                    [vals[hs, 0:TILE], vals[hs, mine], vals[hs, theirs]], axis=1
                )
                scores = jnp.where(seen, tn(key, qkv[hs, lanes]), MASKED)
                finish(h, lanes, scores, value)


def front(par, sets, tokens, wqkvo, gain, cosine, sine):
    dim = tokens[0].shape[2]
    length = sets[0].shape[1] - dim
    width = wqkvo.shape[0] // 3
    ng = sets[0].shape[0]
    tall = lambda r, _: (r, 0)
    wide = lambda r, _: (0, r)
    return pl.pallas_call(
        front_kernel,
        grid_spec=pltpu.PrefetchScalarGridSpec(
            num_scalar_prefetch=1,
            grid=(length // TILE,),
            in_specs=[pl.BlockSpec((ng, TILE), lambda r, _: (0, r + dim // TILE))] * 4
            + [whole((ng, dim))] * 4
            + [whole((1, TILE, dim))] * 4
            + [
                whole((3 * width, dim)),
                whole((1, dim)),
                pl.BlockSpec((HD // 2, TILE), wide),
                pl.BlockSpec((HD // 2, TILE), wide),
            ],
            out_specs=[
                pl.BlockSpec((TILE, dim), tall),
                pl.BlockSpec((TILE, dim), tall),
                pl.BlockSpec((3 * width, TILE), wide),
                pl.BlockSpec((width, TILE), wide),
                pl.BlockSpec((8, TILE), wide),
            ],
            scratch_shapes=[VMEM((width, length), BF16), VMEM((width, length), BF16)],
        ),
        out_shape=[
            jax.ShapeDtypeStruct((length, dim), F32),
            jax.ShapeDtypeStruct((length, dim), BF16),
            jax.ShapeDtypeStruct((3 * width, length), BF16),
            jax.ShapeDtypeStruct((width, length), BF16),
            jax.ShapeDtypeStruct((8, length), F32),
        ],
        name="front",
    )(par, *sets, *sets, *tokens, wqkvo, gain, cosine, sine)


def slot_of(xor):
    return (xor & 1) * 2 + (xor >> 1)


def middle_kernel(
    who,
    mix0,
    mix1,
    mix2,
    mix3,
    out0,
    out1,
    out2,
    out3,
    resid,
    gain,
    ffn0,
    ffn1,
    ffn2,
    ffn3,
    cot0,
    cot1,
    cot2,
    cot3,
    feed_stay,
    feed_leave,
    resid_own,
    normed,
    hidden,
    grads,
    grad_res,
    mix_stay,
    mix_leave,
    grad_gain,
    cot_all,
    ffn,
):
    tile = pl.program_id(0)
    units = hidden.shape[1]

    @pl.when(tile == 0)
    def _():
        if len(ffn0.shape) == 3:
            place_rows(who, (ffn0, ffn1, ffn2, ffn3), 0, ffn)
        else:
            ffn[...] = ffn0[...]

    outs = jnp.concatenate([out0[...], out1[...], out2[...], out3[...]], axis=0)
    mix = jnp.concatenate([mix0[...], mix1[...], mix2[...], mix3[...]], axis=0)
    res = resid[...] + tn(mix, outs)

    @pl.when(tile == who[0])
    def _():
        resid_own[...] = res

    rate = lax.rsqrt(jnp.mean(res * res, axis=-1, keepdims=True) + EPS)
    norm = (res * rate * gain[...]).astype(BF16)
    normed[...] = norm
    gate = nn(norm, ffn[:, :units])
    upward = nn(norm, ffn[:, units : 2 * units])
    sig = 1.0 / (1.0 + jnp.exp(-gate))
    silu = gate * sig
    hid = (silu * upward).astype(BF16)
    hidden[...] = hid
    fed = nt(hid, ffn[:, 2 * units :]).astype(BF16)
    slot = slot_of(tile ^ who[0])

    @pl.when(slot < 2)
    def _():
        feed_stay[0] = fed

    @pl.when(slot >= 2)
    def _():
        feed_leave[0] = fed

    cot = pick((cot0, cot1, cot2, cot3), tile ^ who[0])
    cot_all[...] = cot
    back = nn(cot, ffn[:, 2 * units :])
    grad_gate = (back * upward * sig * (1.0 + gate * (1.0 - sig))).astype(BF16)
    grad_up = (back * silu).astype(BF16)
    grads[:, :units] = grad_gate
    grads[:, units:] = grad_up
    pulled = nt(grad_gate, ffn[:, :units]) + nt(grad_up, ffn[:, units : 2 * units])
    scaled = pulled * gain[...]
    dots = jnp.mean(scaled * res, axis=-1, keepdims=True)
    part = rate * scaled - res * (rate * rate * rate * dots) + 0.25 * cot.astype(F32)
    part = part.astype(BF16)
    grad_res[...] = part
    by_head = nt(outs, part).astype(BF16)
    width = out0.shape[0]
    for k in range(4):
        out = (mix_stay, mix_leave)[k % 2]
        out[k // 2] = by_head[k * width : (k + 1) * width]
    gained = jnp.sum(pulled * res * rate, axis=0, keepdims=True)

    @pl.when(tile == 0)
    def _():
        grad_gain[...] = gained

    @pl.when(tile > 0)
    def _():
        grad_gain[...] += gained


def middle(who, mixes, outs, resid, gain, ffns, tokens):
    length, dim = resid.shape
    width = mixes[0].shape[0]
    units = ffns[0].shape[-1] // 3
    tiles = length // TILE
    tall = lambda r, _: (r, 0)
    wide = lambda r, _: (0, r)
    return pl.pallas_call(
        middle_kernel,
        grid_spec=pltpu.PrefetchScalarGridSpec(
            num_scalar_prefetch=1,
            grid=(tiles,),
            in_specs=[pl.BlockSpec((width, TILE), wide)] * 4
            + [whole((width, dim))] * 4
            + [
                pl.BlockSpec((TILE, dim), tall),
                whole((1, dim)),
            ]
            + [whole(array.shape) for array in ffns]
            + [pl.BlockSpec((1, TILE, dim), lambda *_: (1, 0, 0))] * 4,
            scratch_shapes=[VMEM((dim, 3 * units), BF16)],
            out_specs=[
                pl.BlockSpec((1, TILE, dim), lambda r, who: ((r >> 1) ^ (who[0] >> 1), 0, 0)),
                pl.BlockSpec((1, TILE, dim), lambda r, who: ((r >> 1) ^ (who[0] >> 1), 0, 0)),
                whole((TILE, dim)),
                pl.BlockSpec((TILE, dim), tall),
                pl.BlockSpec((TILE, units), tall),
                pl.BlockSpec((TILE, 2 * units), tall),
                pl.BlockSpec((TILE, dim), tall),
                pl.BlockSpec((2, width, TILE), lambda r, _: (0, 0, r)),
                pl.BlockSpec((2, width, TILE), lambda r, _: (0, 0, r)),
                whole((1, dim)),
                pl.BlockSpec((TILE, dim), tall),
            ],
        ),
        out_shape=[
            jax.ShapeDtypeStruct((tiles // 2, TILE, dim), BF16),
            jax.ShapeDtypeStruct((tiles // 2, TILE, dim), BF16),
            jax.ShapeDtypeStruct((TILE, dim), F32),
            jax.ShapeDtypeStruct((length, dim), BF16),
            jax.ShapeDtypeStruct((length, units), BF16),
            jax.ShapeDtypeStruct((length, 2 * units), BF16),
            jax.ShapeDtypeStruct((length, dim), BF16),
            jax.ShapeDtypeStruct((2, width, length), BF16),
            jax.ShapeDtypeStruct((2, width, length), BF16),
            jax.ShapeDtypeStruct((1, dim), F32),
            jax.ShapeDtypeStruct((length, dim), BF16),
        ],
        name="middle",
    )(who, *mixes, *outs, resid, gain, *ffns, *tokens)


def unrope_into(out, row, values, cosine, sine):
    half = HD // 2
    one, two = values[:half], values[half:]
    out[row : row + half, :] = (one * cosine + two * sine).astype(BF16)
    out[row + half : row + HD, :] = (two * cosine - one * sine).astype(BF16)


def back_kernel(
    info,
    qkv,
    gmix,
    mixed,
    lse,
    grad_res,
    resid,
    gain,
    gain_two,
    wqkv,
    up0,
    up1,
    up2,
    up3,
    row0,
    row1,
    row2,
    row3,
    cos_ref,
    sin_ref,
    feed_stay,
    feed_leave,
    out_stay,
    out_leave,
    gproj,
    stay,
    leave,
    up_stay,
    up_leave,
    row_stay,
    row_leave,
    keys_sum,
    vals_sum,
    query_sum,
    grad_gain,
    grad_ups,
):
    step = pl.program_id(0)
    tile = pl.num_programs(0) - 1 - step
    width = gmix.shape[0]
    heads = width // HD

    @pl.when(step == 0)
    def _():
        keys_sum[...] = jnp.zeros_like(keys_sum)
        vals_sum[...] = jnp.zeros_like(vals_sum)

    base = pl.multiple_of(tile * TILE, TILE)

    def pull(h, lanes, query, key, value, seen):
        hs = slice(h * HD, (h + 1) * HD)
        grad = gmix[hs, lanes]
        delta = jnp.sum(grad.astype(F32) * mixed[hs, lanes].astype(F32), axis=0, keepdims=True)
        scores = jnp.where(seen, tn(key, query), MASKED)
        probs = jnp.exp(scores - lse[h : h + 1, lanes])
        dval = nt(grad, probs.astype(BF16))
        dscore = (probs * (tn(value, grad) - delta)).astype(BF16)
        query_sum[hs, lanes] = nn(key, dscore) * HD**-0.5
        return nt(query, dscore), dval

    @pl.when(tile == 0)
    def _():
        key_at = lax.broadcasted_iota(jnp.int32, (TILE, TILE), 0)
        query_at = lax.broadcasted_iota(jnp.int32, (TILE, TILE), 1)
        seen = key_at <= query_at
        for h in range(heads):
            hs = slice(h * HD, (h + 1) * HD)
            key = qkv[width + h * HD : width + (h + 1) * HD, 0:TILE]
            value = qkv[2 * width + h * HD : 2 * width + (h + 1) * HD, 0:TILE]
            dkey, dval = pull(h, slice(0, TILE), qkv[hs, 0:TILE], key, value, seen)
            keys_sum[hs, 0:TILE] += dkey
            vals_sum[hs, 0:TILE] += dval

    @pl.when(tile > 0)
    def _():
        key_at = lax.broadcasted_iota(jnp.int32, (4 * SEG, SEG), 0)
        query_at = lax.broadcasted_iota(jnp.int32, (4 * SEG, SEG), 1)
        for half in range(2):
            parent = info[2 + 2 * tile + half]
            mine = pl.ds(pl.multiple_of(base + half * SEG, SEG), SEG)
            theirs = pl.ds(key_offset(parent), SEG)
            limit = jnp.where(parent > 0, 4 * SEG, 3 * SEG)
            seen = (key_at < TILE) | ((key_at - TILE <= query_at) & (key_at < 3 * SEG))
            seen = seen | ((key_at >= 3 * SEG) & (key_at < limit))
            lanes = slice(half * SEG, (half + 1) * SEG)
            for h in range(heads):
                hs = slice(h * HD, (h + 1) * HD)
                ks = slice(width + h * HD, width + (h + 1) * HD)
                vs = slice(2 * width + h * HD, 2 * width + (h + 1) * HD)
                key = jnp.concatenate([qkv[ks, 0:TILE], qkv[ks, mine], qkv[ks, theirs]], axis=1)
                value = jnp.concatenate([qkv[vs, 0:TILE], qkv[vs, mine], qkv[vs, theirs]], axis=1)
                dkey, dval = pull(h, lanes, qkv[hs, mine], key, value, seen)
                for total, part in ((keys_sum, dkey), (vals_sum, dval)):
                    total[hs, 0:TILE] += part[:, 0:TILE]
                    total[hs, mine] += part[:, TILE : 3 * SEG]
                    total[hs, theirs] += part[:, 3 * SEG :]

    cosine, sine = cos_ref[...], sin_ref[...]
    place = pl.ds(base, TILE)
    for h in range(heads):
        hs = slice(h * HD, (h + 1) * HD)
        unrope_into(gproj, h * HD, query_sum[hs, :], cosine, sine)
        unrope_into(gproj, width + h * HD, keys_sum[hs, place], cosine, sine)
    gproj[2 * width :, :] = vals_sum[:, place].astype(BF16)
    pulled = tn(gproj[...], wqkv[...])
    hidden = resid[...]
    rate = lax.rsqrt(jnp.mean(hidden * hidden, axis=-1, keepdims=True) + EPS)
    scaled = pulled * gain[...]
    dots = jnp.mean(scaled * hidden, axis=-1, keepdims=True)
    part = grad_res[...].astype(F32) + rate * scaled - hidden * (rate * rate * rate * dots)
    part = part.astype(BF16)
    slot = slot_of(tile ^ info[0])

    @pl.when(slot < 2)
    def _():
        stay[0, :TILE] = part
        stay[0, TILE:] = feed_stay[0]

    @pl.when(slot >= 2)
    def _():
        leave[0, :TILE] = part
        leave[0, TILE:] = feed_leave[0]

    rows = jnp.concatenate([row0[...], row1[...], row2[...], row3[...]], axis=0)
    up_part = nn(rows, part)
    ups = jnp.concatenate([up0[...], up1[...], up2[...], up3[...]], axis=0)
    by_column = nt(ups, part).astype(BF16)
    wide = up0.shape[0]
    for k in range(4):
        (row_stay, row_leave)[k % 2][k // 2] = by_column[k * wide : (k + 1) * wide]
    gained = jnp.sum(pulled * hidden * rate, axis=0, keepdims=True)

    @pl.when(step == 0)
    def _():
        grad_gain[...] = gained
        grad_ups[...] = up_part

    @pl.when(step > 0)
    def _():
        grad_gain[...] += gained
        grad_ups[...] += up_part

    @pl.when(tile == 0)
    def _():
        dim = grad_gain.shape[1]
        gains = jnp.concatenate(
            [grad_gain[...], gain_two[...], jnp.zeros((14, dim), F32)], axis=0
        ).astype(BF16)
        for k in range(4):
            out = (up_stay, up_leave)[k % 2]
            other = (out_stay, out_leave)[k % 2][k // 2]
            out[k // 2, :wide, :] = grad_ups[k * wide : (k + 1) * wide, :].astype(BF16)
            out[k // 2, wide : wide + width, :] = other
            out[k // 2, wide + width :, :] = gains


def back(info, qkv, gmix, mixed, lse, grad_res, resid, gain, gain_part, wqkvo, sets, cosine, sine, feeds, outs):
    length, dim = resid.shape
    width = gmix.shape[0]
    ng = sets[0].shape[0]
    tiles = length // TILE
    last = tiles - 1
    token_slot = lambda r, info: (((last - r) >> 1) ^ (info[0] >> 1), 0, 0)
    tall = lambda r, _: (last - r, 0)
    wide = lambda r, _: (0, last - r)
    return pl.pallas_call(
        back_kernel,
        grid_spec=pltpu.PrefetchScalarGridSpec(
            num_scalar_prefetch=1,
            grid=(tiles,),
            in_specs=[
                whole((3 * width, length)),
                pl.BlockSpec((width, TILE), wide),
                pl.BlockSpec((width, TILE), wide),
                pl.BlockSpec((8, TILE), wide),
                pl.BlockSpec((TILE, dim), tall),
                pl.BlockSpec((TILE, dim), tall),
                whole((1, dim)),
                whole((1, dim)),
                whole((3 * width, dim)),
            ]
            + [whole((ng, dim))] * 4
            + [pl.BlockSpec((ng, TILE), lambda r, _: (0, last - r + dim // TILE))] * 4
            + [
                pl.BlockSpec((HD // 2, TILE), wide),
                pl.BlockSpec((HD // 2, TILE), wide),
                pl.BlockSpec((1, TILE, dim), token_slot),
                pl.BlockSpec((1, TILE, dim), token_slot),
                whole((2, width, dim)),
                whole((2, width, dim)),
            ],
            out_specs=[
                pl.BlockSpec((3 * width, TILE), wide),
                pl.BlockSpec((1, 2 * TILE, dim), token_slot),
                pl.BlockSpec((1, 2 * TILE, dim), token_slot),
                whole((2, ng + width + 16, dim)),
                whole((2, ng + width + 16, dim)),
                pl.BlockSpec((2, ng, TILE), lambda r, _: (0, 0, last - r)),
                pl.BlockSpec((2, ng, TILE), lambda r, _: (0, 0, last - r)),
            ],
            scratch_shapes=[
                VMEM((width, length), F32),
                VMEM((width, length), F32),
                VMEM((width, TILE), F32),
                VMEM((1, dim), F32),
                VMEM((4 * ng, dim), F32),
            ],
        ),
        out_shape=[
            jax.ShapeDtypeStruct((3 * width, length), BF16),
            jax.ShapeDtypeStruct((2, 2 * TILE, dim), BF16),
            jax.ShapeDtypeStruct((2, 2 * TILE, dim), BF16),
            jax.ShapeDtypeStruct((2, ng + width + 16, dim), BF16),
            jax.ShapeDtypeStruct((2, ng + width + 16, dim), BF16),
            jax.ShapeDtypeStruct((2, ng, length), BF16),
            jax.ShapeDtypeStruct((2, ng, length), BF16),
        ],
        name="back",
    )(info, qkv, gmix, mixed, lse, grad_res, resid, gain, gain_part, wqkvo, *sets, *sets, cosine, sine, *feeds, *outs)


def rotary(parents):
    length = parents.shape[0]
    token = jnp.arange(length, dtype=jnp.int32)
    trunk = 2 * SEG
    inside = token < trunk
    block = jnp.where(inside, 0, (token - trunk) // SEG + 1)
    offset = jnp.where(inside, token, token - trunk - (block - 1) * SEG)
    position = jnp.where(inside, 0, jnp.where(parents == 0, 2 * SEG, 3 * SEG)) + offset
    half = HD // 2
    frequency = ROPE_BASE ** (-(jnp.arange(half, dtype=F32) * 2.0 / HD))
    angles = frequency[:, None] * position.astype(F32)[None, :]
    return jnp.cos(angles), jnp.sin(angles)


def shards(
    dp,
    embedded,
    ids_two,
    ids_three,
    parents,
    table_two,
    table_three,
    w_two,
    w_three,
    norm_attn,
    w_query,
    w_key,
    w_value,
    w_output,
    norm_ffn,
    w_gate,
    w_up,
    w_down,
    cotangent,
):
    own_d = lax.axis_index("dp")
    own_t = lax.axis_index("tensor")
    own_rows, ng = table_two.shape
    rows, dim = embedded.shape
    width = w_query.shape[1]
    units = w_gate.shape[1]
    own_dim = w_query.shape[0]
    gain_one = norm_attn.reshape(1, dim)
    gain_two = norm_ffn.reshape(1, dim)

    ids = jnp.stack([ids_two, ids_three])
    info = jnp.concatenate(
        [jnp.stack([own_t, own_d]).astype(jnp.int32), parents.reshape(-1, SEG)[:, 0]]
    )
    cosine, sine = rotary(parents)

    digits = jnp.stack([ids_two // 256, ids_two % 256, ids_three // 256, ids_three % 256])
    digits = jnp.pad(digits.astype(BF16), ((0, 12), (0, 0)))
    first = pack_first(table_two.T, table_three.T, w_two, w_three)
    attn_pack, ffn_pack = pack(w_query, w_key, w_value, w_output, w_gate, w_up, w_down.T)
    token_pair = jnp.stack([embedded, cotangent])
    token_near = xor_tensor(token_pair, 1)
    if dp == 8:
        arrays, (got, token_near) = double_dp(
            first,
            (attn_pack, ffn_pack, cosine, sine, gain_one, gain_two, digits),
            lambda zero: [lookup(info, [zero], (0, 4), own_rows, ids, None), token_near],
        )
        _, two, one, three = arrays
        token_far = xor_tensor(after(token_pair, arrays[0]), 2)
        got = lookup(info, [two, one], (2, 6, 1, 5), own_rows, ids, got)
        attn_arrays, (got, token_far) = double_dp(
            after(attn_pack, arrays[0]),
            (got,),
            lambda zero: [lookup(info, [three], (3, 7), own_rows, ids, got, arrays), token_far],
        )
        wqkv, wo = assemble(info, attn_arrays, True)
        ffn_arrays, _ = double_dp(after(ffn_pack, two), (attn_arrays[1],))
        wqkv, ffn_zero = lax.optimization_barrier((wqkv, ffn_arrays[0]))
        ffns = (ffn_zero, *ffn_arrays[1:])
    else:
        every = lax.all_gather(first[:, :own_rows], "dp", axis=0)
        small = jnp.concatenate([w_two.astype(BF16).T, w_three.astype(BF16).T], axis=1)
        ups = lax.all_gather(small, "dp", axis=0, tiled=True).T
        wqkvo = lax.all_gather(attn_pack, "dp", axis=0, tiled=True).T
        wqkv, wo = wqkvo[: 3 * width], wqkvo[3 * width :]
        ffns = [lax.all_gather(ffn_pack, "dp", axis=0, tiled=True)]
        ffns += [jnp.zeros((8, SEG), BF16)] * 3
        token_far = xor_tensor(token_pair, 2)

        def take(i, so_far):
            piece = lax.dynamic_index_in_dim(every, i, 0, keepdims=False)
            at = jnp.stack([own_t, i]).astype(jnp.int32)
            return lookup(at, [piece], (0,), own_rows, ids, so_far)

        got = lax.fori_loop(0, dp, take, jnp.zeros((2 * ng, ids.shape[1]), BF16))
        got = jnp.concatenate([ups, got], axis=1)

    tokens = [token_pair, token_near, token_far, xor_tensor(token_far, 1)]
    sets = gather_tensor(got)
    outs = gather_tensor(after(wo, sets[2]))

    resid, normed, qkv, mixed, lse = front(info, sets, tokens, wqkv, gain_one, cosine, sine)
    mixed = after(mixed, outs[2])
    mixes = gather_tensor(mixed)
    (
        feed_stay, feed_leave, resid_own, normed_two, hidden, grads, grad_res, stay, leave,
        gain_part_two, cot_all,
    ) = middle(info, mixes, outs, resid, gain_two, ffns, tokens)
    near = xor_tensor(leave, 1)
    near_far = add_round(stay[1], near[1])
    far = xor_tensor(near_far, 2)
    halves, out_pair = weigh(
        info, cot_all, after(hidden, near_far), normed_two, grads, mixes, grad_res, dp, own_dim
    )
    ffn_sum = SumDp(halves, dp)
    far, _ = lax.optimization_barrier((far, halves))
    gmix = total((stay[0], near[0], far)).astype(BF16)

    gproj, stay, leave, up_stay, up_leave, row_stay, row_leave = back(
        info, qkv, gmix, mixed, lse, grad_res, resid, gain_one, gain_part_two, wqkv, sets,
        cosine, sine, (feed_stay, feed_leave), out_pair,
    )

    near = xor_tensor(row_leave, 1)
    near_far = add_round(row_stay[1], near[1])
    if dp == 8:
        near_far, ffn_sum.first = lax.optimization_barrier((near_far, ffn_sum.first))
        ffn_sum.across()
    far = xor_tensor(near_far, 2)
    gproj = after(gproj, near_far)
    attn_halves = weigh_turned(info, normed, gproj, dp, own_dim)
    attn_sum = SumDp(attn_halves, dp)
    far, _ = lax.optimization_barrier((far, attn_halves))
    row_total = total((row_stay[0], near[0], far)).astype(BF16)
    row_pack = jnp.concatenate([row_total, digits], axis=0)
    up_near = xor_tensor(after(up_leave, near_far), 1)
    up_near_far = after(add_round(up_stay[1], up_near[1]), far)
    up_far = xor_tensor(up_near_far, 2)
    below = add_round(add_round(up_stay[0], up_near[0]), up_far)
    wide_grad, gains = below[: 2 * ng + width], below[2 * ng + width : 2 * ng + width + 2]
    token_near = xor_tensor(after(leave, far), 1)
    token_far = xor_tensor(after(add_round(stay[1], token_near[1]), up_near_far), 2)
    if dp == 8:
        folded = gains.reshape(2 * dim // (2 * ng), 2 * ng)
        proj_sum = SumDp(turn(info, wide_grad, folded, dp, own_dim), dp)

        def own_rows_first(zero):
            zero, attn_sum.first, ffn_sum.second = lax.optimization_barrier(
                (zero, attn_sum.first, ffn_sum.second)
            )
            ffn_sum.between()
            return [spread(info, [zero], own_rows, ng, None, False)]

        (_, two, one, three), (table_grad,) = double_dp(row_pack, (up_far,), own_rows_first)
        table_grad = spread(info, [two, one], own_rows, ng, table_grad, False)
        attn_sum.first, token_far, table_grad = lax.optimization_barrier(
            (attn_sum.first, token_far, table_grad)
        )
        attn_sum.across()
        table_grad = spread(info, [three], own_rows, ng, table_grad, True)
        attn_sum.second, proj_sum.first = (
            after(x, *table_grad) for x in (attn_sum.second, proj_sum.first)
        )
        attn_sum.between()
        proj_sum.across()
        ffn_sum.third, token_far, proj_sum.second = (
            after(x, attn_sum.second) for x in (ffn_sum.third, token_far, proj_sum.second)
        )
        proj_sum.between()
    else:
        every = lax.all_gather(row_pack, "dp", axis=0)

        def put(i, so_far):
            piece = lax.dynamic_index_in_dim(every, i, 0, keepdims=False)
            return spread(info, [piece], own_rows, ng, so_far, False)

        table_grad = lax.fori_loop(0, dp, put, jnp.zeros((2 * ng, own_rows), F32))
        table_grad = table_grad[:ng], table_grad[ng:]
    ffn_total, attn_total = ffn_sum.total(), attn_sum.total()
    sums = total((stay[0], token_near[0], token_far))
    embed_grad = sums[:rows].astype(BF16)
    output = (resid_own + sums[rows:]).astype(BF16)
    if dp == 8:
        proj_up_total = proj_sum.total()
        gains = proj_up_total[own_dim:, : 2 * ng].reshape(2, dim)
    else:
        proj_up_total = SumDp(turn(info, wide_grad, None, dp, own_dim), dp).total()
        gains = lax.psum(gains.astype(F32), "dp")

    return (
        output,
        embed_grad,
        table_grad[0].T,
        table_grad[1].T,
        proj_up_total[:own_dim, :ng].T,
        proj_up_total[:own_dim, ng : 2 * ng].T,
        gains[0],
        attn_total[:, :width],
        attn_total[:, width : 2 * width],
        attn_total[:, 2 * width : 3 * width],
        proj_up_total[:own_dim, 2 * ng :].T,
        gains[1],
        ffn_total[:, :units],
        ffn_total[:, units : 2 * units],
        ffn_total[:, 2 * units :].T,
    )


def solution(mesh):
    tokens = P(("dp", "tensor"), None)
    down, across = P("dp", "tensor"), P("tensor", "dp")
    in_specs = (
        (tokens, P("dp"), P("dp"), P("dp"), down, down, across, across, P())
        + (down, down, down, across, P(), down, down, across, tokens)
    )
    out_specs = (
        (tokens, tokens, down, down, across, across, P())
        + (down, down, down, across, P(), down, down, across)
    )
    body = functools.partial(shards, mesh.shape["dp"])
    return jax.shard_map(body, mesh=mesh, in_specs=in_specs, out_specs=out_specs, check_vma=False)
```

```python
import functools

import jax
import jax.numpy as jnp
from jax import lax
from jax.experimental import pallas as pl
from jax.experimental.pallas import tpu as pltpu
from jax.sharding import PartitionSpec as P

HD = 64
SEG = 128
TILE = 2 * SEG
EPS = 1e-05
MASKED = -1e30
ROPE_BASE = 10000.0
F32 = jnp.float32
BF16 = jnp.bfloat16
VMEM = pltpu.VMEM


def xor_tensor(value, step):
    return lax.ppermute(value, "tensor", [(i, i ^ step) for i in range(4)])


def xor_dp(value, step, count):
    return lax.ppermute(value, "dp", [(i, i ^ step) for i in range(count)])


def after(value, *others):
    return lax.optimization_barrier((value,) + others)[0]


def gather_tensor(value):
    far = xor_tensor(value, 2)
    near = xor_tensor(value, 1)
    return [value, near, far, xor_tensor(far, 1)]


def add_round(one, two):
    return (one.astype(F32) + two.astype(F32)).astype(BF16)


def scatter_tensor(stay, leave):
    come = xor_tensor(leave, 1)
    far = xor_tensor(add_round(stay[1], come[1]), 2)
    return stay[0], come[0], far


def total(terms):
    return terms[0].astype(F32) + terms[1].astype(F32) + terms[2].astype(F32)


def double_dp(value, others=(), window=lambda zero: ()):
    zero = jnp.stack([value, after(xor_dp(value, 4, 8), *others)])
    made = window(zero)
    two, one, *made = lax.optimization_barrier((xor_dp(zero, 2, 8), xor_dp(zero, 1, 8), *made))
    return (zero, two, one, xor_dp(two, 1, 8)), made


DOUBLED = (0, 4, 2, 6, 1, 5, 3, 7)
HALVED = (0, 2, 1, 3)


def halve_first(keep, come):
    return add_round(keep[:2], come[:2]), add_round(keep[2:], come[2:])


def halve_second(stay, come):
    return add_round(stay[0], come[0]), add_round(stay[1], come[1])


class SumDp:
    def __init__(self, halves, count):
        self.count, self.halves = count, halves
        if count == 8:
            away, self.keep = halves
            self.first = xor_dp(away, 1, count)

    def across(self):
        if self.count == 8:
            self.stay, leave = halve_first(self.keep, self.first)
            self.second = xor_dp(leave, 2, self.count)

    def total(self):
        if self.count != 8:
            values = self.halves[0].astype(F32)
            return lax.psum_scatter(values, "dp", scatter_dimension=0, tiled=True)[0]
        return self.ours.astype(F32) + self.third.astype(F32)

    def between(self):
        if self.count == 8:
            self.ours, leave = halve_second(self.stay, self.second)
            self.third = xor_dp(leave, 4, self.count)


def entries(refs):
    out = []
    for ref in refs:
        out += [ref] if len(ref.shape) == 2 else [ref.at[i] for i in range(ref.shape[0])]
    return out


def place_rows(info, refs, lane, whole_ref):
    for piece, xor in zip(entries(refs), DOUBLED):
        rows = piece.shape[0]
        at = pl.ds(pl.multiple_of((info[1] ^ xor) * rows, 16), rows)
        whole_ref[at, :] = piece[:, lane : lane + whole_ref.shape[1]]


def assemble_kernel(turn, info, *refs):
    pieces, out = refs[:4], refs[4]
    whole_ref = refs[-1] if turn else out
    place_rows(info, pieces, 0, whole_ref)
    if turn:
        turned = whole_ref[...].T
        out[...] = turned[: out.shape[0]]
        refs[5][...] = turned[out.shape[0] :]


def assemble(info, arrays, turn):
    rows, cols = arrays[0].shape[1:]
    shapes = [(8 * rows, cols)]
    if turn:
        shapes = [(cols - cols // 4, 8 * rows), (cols // 4, 8 * rows)]
    return pl.pallas_call(
        functools.partial(assemble_kernel, turn),
        out_shape=[jax.ShapeDtypeStruct(shape, BF16) for shape in shapes],
        in_specs=[pl.BlockSpec(memory_space=pltpu.SMEM)] + [pl.BlockSpec(memory_space=VMEM)] * 4,
        out_specs=[pl.BlockSpec(memory_space=VMEM)] * len(shapes),
        scratch_shapes=[VMEM((8 * rows, cols), BF16)] if turn else [],
        name="assemble",
    )(info, *arrays)


def pick(refs, which):
    value = refs[3][0]
    for k in range(3):
        value = jnp.where(which == k, refs[k][0], value)
    return value


def whole(shape):
    return pl.BlockSpec(shape, lambda *_: (0,) * len(shape))


def nn(a, b):
    return lax.dot_general(a, b, (((1,), (0,)), ((), ())), preferred_element_type=F32)


def nt(a, b):
    return lax.dot_general(a, b, (((1,), (1,)), ((), ())), preferred_element_type=F32)


def tn(a, b):
    return lax.dot_general(a, b, (((0,), (0,)), ((), ())), preferred_element_type=F32)


def pack_first_kernel(two, three, up_two, up_three, out):
    ng, rows = two.shape
    out[:ng, :rows] = two[...].astype(BF16)
    out[ng:, :rows] = three[...].astype(BF16)
    out[:, rows:] = jnp.zeros((2 * ng, SEG), BF16)
    if up_two.shape[1] == 2 * ng:
        small = jnp.concatenate([up_two[...], up_three[...]], axis=0)
        out[:, rows : rows + 2 * ng] = small.T.astype(BF16)


def pack_first(two, three, up_two, up_three):
    ng, rows = two.shape
    return pl.pallas_call(
        pack_first_kernel,
        out_shape=jax.ShapeDtypeStruct((2 * ng, rows + SEG), BF16),
        name="pack_first",
    )(two, three, up_two, up_three)


def pack_kernel(query, key, value, output, gate, up, down, attn, ffn):
    width, units = query.shape[1], gate.shape[1]
    for i, ref in enumerate((query, key, value)):
        attn[:, i * width : (i + 1) * width] = ref[...].astype(BF16)
    attn[:, 3 * width :] = output[...].T.astype(BF16)
    for i, ref in enumerate((gate, up, down)):
        ffn[:, i * units : (i + 1) * units] = ref[...].astype(BF16)


def pack(query, key, value, output, gate, up, down):
    rows, width = query.shape
    return pl.pallas_call(
        pack_kernel,
        out_shape=[
            jax.ShapeDtypeStruct((rows, 4 * width), BF16),
            jax.ShapeDtypeStruct((rows, 3 * gate.shape[1]), BF16),
        ],
        name="pack",
    )(query, key, value, output, gate, up, down)


def split_rows(info, whole_ref, outs, rows):
    if len(outs) == 1:
        for i in range(outs[0].shape[0]):
            outs[0][i] = whole_ref[i * rows : (i + 1) * rows, :]
        return
    for entry, xor in enumerate(HALVED):
        for out, other in zip(outs, (1, 0)):
            at = info[1] ^ (2 * xor + other)
            out[entry] = whole_ref[pl.ds(pl.multiple_of(at * rows, 16), rows), :]


def weigh_kernel(rows, halves, info, hidden, norm, grads, *refs):
    cots, mixes, grad, refs = refs[:4], refs[4:8], refs[8], refs[9:]
    outs, (stay, leave, turned, whole_ref) = refs[:halves], refs[halves:]
    at = grads.shape[1]
    for tile in range(4):
        cot = pick([ref.at[1:2] for ref in cots], tile ^ info[0])
        turned[:, tile * TILE : (tile + 1) * TILE] = cot.T
    whole_ref[:, at:] = nn(turned[...], hidden[...]).astype(BF16)
    turned[...] = norm[...].T
    whole_ref[:, :at] = nn(turned[...], grads[...]).astype(BF16)
    split_rows(info, whole_ref, outs, rows)
    for xor in range(4):
        (stay, leave)[xor % 2][xor // 2] = nn(mixes[xor][...], grad[...]).astype(BF16)


def weigh(info, tokens, hidden, norm, grads, mixes, grad, count, own_dim):
    length, dim = norm.shape
    lead = [4, 4] if count == 8 else [count]
    cols = hidden.shape[1] + grads.shape[1]
    shapes = [(n, own_dim, cols) for n in lead] + [(2, mixes[0].shape[0], dim)] * 2
    operands = [hidden, norm, grads, *tokens, *mixes, grad]
    vm = pl.BlockSpec(memory_space=VMEM)
    got = pl.pallas_call(
        functools.partial(weigh_kernel, own_dim, len(lead)),
        in_specs=[pl.BlockSpec(memory_space=pltpu.SMEM)] + [vm] * len(operands),
        out_specs=[vm] * len(shapes),
        scratch_shapes=[VMEM((dim, length), BF16), VMEM((dim, cols), BF16)],
        out_shape=[jax.ShapeDtypeStruct(shape, BF16) for shape in shapes],
        name="weigh",
    )(info, *operands)
    return got[: len(lead)], got[len(lead) :]


def weigh_turned_kernel(rows, info, left, right, *refs):
    outs, whole_ref = refs[:-1], refs[-1]
    whole_ref[...] = nn(right[...], left[...]).astype(BF16).T
    split_rows(info, whole_ref, outs, rows)


def turn_kernel(rows, info, wide, *refs):
    outs, whole_ref = refs[:-1], refs[-1]
    whole_ref[...] = wide[...].T
    split_rows(info, whole_ref, outs, rows)


def turn_below_kernel(rows, info, wide, below, *refs):
    outs = refs[:-1]
    turn_kernel(rows, info, wide, *(out.at[:, :rows] for out in outs), refs[-1])
    for out in outs:
        for z in range(out.shape[0]):
            out[z, rows:, : below.shape[1]] = below[...]


def split_call(body, info, operands, count, own_dim, cols, below=0):
    vm = pl.BlockSpec(memory_space=VMEM)
    lead = [4, 4] if count == 8 else [count]
    shapes = [jax.ShapeDtypeStruct((n, own_dim + below, cols), BF16) for n in lead]
    return pl.pallas_call(
        functools.partial(body, own_dim),
        out_shape=shapes,
        in_specs=[pl.BlockSpec(memory_space=pltpu.SMEM)] + [vm] * len(operands),
        out_specs=[vm] * len(shapes),
        scratch_shapes=[VMEM((count * own_dim, cols), BF16)],
        name="split",
    )(info, *operands)


def weigh_turned(info, left, right, count, own_dim):
    return split_call(weigh_turned_kernel, info, [left, right], count, own_dim, right.shape[0])


def turn(info, wide, below, count, own_dim):
    if below is None:
        return split_call(turn_kernel, info, [wide], count, own_dim, wide.shape[0])
    return split_call(
        turn_below_kernel, info, [wide, below], count, own_dim, wide.shape[0], below.shape[0]
    )


def finish_kernel(attn, attn_come, wide, wide_come, query, key, value, two, three, output, gains):
    width, ng = query.shape[1], two.shape[0]
    rows = query.shape[0]
    sums = attn[...].astype(F32) + attn_come[...].astype(F32)
    for i, out in enumerate((query, key, value)):
        out[...] = sums[:, i * width : (i + 1) * width]
    sums = wide[...].astype(F32) + wide_come[...].astype(F32)
    turned = sums[:rows].T
    two[...] = turned[:ng]
    three[...] = turned[ng : 2 * ng]
    output[...] = turned[2 * ng :]
    gains[...] = sums[rows:, : gains.shape[1]]


def finish(attn_sum, wide_sum, ng):
    rows, cols = attn_sum.ours.shape
    width = cols // 3
    operands = [attn_sum.ours, attn_sum.third, wide_sum.ours, wide_sum.third]
    below = wide_sum.ours.shape[0] - rows
    shapes = [(rows, width)] * 3 + [(ng, rows)] * 2 + [(width, rows), (below, 2 * ng)]
    vm = pl.BlockSpec(memory_space=VMEM)
    return pl.pallas_call(
        finish_kernel,
        out_shape=[jax.ShapeDtypeStruct(shape, F32) for shape in shapes],
        in_specs=[vm] * 4,
        out_specs=[vm] * 7,
        name="finish",
    )(*operands)


def one_hot(low):
    rows = lax.broadcasted_iota(jnp.int32, (TILE, SEG), 0).astype(F32).astype(BF16)
    parts = [
        jnp.where(rows == low[:, c : c + SEG], BF16(1.0), BF16(0.0))
        for c in range(0, low.shape[1], SEG)
    ]
    return jnp.concatenate(parts, axis=1)


def lookup_kernel(owners, arrays, width, own_rows, start, end, *refs):
    info, ids = refs[0], refs[1]
    arrays, refs = refs[2 : 2 + arrays], refs[2 + arrays :]
    pieces = entries(arrays)
    count = len(owners)
    at = 0
    if end:
        ups, refs, out, whole_ref = refs[:4], refs[4:-2], refs[-2], refs[-1]
        at = out.shape[1] - ids.shape[1]
        place_rows(info, ups, own_rows, whole_ref)
        out[:, :at] = whole_ref[...].T[: 2 * width]
    else:
        out = refs[-1]
    prior = None if start else refs[0]
    chunks = own_rows // TILE
    for half in range(2):
        lanes = slice(half * width, (half + 1) * width)
        stacks = [
            jnp.concatenate([piece[lanes, c * TILE : (c + 1) * TILE] for c in range(chunks)], axis=0)
            for piece in pieces
        ]

        def part(n, carry):
            cut = pl.ds(pl.multiple_of(n * TILE, TILE), TILE)
            wanted = ids[half : half + 1, cut]
            high = wanted // TILE
            low = (wanted - high * TILE).astype(F32).astype(BF16)
            hot = one_hot(low)
            sofar = jnp.zeros((width, TILE), F32) if start else prior[lanes, cut].astype(F32)
            for stack, owner in zip(stacks, owners):
                got = nn(stack, hot)
                first = (info[1] ^ owner) * chunks
                for c in range(chunks):
                    mine = got[c * width : (c + 1) * width]
                    sofar = sofar + jnp.where(high == first + c, mine, 0.0)
            out[lanes, pl.ds(pl.multiple_of(at + n * TILE, TILE), TILE)] = sofar.astype(BF16)
            return carry

        lax.fori_loop(0, ids.shape[1] // TILE, part, 0)


def lookup(info, pieces, owners, own_rows, ids, prior, ups=()):
    width = pieces[0].shape[-2] // 2
    vm = pl.BlockSpec(memory_space=VMEM)
    operands = [info, ids, *pieces, *ups] + ([] if prior is None else [prior])
    at = 8 * ups[0].shape[1] if ups else 0
    return pl.pallas_call(
        functools.partial(
            lookup_kernel, owners, len(pieces), width, own_rows, prior is None, bool(ups)
        ),
        out_shape=jax.ShapeDtypeStruct((2 * width, at + ids.shape[1]), BF16),
        in_specs=[pl.BlockSpec(memory_space=pltpu.SMEM)] + [vm] * (len(operands) - 1),
        out_specs=vm,
        scratch_shapes=[VMEM((at, SEG), BF16)] if ups else [],
        name="lookup",
    )(*operands)


def spread_kernel(arrays, width, start, end, *refs):
    outs = refs[-2:] if end else refs[-1:]
    info, pieces = refs[0], entries(refs[1 : 1 + arrays])
    prior = None if start else refs[1 + arrays]
    own_rows = outs[0].shape[1]
    chunks = own_rows // TILE
    for half in range(2):
        lanes = slice(half * width, (half + 1) * width)
        sofar = None
        for piece in pieces:
            digits = piece[2 * width :, :]
            high, low = digits[2 * half : 2 * half + 1], digits[2 * half + 1 : 2 * half + 2]
            grads = piece[lanes, :]
            stack = [
                jnp.where(high == (info[1] * chunks + c).astype(F32).astype(BF16), grads, BF16(0.0))
                for c in range(chunks)
            ]
            got = nt(jnp.concatenate(stack, axis=0), one_hot(low))
            sofar = got if sofar is None else sofar + got
        for c in range(chunks):
            cut = slice(c * TILE, (c + 1) * TILE)
            part = sofar[c * width : (c + 1) * width]
            if not start:
                part = part + prior[lanes, cut]
            if end:
                outs[half][:, cut] = part
            else:
                outs[0][lanes, cut] = part


def spread(info, pieces, own_rows, width, prior, end):
    operands = [info, *pieces] + ([] if prior is None else [prior])
    vm = pl.BlockSpec(memory_space=VMEM)
    shapes = [(width, own_rows)] * 2 if end else [(2 * width, own_rows)]
    got = pl.pallas_call(
        functools.partial(spread_kernel, len(pieces), width, prior is None, end),
        out_shape=[jax.ShapeDtypeStruct(shape, F32) for shape in shapes],
        in_specs=[pl.BlockSpec(memory_space=pltpu.SMEM)] + [vm] * (len(operands) - 1),
        out_specs=[vm] * len(shapes),
        name="spread",
    )(*operands)
    return got if end else got[0]


def rope_into(out, row, values, cosine, sine, scale):
    half = HD // 2
    one, two = values[:half], values[half:]
    out[row : row + half, :] = (one * cosine - two * sine).astype(BF16) * scale
    out[row + half : row + HD, :] = (one * sine + two * cosine).astype(BF16) * scale


def key_offset(parent):
    return pl.multiple_of(jnp.where(parent > 0, parent + 1, 0) * SEG, SEG)


def block_keys(parent, start):
    key_at = lax.broadcasted_iota(jnp.int32, (4 * SEG, SEG), 0)
    query_at = lax.broadcasted_iota(jnp.int32, (4 * SEG, SEG), 1)
    limit = jnp.where(parent > 0, 4 * SEG, 3 * SEG)
    seen = (key_at < TILE) | ((key_at - TILE <= query_at) & (key_at < 3 * SEG))
    seen = seen | ((key_at >= 3 * SEG) & (key_at < limit))
    mine = pl.ds(pl.multiple_of(start, SEG), SEG)
    return (slice(0, TILE), mine, pl.ds(key_offset(parent), SEG)), seen


def trunk_seen():
    key_at = lax.broadcasted_iota(jnp.int32, (TILE, TILE), 0)
    return key_at <= lax.broadcasted_iota(jnp.int32, (TILE, TILE), 1)


def front_kernel(
    info,
    set0,
    set1,
    set2,
    set3,
    emb0,
    emb1,
    emb2,
    emb3,
    wqkv,
    gain,
    cos_ref,
    sin_ref,
    resid,
    normed,
    qkv,
    mixed,
    lse,
):
    length, dim = resid.shape
    sets = (set0, set1, set2, set3)
    rows = jnp.concatenate([ref[:, dim:] for ref in sets], axis=0)
    ups = jnp.concatenate([ref[:, :dim] for ref in sets], axis=0)
    own = [pick((emb0, emb1, emb2, emb3), i ^ info[0]) for i in range(length // TILE)]
    hidden = jnp.concatenate(own, axis=0).astype(F32) + tn(rows, ups)
    resid[...] = hidden
    rate = lax.rsqrt(jnp.mean(hidden * hidden, axis=-1, keepdims=True) + EPS)
    norm = (hidden * rate * gain[...]).astype(BF16)
    normed[...] = norm
    proj = nt(wqkv[...], norm)
    cosine, sine = cos_ref[...], sin_ref[...]
    width = mixed.shape[0]
    heads = width // HD
    for h in range(heads):
        rope_into(qkv, h * HD, proj[h * HD : (h + 1) * HD], cosine, sine, BF16(HD**-0.5))
        low = width + h * HD
        rope_into(qkv, low, proj[low : low + HD], cosine, sine, BF16(1.0))
    qkv[2 * width :, :] = proj[2 * width :].astype(BF16)

    def attend(h, lanes, cuts, seen):
        hs = slice(h * HD, (h + 1) * HD)
        ks = slice(width + h * HD, width + (h + 1) * HD)
        vs = slice(2 * width + h * HD, 2 * width + (h + 1) * HD)
        key = jnp.concatenate([qkv[ks, cut] for cut in cuts], axis=1)
        value = jnp.concatenate([qkv[vs, cut] for cut in cuts], axis=1)
        scores = jnp.where(seen, tn(key, qkv[hs, lanes]), MASKED)
        top = jnp.max(scores, axis=0, keepdims=True)
        weights = jnp.exp(scores - top)
        sums = jnp.sum(weights, axis=0, keepdims=True)
        got = nn(value, weights.astype(BF16))
        mixed[hs, lanes] = (got * (1.0 / sums)).astype(BF16)
        lse[h : h + 1, lanes] = top + jnp.log(sums)

    for h in range(heads):
        attend(h, slice(0, TILE), (slice(0, TILE),), trunk_seen())

    def block(j, carry):
        cuts, seen = block_keys(info[2 + j], j * SEG)
        for h in range(heads):
            attend(h, cuts[1], cuts, seen)
        return carry

    lax.fori_loop(TILE // SEG, length // SEG, block, 0)


def front(info, sets, tokens, wqkv, gain, cosine, sine):
    dim = tokens[0].shape[2]
    length = sets[0].shape[1] - dim
    width = wqkv.shape[0] // 3
    vm = pl.BlockSpec(memory_space=VMEM)
    operands = [*sets, *tokens, wqkv, gain, cosine, sine]
    shapes = [
        ((length, dim), F32),
        ((length, dim), BF16),
        ((3 * width, length), BF16),
        ((width, length), BF16),
        ((8, length), F32),
    ]
    return pl.pallas_call(
        front_kernel,
        out_shape=[jax.ShapeDtypeStruct(*shape) for shape in shapes],
        in_specs=[pl.BlockSpec(memory_space=pltpu.SMEM)] + [vm] * len(operands),
        out_specs=[vm] * len(shapes),
        name="front",
    )(info, *operands)


def slot_of(xor):
    return (xor & 1) * 2 + (xor >> 1)


def middle_kernel(
    who,
    mix0,
    mix1,
    mix2,
    mix3,
    out0,
    out1,
    out2,
    out3,
    resid,
    gain,
    ffn0,
    ffn1,
    ffn2,
    ffn3,
    cot0,
    cot1,
    cot2,
    cot3,
    feed_stay,
    feed_leave,
    resid_own,
    normed,
    hidden,
    grads,
    grad_res,
    mix_stay,
    mix_leave,
    grad_gain,
    ffn,
):
    units = hidden.shape[1]
    if len(ffn0.shape) == 3:
        place_rows(who, (ffn0, ffn1, ffn2, ffn3), 0, ffn)
    else:
        ffn[...] = ffn0[...]
    outs = jnp.concatenate([out0[...], out1[...], out2[...], out3[...]], axis=0)
    mix = jnp.concatenate([mix0[...], mix1[...], mix2[...], mix3[...]], axis=0)
    res = resid[...] + tn(mix, outs)
    tiles = range(res.shape[0] // TILE)
    for i in tiles:

        @pl.when(who[0] == i)
        def _():
            resid_own[...] = res[i * TILE : (i + 1) * TILE]

    rate = lax.rsqrt(jnp.mean(res * res, axis=-1, keepdims=True) + EPS)
    norm = (res * rate * gain[...]).astype(BF16)
    normed[...] = norm
    gate = nn(norm, ffn[:, :units])
    upward = nn(norm, ffn[:, units : 2 * units])
    sig = 1.0 / (1.0 + jnp.exp(-gate))
    silu = gate * sig
    hid = (silu * upward).astype(BF16)
    hidden[...] = hid
    fed = nt(hid, ffn[:, 2 * units :]).astype(BF16)
    for i in tiles:
        slot = slot_of(i ^ who[0])
        part = fed[i * TILE : (i + 1) * TILE]

        @pl.when(slot < 2)
        def _():
            feed_stay[slot % 2] = part

        @pl.when(slot >= 2)
        def _():
            feed_leave[slot % 2] = part

    cots = [ref.at[1:2] for ref in (cot0, cot1, cot2, cot3)]
    cot = jnp.concatenate([pick(cots, i ^ who[0]) for i in tiles], axis=0)
    back = nn(cot, ffn[:, 2 * units :])
    grad_gate = (back * upward * sig * (1.0 + gate * (1.0 - sig))).astype(BF16)
    grad_up = (back * silu).astype(BF16)
    grads[:, :units] = grad_gate
    grads[:, units:] = grad_up
    pulled = nt(grad_gate, ffn[:, :units]) + nt(grad_up, ffn[:, units : 2 * units])
    scaled = pulled * gain[...]
    dots = jnp.mean(scaled * res, axis=-1, keepdims=True)
    part = rate * scaled - res * (rate * rate * rate * dots) + 0.25 * cot.astype(F32)
    part = part.astype(BF16)
    grad_res[...] = part
    by_head = nt(outs, part).astype(BF16)
    width = out0.shape[0]
    for k in range(4):
        (mix_stay, mix_leave)[k % 2][k // 2] = by_head[k * width : (k + 1) * width]
    grad_gain[...] = jnp.sum(pulled * res * rate, axis=0, keepdims=True)


def middle(info, mixes, outs, resid, gain, ffns, tokens):
    length, dim = resid.shape
    width = mixes[0].shape[0]
    units = ffns[0].shape[-1] // 3
    vm = pl.BlockSpec(memory_space=VMEM)
    operands = [*mixes, *outs, resid, gain, *ffns, *tokens]
    shapes = [
        ((2, TILE, dim), BF16),
        ((2, TILE, dim), BF16),
        ((TILE, dim), F32),
        ((length, dim), BF16),
        ((length, units), BF16),
        ((length, 2 * units), BF16),
        ((length, dim), BF16),
        ((2, width, length), BF16),
        ((2, width, length), BF16),
        ((1, dim), F32),
    ]
    return pl.pallas_call(
        middle_kernel,
        in_specs=[pl.BlockSpec(memory_space=pltpu.SMEM)] + [vm] * len(operands),
        out_specs=[vm] * len(shapes),
        scratch_shapes=[VMEM((dim, 3 * units), BF16)],
        out_shape=[jax.ShapeDtypeStruct(*shape) for shape in shapes],
        name="middle",
    )(info, *operands)


def unrope_into(out, row, values, cosine, sine):
    half = HD // 2
    one, two = values[:half], values[half:]
    out[row : row + half, :] = (one * cosine + two * sine).astype(BF16)
    out[row + half : row + HD, :] = (two * cosine - one * sine).astype(BF16)


def back_kernel(
    info,
    qkv,
    gmix,
    mixed,
    lse,
    grad_res,
    resid,
    gain,
    gain_two,
    wqkv,
    set0,
    set1,
    set2,
    set3,
    cos_ref,
    sin_ref,
    feed_stay,
    feed_leave,
    out_stay,
    out_leave,
    gproj,
    stay,
    leave,
    up_stay,
    up_leave,
    row_stay,
    row_leave,
    keys_sum,
    vals_sum,
    query_sum,
):
    length, dim = resid.shape
    width = gmix.shape[0]
    heads = width // HD
    keys_sum[...] = jnp.zeros_like(keys_sum)
    vals_sum[...] = jnp.zeros_like(vals_sum)

    def pull(h, lanes, cuts, seen):
        hs = slice(h * HD, (h + 1) * HD)
        ks = slice(width + h * HD, width + (h + 1) * HD)
        vs = slice(2 * width + h * HD, 2 * width + (h + 1) * HD)
        query, grad = qkv[hs, lanes], gmix[hs, lanes]
        key = jnp.concatenate([qkv[ks, cut] for cut in cuts], axis=1)
        value = jnp.concatenate([qkv[vs, cut] for cut in cuts], axis=1)
        delta = jnp.sum(grad.astype(F32) * mixed[hs, lanes].astype(F32), axis=0, keepdims=True)
        scores = jnp.where(seen, tn(key, query), MASKED)
        probs = jnp.exp(scores - lse[h : h + 1, lanes])
        dval = nt(grad, probs.astype(BF16))
        dscore = (probs * (tn(value, grad) - delta)).astype(BF16)
        query_sum[hs, lanes] = nn(key, dscore) * HD**-0.5
        dkey = nt(query, dscore)
        at = 0
        for cut, size in zip(cuts, (TILE, SEG, SEG)):
            keys_sum[hs, cut] += dkey[:, at : at + size]
            vals_sum[hs, cut] += dval[:, at : at + size]
            at += size

    for h in range(heads):
        pull(h, slice(0, TILE), (slice(0, TILE),), trunk_seen())

    def tile(r, carry):
        for half in range(2):
            start = r * TILE + half * SEG
            cuts, seen = block_keys(info[2 + 2 * r + half], start)
            for h in range(heads):
                pull(h, cuts[1], cuts, seen)
        return carry

    lax.fori_loop(1, length // TILE, tile, 0)

    cosine, sine = cos_ref[...], sin_ref[...]
    for h in range(heads):
        hs = slice(h * HD, (h + 1) * HD)
        unrope_into(gproj, h * HD, query_sum[hs, :], cosine, sine)
        unrope_into(gproj, width + h * HD, keys_sum[hs, :], cosine, sine)
    gproj[2 * width :, :] = vals_sum[...].astype(BF16)
    pulled = tn(gproj[...], wqkv[...])
    hidden = resid[...]
    rate = lax.rsqrt(jnp.mean(hidden * hidden, axis=-1, keepdims=True) + EPS)
    scaled = pulled * gain[...]
    dots = jnp.mean(scaled * hidden, axis=-1, keepdims=True)
    part = grad_res[...].astype(F32) + rate * scaled - hidden * (rate * rate * rate * dots)
    part = part.astype(BF16)
    for i in range(length // TILE):
        slot = slot_of(i ^ info[0])
        piece = part[i * TILE : (i + 1) * TILE]

        @pl.when(slot < 2)
        def _():
            stay[slot % 2, :TILE] = piece

        @pl.when(slot >= 2)
        def _():
            leave[slot % 2, :TILE] = piece

    stay[:, TILE:] = feed_stay[...]
    leave[:, TILE:] = feed_leave[...]
    sets = (set0, set1, set2, set3)
    ng = set0.shape[0]
    ups = jnp.concatenate([ref[:, :dim] for ref in sets], axis=0)
    by_column = nt(ups, part).astype(BF16)
    rows = jnp.concatenate([ref[:, dim:] for ref in sets], axis=0)
    grad_ups = nn(rows, part).astype(BF16)
    grad_gain = jnp.sum(pulled * hidden * rate, axis=0, keepdims=True)
    gains = jnp.concatenate([grad_gain, gain_two[...], jnp.zeros((14, dim), F32)], axis=0)
    gains = gains.astype(BF16)
    for k in range(4):
        (row_stay, row_leave)[k % 2][k // 2] = by_column[k * ng : (k + 1) * ng]
        out = (up_stay, up_leave)[k % 2]
        out[k // 2, :ng, :] = grad_ups[k * ng : (k + 1) * ng]
        out[k // 2, ng : ng + width, :] = (out_stay, out_leave)[k % 2][k // 2]
        out[k // 2, ng + width :, :] = gains


def back(
    info, qkv, gmix, mixed, lse, grad_res, resid, gain, gain_part, wqkv, sets, cosine, sine, feeds, outs
):
    length, dim = resid.shape
    width = gmix.shape[0]
    ng = sets[0].shape[0]
    vm = pl.BlockSpec(memory_space=VMEM)
    operands = [qkv, gmix, mixed, lse, grad_res, resid, gain, gain_part, wqkv, *sets, cosine, sine]
    operands += [*feeds, *outs]
    shapes = [(3 * width, length)] + [(2, 2 * TILE, dim)] * 2
    shapes += [(2, ng + width + 16, dim)] * 2 + [(2, ng, length)] * 2
    return pl.pallas_call(
        back_kernel,
        out_shape=[jax.ShapeDtypeStruct(shape, BF16) for shape in shapes],
        in_specs=[pl.BlockSpec(memory_space=pltpu.SMEM)] + [vm] * len(operands),
        out_specs=[vm] * len(shapes),
        scratch_shapes=[VMEM((width, length), F32)] * 3,
        name="back",
    )(info, *operands)


def rotary(parents):
    length = parents.shape[0]
    token = jnp.arange(length, dtype=jnp.int32)
    trunk = 2 * SEG
    inside = token < trunk
    block = jnp.where(inside, 0, (token - trunk) // SEG + 1)
    offset = jnp.where(inside, token, token - trunk - (block - 1) * SEG)
    position = jnp.where(inside, 0, jnp.where(parents == 0, 2 * SEG, 3 * SEG)) + offset
    half = HD // 2
    frequency = ROPE_BASE ** (-(jnp.arange(half, dtype=F32) * 2.0 / HD))
    angles = frequency[:, None] * position.astype(F32)[None, :]
    return jnp.cos(angles), jnp.sin(angles)


def shards(
    dp,
    embedded,
    ids_two,
    ids_three,
    parents,
    table_two,
    table_three,
    w_two,
    w_three,
    norm_attn,
    w_query,
    w_key,
    w_value,
    w_output,
    norm_ffn,
    w_gate,
    w_up,
    w_down,
    cotangent,
):
    own_d = lax.axis_index("dp")
    own_t = lax.axis_index("tensor")
    own_rows, ng = table_two.shape
    rows, dim = embedded.shape
    width = w_query.shape[1]
    units = w_gate.shape[1]
    own_dim = w_query.shape[0]
    gain_one = norm_attn.reshape(1, dim)
    gain_two = norm_ffn.reshape(1, dim)

    ids = jnp.stack([ids_two, ids_three])
    info = jnp.concatenate(
        [jnp.stack([own_t, own_d]).astype(jnp.int32), parents.reshape(-1, SEG)[:, 0]]
    )
    cosine, sine = rotary(parents)

    digits = jnp.stack([ids_two // 256, ids_two % 256, ids_three // 256, ids_three % 256])
    digits = jnp.pad(digits.astype(BF16), ((0, 12), (0, 0)))
    first = pack_first(table_two.T, table_three.T, w_two, w_three)
    attn_pack, ffn_pack = pack(w_query, w_key, w_value, w_output, w_gate, w_up, w_down.T)
    token_pair = jnp.stack([embedded, cotangent])
    token_near = xor_tensor(token_pair, 1)
    if dp == 8:
        arrays, (got, token_near) = double_dp(
            first,
            (attn_pack, ffn_pack, cosine, sine, gain_one, gain_two, digits),
            lambda zero: [lookup(info, [zero], (0, 4), own_rows, ids, None), token_near],
        )
        _, two, one, three = arrays
        token_far = xor_tensor(after(token_pair, arrays[0]), 2)
        got = lookup(info, [two, one], (2, 6, 1, 5), own_rows, ids, got)
        attn_arrays, (got, token_far) = double_dp(
            after(attn_pack, arrays[0]),
            (got,),
            lambda zero: [lookup(info, [three], (3, 7), own_rows, ids, got, arrays), token_far],
        )
        wqkv, wo = assemble(info, attn_arrays, True)
        ffn_arrays, _ = double_dp(after(ffn_pack, two), (attn_arrays[1],))
        wqkv, ffn_zero = lax.optimization_barrier((wqkv, ffn_arrays[0]))
        ffns = (ffn_zero, *ffn_arrays[1:])
    else:
        every = lax.all_gather(first[:, :own_rows], "dp", axis=0)
        small = jnp.concatenate([w_two.astype(BF16).T, w_three.astype(BF16).T], axis=1)
        ups = lax.all_gather(small, "dp", axis=0, tiled=True).T
        wqkvo = lax.all_gather(attn_pack, "dp", axis=0, tiled=True).T
        wqkv, wo = wqkvo[: 3 * width], wqkvo[3 * width :]
        ffns = [lax.all_gather(ffn_pack, "dp", axis=0, tiled=True)]
        ffns += [jnp.zeros((8, SEG), BF16)] * 3
        token_far = xor_tensor(token_pair, 2)

        def take(i, so_far):
            piece = lax.dynamic_index_in_dim(every, i, 0, keepdims=False)
            at = jnp.stack([own_t, i]).astype(jnp.int32)
            return lookup(at, [piece], (0,), own_rows, ids, so_far)

        got = lax.fori_loop(0, dp, take, jnp.zeros((2 * ng, ids.shape[1]), BF16))
        got = jnp.concatenate([ups, got], axis=1)

    tokens = [token_pair, token_near, token_far, xor_tensor(token_far, 1)]
    sets = gather_tensor(got)
    outs = gather_tensor(after(wo, sets[2]))

    resid, normed, qkv, mixed, lse = front(info, sets, tokens, wqkv, gain_one, cosine, sine)
    mixed = after(mixed, outs[2])
    mixes = gather_tensor(mixed)
    (
        feed_stay, feed_leave, resid_own, normed_two, hidden, grads, grad_res, stay, leave,
        gain_part_two,
    ) = middle(info, mixes, outs, resid, gain_two, ffns, tokens)
    near = xor_tensor(leave, 1)
    near_far = add_round(stay[1], near[1])
    far = xor_tensor(near_far, 2)
    halves, out_pair = weigh(
        info, tokens, after(hidden, near_far), normed_two, grads, mixes, grad_res, dp, own_dim
    )
    ffn_sum = SumDp(halves, dp)
    far, _ = lax.optimization_barrier((far, halves))
    gmix = total((stay[0], near[0], far)).astype(BF16)

    gproj, stay, leave, up_stay, up_leave, row_stay, row_leave = back(
        info, qkv, gmix, mixed, lse, grad_res, resid, gain_one, gain_part_two, wqkv, sets,
        cosine, sine, (feed_stay, feed_leave), out_pair,
    )

    near = xor_tensor(row_leave, 1)
    near_far = add_round(row_stay[1], near[1])
    if dp == 8:
        near_far, ffn_sum.first = lax.optimization_barrier((near_far, ffn_sum.first))
        ffn_sum.across()
    far = xor_tensor(near_far, 2)
    gproj = after(gproj, near_far)
    attn_halves = weigh_turned(info, normed, gproj, dp, own_dim)
    attn_sum = SumDp(attn_halves, dp)
    far, _ = lax.optimization_barrier((far, attn_halves))
    row_total = total((row_stay[0], near[0], far)).astype(BF16)
    row_pack = jnp.concatenate([row_total, digits], axis=0)
    up_near = xor_tensor(after(up_leave, near_far), 1)
    up_near_far = after(add_round(up_stay[1], up_near[1]), far)
    up_far = xor_tensor(up_near_far, 2)
    token_near = xor_tensor(after(leave, far), 1)
    token_far = xor_tensor(after(add_round(stay[1], token_near[1]), up_near_far), 2)
    if dp == 8:
        zero = jnp.stack([row_pack, xor_dp(row_pack, 4, dp)])
        zero, attn_sum.first, up_far, ffn_sum.second = lax.optimization_barrier(
            (zero, attn_sum.first, up_far, ffn_sum.second)
        )
    below = add_round(add_round(up_stay[0], up_near[0]), up_far)
    wide_grad, gains = below[: 2 * ng + width], below[2 * ng + width : 2 * ng + width + 2]
    if dp == 8:
        folded = gains.reshape(2 * dim // (2 * ng), 2 * ng)
        halves = turn(info, wide_grad, folded, dp, own_dim)
        two, one, ffn_sum.second, halves = lax.optimization_barrier(
            (xor_dp(zero, 2, dp), xor_dp(zero, 1, dp), ffn_sum.second, halves)
        )
        three = xor_dp(two, 1, dp)
        proj_sum = SumDp(halves, dp)
        ffn_sum.between()
        attn_sum.first = after(attn_sum.first, two)
        attn_sum.across()
        table_grad = spread(info, [zero, two, one], own_rows, ng, None, False)
        proj_sum.first, token_far, table_grad = lax.optimization_barrier(
            (proj_sum.first, token_far, table_grad)
        )
        proj_sum.across()
        ffn_total = ffn_sum.total()
        sums = total((stay[0], token_near[0], token_far))
        embed_grad = sums[:rows].astype(BF16)
        output = (resid_own + sums[rows:]).astype(BF16)
        gate_grad, up_grad, down_grad = (
            ffn_total[:, i * units : (i + 1) * units] for i in range(3)
        )
        attn_sum.second, proj_sum.second, embed_grad, output, table_grad = (
            lax.optimization_barrier(
                (attn_sum.second, proj_sum.second, embed_grad, output, table_grad)
            )
        )
        proj_sum.between()
        attn_sum.between()
        table_grad = spread(info, [three], own_rows, ng, table_grad, True)
        *grads_done, folded = finish(attn_sum, proj_sum, ng)
        gains = folded.reshape(2, dim)
    else:
        every = lax.all_gather(row_pack, "dp", axis=0)

        def put(i, so_far):
            piece = lax.dynamic_index_in_dim(every, i, 0, keepdims=False)
            return spread(info, [piece], own_rows, ng, so_far, False)

        table_grad = lax.fori_loop(0, dp, put, jnp.zeros((2 * ng, own_rows), F32))
        table_grad = table_grad[:ng], table_grad[ng:]
        sums = total((stay[0], token_near[0], token_far))
        embed_grad = sums[:rows].astype(BF16)
        output = (resid_own + sums[rows:]).astype(BF16)
        ffn_total = ffn_sum.total()
        gate_grad, up_grad, down_grad = (
            ffn_total[:, i * units : (i + 1) * units] for i in range(3)
        )
        attn_total = attn_sum.total()
        wide_total = SumDp(turn(info, wide_grad, None, dp, own_dim), dp).total()
        grads_done = [attn_total[:, i * width : (i + 1) * width] for i in range(3)]
        grads_done += [wide_total[:, :ng].T, wide_total[:, ng : 2 * ng].T, wide_total[:, 2 * ng :].T]
        gains = lax.psum(gains.astype(F32), "dp")
    query_grad, key_grad, value_grad, two_grad, three_grad, output_grad = grads_done

    return (
        output,
        embed_grad,
        table_grad[0].T,
        table_grad[1].T,
        two_grad,
        three_grad,
        gains[0],
        query_grad,
        key_grad,
        value_grad,
        output_grad,
        gains[1],
        gate_grad,
        up_grad,
        down_grad.T,
    )


def solution(mesh):
    tokens = P(("dp", "tensor"), None)
    down, across = P("dp", "tensor"), P("tensor", "dp")
    in_specs = (
        (tokens, P("dp"), P("dp"), P("dp"), down, down, across, across, P())
        + (down, down, down, across, P(), down, down, across, tokens)
    )
    out_specs = (
        (tokens, tokens, down, down, across, across, P())
        + (down, down, down, across, P(), down, down, across)
    )
    body = functools.partial(shards, mesh.shape["dp"])
    return jax.shard_map(body, mesh=mesh, in_specs=in_specs, out_specs=out_specs, check_vma=False)
```

```python
import functools

import jax
import jax.numpy as jnp
from jax import lax
from jax.experimental import pallas as pl
from jax.experimental.pallas import tpu as pltpu
from jax.sharding import PartitionSpec as P

HD = 64
SEG = 128
TILE = 2 * SEG
EPS = 1e-05
MASKED = -1e30
ROPE_BASE = 10000.0
F32 = jnp.float32
BF16 = jnp.bfloat16
VMEM = pltpu.VMEM


def xor_tensor(value, step):
    return lax.ppermute(value, "tensor", [(i, i ^ step) for i in range(4)])


def xor_dp(value, step, count):
    return lax.ppermute(value, "dp", [(i, i ^ step) for i in range(count)])


def after(value, *others):
    return lax.optimization_barrier((value,) + others)[0]


def gather_tensor(value):
    far = xor_tensor(value, 2)
    near = xor_tensor(value, 1)
    return [value, near, far, xor_tensor(far, 1)]


def add_round(one, two):
    return (one.astype(F32) + two.astype(F32)).astype(BF16)


def scatter_tensor(stay, leave):
    come = xor_tensor(leave, 1)
    far = xor_tensor(add_round(stay[1], come[1]), 2)
    return stay[0], come[0], far


def total(terms):
    return terms[0].astype(F32) + terms[1].astype(F32) + terms[2].astype(F32)


def double_dp(value, others=(), window=lambda zero: ()):
    zero = jnp.stack([value, after(xor_dp(value, 4, 8), *others)])
    made = window(zero)
    two, one, *made = lax.optimization_barrier((xor_dp(zero, 2, 8), xor_dp(zero, 1, 8), *made))
    return (zero, two, one, xor_dp(two, 1, 8)), made


DOUBLED = (0, 4, 2, 6, 1, 5, 3, 7)
HALVED = (0, 2, 1, 3)


def halve_first(keep, come):
    return add_round(keep[:2], come[:2]), add_round(keep[2:], come[2:])


def halve_second(stay, come):
    return add_round(stay[0], come[0]), add_round(stay[1], come[1])


class SumDp:
    def __init__(self, halves, count):
        self.count, self.halves = count, halves
        if count == 8:
            away, self.keep = halves
            self.first = xor_dp(away, 1, count)

    def across(self):
        if self.count == 8:
            self.stay, leave = halve_first(self.keep, self.first)
            self.second = xor_dp(leave, 2, self.count)

    def total(self):
        if self.count != 8:
            values = self.halves[0].astype(F32)
            return lax.psum_scatter(values, "dp", scatter_dimension=0, tiled=True)[0]
        return self.ours.astype(F32) + self.third.astype(F32)

    def between(self):
        if self.count == 8:
            self.ours, leave = halve_second(self.stay, self.second)
            self.third = xor_dp(leave, 4, self.count)


def entries(refs):
    out = []
    for ref in refs:
        out += [ref] if len(ref.shape) == 2 else [ref.at[i] for i in range(ref.shape[0])]
    return out


def place_rows(info, refs, lane, whole_ref):
    for piece, xor in zip(entries(refs), DOUBLED):
        rows = piece.shape[0]
        at = pl.ds(pl.multiple_of((info[1] ^ xor) * rows, 16), rows)
        whole_ref[at, :] = piece[:, lane : lane + whole_ref.shape[1]]


def assemble_kernel(turn, info, *refs):
    pieces, out = refs[:4], refs[4]
    whole_ref = refs[-1] if turn else out
    place_rows(info, pieces, 0, whole_ref)
    if turn:
        turned = whole_ref[...].T
        out[...] = turned[: out.shape[0]]
        refs[5][...] = turned[out.shape[0] :]


def assemble(info, arrays, turn):
    rows, cols = arrays[0].shape[1:]
    shapes = [(8 * rows, cols)]
    if turn:
        shapes = [(cols - cols // 4, 8 * rows), (cols // 4, 8 * rows)]
    return pl.pallas_call(
        functools.partial(assemble_kernel, turn),
        out_shape=[jax.ShapeDtypeStruct(shape, BF16) for shape in shapes],
        in_specs=[pl.BlockSpec(memory_space=pltpu.SMEM)] + [pl.BlockSpec(memory_space=VMEM)] * 4,
        out_specs=[pl.BlockSpec(memory_space=VMEM)] * len(shapes),
        scratch_shapes=[VMEM((8 * rows, cols), BF16)] if turn else [],
        name="assemble",
    )(info, *arrays)


def pick(refs, which):
    value = refs[3][0]
    for k in range(3):
        value = jnp.where(which == k, refs[k][0], value)
    return value


def whole(shape):
    return pl.BlockSpec(shape, lambda *_: (0,) * len(shape))


def nn(a, b):
    return lax.dot_general(a, b, (((1,), (0,)), ((), ())), preferred_element_type=F32)


def nt(a, b):
    return lax.dot_general(a, b, (((1,), (1,)), ((), ())), preferred_element_type=F32)


def tn(a, b):
    return lax.dot_general(a, b, (((0,), (0,)), ((), ())), preferred_element_type=F32)


def pack_first_kernel(two, three, up_two, up_three, out):
    ng, rows = two.shape
    out[:ng, :rows] = two[...].astype(BF16)
    out[ng:, :rows] = three[...].astype(BF16)
    out[:, rows:] = jnp.zeros((2 * ng, SEG), BF16)
    if up_two.shape[1] == 2 * ng:
        small = jnp.concatenate([up_two[...], up_three[...]], axis=0)
        out[:, rows : rows + 2 * ng] = small.T.astype(BF16)


def pack_first(two, three, up_two, up_three):
    ng, rows = two.shape
    return pl.pallas_call(
        pack_first_kernel,
        out_shape=jax.ShapeDtypeStruct((2 * ng, rows + SEG), BF16),
        name="pack_first",
    )(two, three, up_two, up_three)


def pack_kernel(query, key, value, output, gate, up, down, attn, ffn):
    width, units = query.shape[1], gate.shape[1]
    for i, ref in enumerate((query, key, value)):
        attn[:, i * width : (i + 1) * width] = ref[...].astype(BF16)
    attn[:, 3 * width :] = output[...].T.astype(BF16)
    for i, ref in enumerate((gate, up, down)):
        ffn[:, i * units : (i + 1) * units] = ref[...].astype(BF16)


def pack(query, key, value, output, gate, up, down):
    rows, width = query.shape
    return pl.pallas_call(
        pack_kernel,
        out_shape=[
            jax.ShapeDtypeStruct((rows, 4 * width), BF16),
            jax.ShapeDtypeStruct((rows, 3 * gate.shape[1]), BF16),
        ],
        name="pack",
    )(query, key, value, output, gate, up, down)


def split_rows(info, whole_ref, outs, rows):
    if len(outs) == 1:
        for i in range(outs[0].shape[0]):
            outs[0][i] = whole_ref[i * rows : (i + 1) * rows, :]
        return
    for entry, xor in enumerate(HALVED):
        for out, other in zip(outs, (1, 0)):
            at = info[1] ^ (2 * xor + other)
            out[entry] = whole_ref[pl.ds(pl.multiple_of(at * rows, 16), rows), :]


def weigh_kernel(rows, halves, info, hidden, norm, grads, *refs):
    cots, mixes, grad, refs = refs[:4], refs[4:8], refs[8], refs[9:]
    outs, (stay, leave, turned, whole_ref) = refs[:halves], refs[halves:]
    at = grads.shape[1]
    for tile in range(4):
        cot = pick([ref.at[1:2] for ref in cots], tile ^ info[0])
        turned[:, tile * TILE : (tile + 1) * TILE] = cot.T
    whole_ref[:, at:] = nn(turned[...], hidden[...]).astype(BF16)
    turned[...] = norm[...].T
    whole_ref[:, :at] = nn(turned[...], grads[...]).astype(BF16)
    split_rows(info, whole_ref, outs, rows)
    for xor in range(4):
        (stay, leave)[xor % 2][xor // 2] = nn(mixes[xor][...], grad[...]).astype(BF16)


def weigh(info, tokens, hidden, norm, grads, mixes, grad, count, own_dim):
    length, dim = norm.shape
    lead = [4, 4] if count == 8 else [count]
    cols = hidden.shape[1] + grads.shape[1]
    shapes = [(n, own_dim, cols) for n in lead] + [(2, mixes[0].shape[0], dim)] * 2
    operands = [hidden, norm, grads, *tokens, *mixes, grad]
    vm = pl.BlockSpec(memory_space=VMEM)
    got = pl.pallas_call(
        functools.partial(weigh_kernel, own_dim, len(lead)),
        in_specs=[pl.BlockSpec(memory_space=pltpu.SMEM)] + [vm] * len(operands),
        out_specs=[vm] * len(shapes),
        scratch_shapes=[VMEM((dim, length), BF16), VMEM((dim, cols), BF16)],
        out_shape=[jax.ShapeDtypeStruct(shape, BF16) for shape in shapes],
        name="weigh",
    )(info, *operands)
    return got[: len(lead)], got[len(lead) :]


def weigh_turned_kernel(rows, info, left, right, *refs):
    outs, whole_ref = refs[:-1], refs[-1]
    whole_ref[...] = nn(right[...], left[...]).astype(BF16).T
    split_rows(info, whole_ref, outs, rows)


def turn_kernel(rows, info, wide, *refs):
    outs, whole_ref = refs[:-1], refs[-1]
    whole_ref[...] = wide[...].T
    split_rows(info, whole_ref, outs, rows)


def turn_below_kernel(rows, info, wide, below, *refs):
    outs = refs[:-1]
    turn_kernel(rows, info, wide, *(out.at[:, :rows] for out in outs), refs[-1])
    for out in outs:
        for z in range(out.shape[0]):
            out[z, rows:, : below.shape[1]] = below[...]


def split_call(body, info, operands, count, own_dim, cols, below=0):
    vm = pl.BlockSpec(memory_space=VMEM)
    lead = [4, 4] if count == 8 else [count]
    shapes = [jax.ShapeDtypeStruct((n, own_dim + below, cols), BF16) for n in lead]
    return pl.pallas_call(
        functools.partial(body, own_dim),
        out_shape=shapes,
        in_specs=[pl.BlockSpec(memory_space=pltpu.SMEM)] + [vm] * len(operands),
        out_specs=[vm] * len(shapes),
        scratch_shapes=[VMEM((count * own_dim, cols), BF16)],
        name="split",
    )(info, *operands)


def weigh_turned(info, left, right, count, own_dim):
    return split_call(weigh_turned_kernel, info, [left, right], count, own_dim, right.shape[0])


def turn(info, wide, below, count, own_dim):
    if below is None:
        return split_call(turn_kernel, info, [wide], count, own_dim, wide.shape[0])
    return split_call(
        turn_below_kernel, info, [wide, below], count, own_dim, wide.shape[0], below.shape[0]
    )


def finish_kernel(attn, attn_come, wide, wide_come, query, key, value, two, three, output, gains):
    width, ng = query.shape[1], two.shape[0]
    rows = query.shape[0]
    sums = attn[...].astype(F32) + attn_come[...].astype(F32)
    for i, out in enumerate((query, key, value)):
        out[...] = sums[:, i * width : (i + 1) * width]
    sums = wide[...].astype(F32) + wide_come[...].astype(F32)
    turned = sums[:rows].T
    two[...] = turned[:ng]
    three[...] = turned[ng : 2 * ng]
    output[...] = turned[2 * ng :]
    gains[...] = sums[rows:, : gains.shape[1]]


def finish(attn_sum, wide_sum, ng):
    rows, cols = attn_sum.ours.shape
    width = cols // 3
    operands = [attn_sum.ours, attn_sum.third, wide_sum.ours, wide_sum.third]
    below = wide_sum.ours.shape[0] - rows
    shapes = [(rows, width)] * 3 + [(ng, rows)] * 2 + [(width, rows), (below, 2 * ng)]
    vm = pl.BlockSpec(memory_space=VMEM)
    return pl.pallas_call(
        finish_kernel,
        out_shape=[jax.ShapeDtypeStruct(shape, F32) for shape in shapes],
        in_specs=[vm] * 4,
        out_specs=[vm] * 7,
        name="finish",
    )(*operands)


def one_hot(low):
    rows = lax.broadcasted_iota(jnp.int32, (TILE, SEG), 0).astype(F32).astype(BF16)
    parts = [
        jnp.where(rows == low[:, c : c + SEG], BF16(1.0), BF16(0.0))
        for c in range(0, low.shape[1], SEG)
    ]
    return jnp.concatenate(parts, axis=1)


def lookup_kernel(owners, arrays, width, own_rows, start, end, *refs):
    info, ids = refs[0], refs[1]
    arrays, refs = refs[2 : 2 + arrays], refs[2 + arrays :]
    pieces = entries(arrays)
    count = len(owners)
    at = 0
    if end:
        ups, refs, out, whole_ref = refs[:4], refs[4:-2], refs[-2], refs[-1]
        at = out.shape[1] - ids.shape[1]
        place_rows(info, ups, own_rows, whole_ref)
        out[:, :at] = whole_ref[...].T[: 2 * width]
    else:
        out = refs[-1]
    prior = None if start else refs[0]
    chunks = own_rows // TILE
    for half in range(2):
        lanes = slice(half * width, (half + 1) * width)
        stacks = [
            jnp.concatenate([piece[lanes, c * TILE : (c + 1) * TILE] for c in range(chunks)], axis=0)
            for piece in pieces
        ]

        def part(n, carry):
            cut = pl.ds(pl.multiple_of(n * TILE, TILE), TILE)
            wanted = ids[half : half + 1, cut]
            high = wanted // TILE
            low = (wanted - high * TILE).astype(F32).astype(BF16)
            hot = one_hot(low)
            sofar = jnp.zeros((width, TILE), F32) if start else prior[lanes, cut].astype(F32)
            for stack, owner in zip(stacks, owners):
                got = nn(stack, hot)
                first = (info[1] ^ owner) * chunks
                for c in range(chunks):
                    mine = got[c * width : (c + 1) * width]
                    sofar = sofar + jnp.where(high == first + c, mine, 0.0)
            out[lanes, pl.ds(pl.multiple_of(at + n * TILE, TILE), TILE)] = sofar.astype(BF16)
            return carry

        lax.fori_loop(0, ids.shape[1] // TILE, part, 0)


def lookup(info, pieces, owners, own_rows, ids, prior, ups=()):
    width = pieces[0].shape[-2] // 2
    vm = pl.BlockSpec(memory_space=VMEM)
    operands = [info, ids, *pieces, *ups] + ([] if prior is None else [prior])
    at = 8 * ups[0].shape[1] if ups else 0
    return pl.pallas_call(
        functools.partial(
            lookup_kernel, owners, len(pieces), width, own_rows, prior is None, bool(ups)
        ),
        out_shape=jax.ShapeDtypeStruct((2 * width, at + ids.shape[1]), BF16),
        in_specs=[pl.BlockSpec(memory_space=pltpu.SMEM)] + [vm] * (len(operands) - 1),
        out_specs=vm,
        scratch_shapes=[VMEM((at, SEG), BF16)] if ups else [],
        name="lookup",
    )(*operands)


def spread_kernel(arrays, width, start, end, *refs):
    outs = refs[-2:] if end else refs[-1:]
    info, pieces = refs[0], entries(refs[1 : 1 + arrays])
    prior = None if start else refs[1 + arrays]
    own_rows = outs[0].shape[1]
    chunks = own_rows // TILE
    for half in range(2):
        lanes = slice(half * width, (half + 1) * width)
        sofar = None
        for piece in pieces:
            digits = piece[2 * width :, :]
            high, low = digits[2 * half : 2 * half + 1], digits[2 * half + 1 : 2 * half + 2]
            grads = piece[lanes, :]
            stack = [
                jnp.where(high == (info[1] * chunks + c).astype(F32).astype(BF16), grads, BF16(0.0))
                for c in range(chunks)
            ]
            got = nt(jnp.concatenate(stack, axis=0), one_hot(low))
            sofar = got if sofar is None else sofar + got
        for c in range(chunks):
            cut = slice(c * TILE, (c + 1) * TILE)
            part = sofar[c * width : (c + 1) * width]
            if not start:
                part = part + prior[lanes, cut]
            if end:
                outs[half][:, cut] = part
            else:
                outs[0][lanes, cut] = part


def spread(info, pieces, own_rows, width, prior, end):
    operands = [info, *pieces] + ([] if prior is None else [prior])
    vm = pl.BlockSpec(memory_space=VMEM)
    shapes = [(width, own_rows)] * 2 if end else [(2 * width, own_rows)]
    got = pl.pallas_call(
        functools.partial(spread_kernel, len(pieces), width, prior is None, end),
        out_shape=[jax.ShapeDtypeStruct(shape, F32) for shape in shapes],
        in_specs=[pl.BlockSpec(memory_space=pltpu.SMEM)] + [vm] * (len(operands) - 1),
        out_specs=[vm] * len(shapes),
        name="spread",
    )(*operands)
    return got if end else got[0]


def rope_into(out, row, values, cosine, sine, scale):
    half = HD // 2
    one, two = values[:half], values[half:]
    out[row : row + half, :] = (one * cosine - two * sine).astype(BF16) * scale
    out[row + half : row + HD, :] = (one * sine + two * cosine).astype(BF16) * scale


def key_offset(parent):
    return pl.multiple_of(jnp.where(parent > 0, parent + 1, 0) * SEG, SEG)


def block_keys(parent, start):
    key_at = lax.broadcasted_iota(jnp.int32, (4 * SEG, SEG), 0)
    query_at = lax.broadcasted_iota(jnp.int32, (4 * SEG, SEG), 1)
    limit = jnp.where(parent > 0, 4 * SEG, 3 * SEG)
    seen = (key_at < TILE) | ((key_at - TILE <= query_at) & (key_at < 3 * SEG))
    seen = seen | ((key_at >= 3 * SEG) & (key_at < limit))
    mine = pl.ds(pl.multiple_of(start, SEG), SEG)
    return (slice(0, TILE), mine, pl.ds(key_offset(parent), SEG)), seen


def trunk_seen():
    key_at = lax.broadcasted_iota(jnp.int32, (TILE, TILE), 0)
    return key_at <= lax.broadcasted_iota(jnp.int32, (TILE, TILE), 1)


def front_kernel(
    info,
    set0,
    set1,
    set2,
    set3,
    emb0,
    emb1,
    emb2,
    emb3,
    wqkv,
    gain,
    cos_ref,
    sin_ref,
    resid,
    normed,
    qkv,
    mixed,
    lse,
):
    length, dim = resid.shape
    sets = (set0, set1, set2, set3)
    rows = jnp.concatenate([ref[:, dim:] for ref in sets], axis=0)
    ups = jnp.concatenate([ref[:, :dim] for ref in sets], axis=0)
    own = [pick((emb0, emb1, emb2, emb3), i ^ info[0]) for i in range(length // TILE)]
    hidden = jnp.concatenate(own, axis=0).astype(F32) + tn(rows, ups)
    resid[...] = hidden
    rate = lax.rsqrt(jnp.mean(hidden * hidden, axis=-1, keepdims=True) + EPS)
    norm = (hidden * rate * gain[...]).astype(BF16)
    normed[...] = norm
    proj = nt(wqkv[...], norm)
    cosine, sine = cos_ref[...], sin_ref[...]
    width = mixed.shape[0]
    heads = width // HD
    for h in range(heads):
        rope_into(qkv, h * HD, proj[h * HD : (h + 1) * HD], cosine, sine, BF16(HD**-0.5))
        low = width + h * HD
        rope_into(qkv, low, proj[low : low + HD], cosine, sine, BF16(1.0))
    qkv[2 * width :, :] = proj[2 * width :].astype(BF16)

    def attend(h, lanes, cuts, seen):
        hs = slice(h * HD, (h + 1) * HD)
        ks = slice(width + h * HD, width + (h + 1) * HD)
        vs = slice(2 * width + h * HD, 2 * width + (h + 1) * HD)
        key = jnp.concatenate([qkv[ks, cut] for cut in cuts], axis=1)
        value = jnp.concatenate([qkv[vs, cut] for cut in cuts], axis=1)
        scores = jnp.where(seen, tn(key, qkv[hs, lanes]), MASKED)
        top = jnp.max(scores, axis=0, keepdims=True)
        weights = jnp.exp(scores - top)
        sums = jnp.sum(weights, axis=0, keepdims=True)
        got = nn(value, weights.astype(BF16))
        mixed[hs, lanes] = (got * (1.0 / sums)).astype(BF16)
        lse[h : h + 1, lanes] = top + jnp.log(sums)

    for h in range(heads):
        attend(h, slice(0, TILE), (slice(0, TILE),), trunk_seen())

    def block(j, carry):
        cuts, seen = block_keys(info[2 + j], j * SEG)
        for h in range(heads):
            attend(h, cuts[1], cuts, seen)
        return carry

    lax.fori_loop(TILE // SEG, length // SEG, block, 0)


def front(info, sets, tokens, wqkv, gain, cosine, sine):
    dim = tokens[0].shape[2]
    length = sets[0].shape[1] - dim
    width = wqkv.shape[0] // 3
    vm = pl.BlockSpec(memory_space=VMEM)
    operands = [*sets, *tokens, wqkv, gain, cosine, sine]
    shapes = [
        ((length, dim), F32),
        ((length, dim), BF16),
        ((3 * width, length), BF16),
        ((width, length), BF16),
        ((8, length), F32),
    ]
    return pl.pallas_call(
        front_kernel,
        out_shape=[jax.ShapeDtypeStruct(*shape) for shape in shapes],
        in_specs=[pl.BlockSpec(memory_space=pltpu.SMEM)] + [vm] * len(operands),
        out_specs=[vm] * len(shapes),
        name="front",
    )(info, *operands)


def slot_of(xor):
    return (xor & 1) * 2 + (xor >> 1)


def middle_kernel(
    who,
    mix0,
    mix1,
    mix2,
    mix3,
    out0,
    out1,
    out2,
    out3,
    resid,
    gain,
    ffn0,
    ffn1,
    ffn2,
    ffn3,
    cot0,
    cot1,
    cot2,
    cot3,
    feed_stay,
    feed_leave,
    resid_own,
    normed,
    hidden,
    grads,
    grad_res,
    mix_stay,
    mix_leave,
    grad_gain,
    ffn,
):
    units = hidden.shape[1]
    if len(ffn0.shape) == 3:
        place_rows(who, (ffn0, ffn1, ffn2, ffn3), 0, ffn)
    else:
        ffn[...] = ffn0[...]
    outs = jnp.concatenate([out0[...], out1[...], out2[...], out3[...]], axis=0)
    mix = jnp.concatenate([mix0[...], mix1[...], mix2[...], mix3[...]], axis=0)
    res = resid[...] + tn(mix, outs)
    tiles = range(res.shape[0] // TILE)
    for i in tiles:

        @pl.when(who[0] == i)
        def _():
            resid_own[...] = res[i * TILE : (i + 1) * TILE]

    rate = lax.rsqrt(jnp.mean(res * res, axis=-1, keepdims=True) + EPS)
    norm = (res * rate * gain[...]).astype(BF16)
    normed[...] = norm
    gate = nn(norm, ffn[:, :units])
    upward = nn(norm, ffn[:, units : 2 * units])
    sig = 1.0 / (1.0 + jnp.exp(-gate))
    silu = gate * sig
    hid = (silu * upward).astype(BF16)
    hidden[...] = hid
    fed = nt(hid, ffn[:, 2 * units :]).astype(BF16)
    for i in tiles:
        slot = slot_of(i ^ who[0])
        part = fed[i * TILE : (i + 1) * TILE]

        @pl.when(slot < 2)
        def _():
            feed_stay[slot % 2] = part

        @pl.when(slot >= 2)
        def _():
            feed_leave[slot % 2] = part

    cots = [ref.at[1:2] for ref in (cot0, cot1, cot2, cot3)]
    cot = jnp.concatenate([pick(cots, i ^ who[0]) for i in tiles], axis=0)
    back = nn(cot, ffn[:, 2 * units :])
    grad_gate = (back * upward * sig * (1.0 + gate * (1.0 - sig))).astype(BF16)
    grad_up = (back * silu).astype(BF16)
    grads[:, :units] = grad_gate
    grads[:, units:] = grad_up
    pulled = nt(grad_gate, ffn[:, :units]) + nt(grad_up, ffn[:, units : 2 * units])
    scaled = pulled * gain[...]
    dots = jnp.mean(scaled * res, axis=-1, keepdims=True)
    part = rate * scaled - res * (rate * rate * rate * dots) + 0.25 * cot.astype(F32)
    part = part.astype(BF16)
    grad_res[...] = part
    by_head = nt(outs, part).astype(BF16)
    width = out0.shape[0]
    for k in range(4):
        (mix_stay, mix_leave)[k % 2][k // 2] = by_head[k * width : (k + 1) * width]
    grad_gain[...] = jnp.sum(pulled * res * rate, axis=0, keepdims=True)


def middle(info, mixes, outs, resid, gain, ffns, tokens):
    length, dim = resid.shape
    width = mixes[0].shape[0]
    units = ffns[0].shape[-1] // 3
    vm = pl.BlockSpec(memory_space=VMEM)
    operands = [*mixes, *outs, resid, gain, *ffns, *tokens]
    shapes = [
        ((2, TILE, dim), BF16),
        ((2, TILE, dim), BF16),
        ((TILE, dim), F32),
        ((length, dim), BF16),
        ((length, units), BF16),
        ((length, 2 * units), BF16),
        ((length, dim), BF16),
        ((2, width, length), BF16),
        ((2, width, length), BF16),
        ((1, dim), F32),
    ]
    return pl.pallas_call(
        middle_kernel,
        in_specs=[pl.BlockSpec(memory_space=pltpu.SMEM)] + [vm] * len(operands),
        out_specs=[vm] * len(shapes),
        scratch_shapes=[VMEM((dim, 3 * units), BF16)],
        out_shape=[jax.ShapeDtypeStruct(*shape) for shape in shapes],
        name="middle",
    )(info, *operands)


def unrope_into(out, row, values, cosine, sine):
    half = HD // 2
    one, two = values[:half], values[half:]
    out[row : row + half, :] = (one * cosine + two * sine).astype(BF16)
    out[row + half : row + HD, :] = (two * cosine - one * sine).astype(BF16)


def back_kernel(
    info,
    qkv,
    gmix,
    mixed,
    lse,
    grad_res,
    resid,
    gain,
    gain_two,
    wqkv,
    set0,
    set1,
    set2,
    set3,
    cos_ref,
    sin_ref,
    feed_stay,
    feed_leave,
    out_stay,
    out_leave,
    gproj,
    stay,
    leave,
    up_stay,
    up_leave,
    row_stay,
    row_leave,
    keys_sum,
    vals_sum,
    query_sum,
):
    length, dim = resid.shape
    width = gmix.shape[0]
    heads = width // HD
    keys_sum[...] = jnp.zeros_like(keys_sum)
    vals_sum[...] = jnp.zeros_like(vals_sum)

    def pull(h, lanes, cuts, seen):
        hs = slice(h * HD, (h + 1) * HD)
        ks = slice(width + h * HD, width + (h + 1) * HD)
        vs = slice(2 * width + h * HD, 2 * width + (h + 1) * HD)
        query, grad = qkv[hs, lanes], gmix[hs, lanes]
        key = jnp.concatenate([qkv[ks, cut] for cut in cuts], axis=1)
        value = jnp.concatenate([qkv[vs, cut] for cut in cuts], axis=1)
        delta = jnp.sum(grad.astype(F32) * mixed[hs, lanes].astype(F32), axis=0, keepdims=True)
        scores = jnp.where(seen, tn(key, query), MASKED)
        probs = jnp.exp(scores - lse[h : h + 1, lanes])
        dval = nt(grad, probs.astype(BF16))
        dscore = (probs * (tn(value, grad) - delta)).astype(BF16)
        query_sum[hs, lanes] = nn(key, dscore) * HD**-0.5
        dkey = nt(query, dscore)
        at = 0
        for cut, size in zip(cuts, (TILE, SEG, SEG)):
            keys_sum[hs, cut] += dkey[:, at : at + size]
            vals_sum[hs, cut] += dval[:, at : at + size]
            at += size

    for h in range(heads):
        pull(h, slice(0, TILE), (slice(0, TILE),), trunk_seen())

    def tile(r, carry):
        for half in range(2):
            start = r * TILE + half * SEG
            cuts, seen = block_keys(info[2 + 2 * r + half], start)
            for h in range(heads):
                pull(h, cuts[1], cuts, seen)
        return carry

    lax.fori_loop(1, length // TILE, tile, 0)

    cosine, sine = cos_ref[...], sin_ref[...]
    for h in range(heads):
        hs = slice(h * HD, (h + 1) * HD)
        unrope_into(gproj, h * HD, query_sum[hs, :], cosine, sine)
        unrope_into(gproj, width + h * HD, keys_sum[hs, :], cosine, sine)
    gproj[2 * width :, :] = vals_sum[...].astype(BF16)
    pulled = tn(gproj[...], wqkv[...])
    hidden = resid[...]
    rate = lax.rsqrt(jnp.mean(hidden * hidden, axis=-1, keepdims=True) + EPS)
    scaled = pulled * gain[...]
    dots = jnp.mean(scaled * hidden, axis=-1, keepdims=True)
    part = grad_res[...].astype(F32) + rate * scaled - hidden * (rate * rate * rate * dots)
    part = part.astype(BF16)
    for i in range(length // TILE):
        slot = slot_of(i ^ info[0])
        piece = part[i * TILE : (i + 1) * TILE]

        @pl.when(slot < 2)
        def _():
            stay[slot % 2, :TILE] = piece

        @pl.when(slot >= 2)
        def _():
            leave[slot % 2, :TILE] = piece

    stay[:, TILE:] = feed_stay[...]
    leave[:, TILE:] = feed_leave[...]
    sets = (set0, set1, set2, set3)
    ng = set0.shape[0]
    ups = jnp.concatenate([ref[:, :dim] for ref in sets], axis=0)
    by_column = nt(ups, part).astype(BF16)
    rows = jnp.concatenate([ref[:, dim:] for ref in sets], axis=0)
    grad_ups = nn(rows, part).astype(BF16)
    grad_gain = jnp.sum(pulled * hidden * rate, axis=0, keepdims=True)
    gains = jnp.concatenate([grad_gain, gain_two[...], jnp.zeros((14, dim), F32)], axis=0)
    gains = gains.astype(BF16)
    for k in range(4):
        (row_stay, row_leave)[k % 2][k // 2] = by_column[k * ng : (k + 1) * ng]
        out = (up_stay, up_leave)[k % 2]
        out[k // 2, :ng, :] = grad_ups[k * ng : (k + 1) * ng]
        out[k // 2, ng : ng + width, :] = (out_stay, out_leave)[k % 2][k // 2]
        out[k // 2, ng + width :, :] = gains


def back(
    info, qkv, gmix, mixed, lse, grad_res, resid, gain, gain_part, wqkv, sets, cosine, sine, feeds, outs
):
    length, dim = resid.shape
    width = gmix.shape[0]
    ng = sets[0].shape[0]
    vm = pl.BlockSpec(memory_space=VMEM)
    operands = [qkv, gmix, mixed, lse, grad_res, resid, gain, gain_part, wqkv, *sets, cosine, sine]
    operands += [*feeds, *outs]
    shapes = [(3 * width, length)] + [(2, 2 * TILE, dim)] * 2
    shapes += [(2, ng + width + 16, dim)] * 2 + [(2, ng, length)] * 2
    return pl.pallas_call(
        back_kernel,
        out_shape=[jax.ShapeDtypeStruct(shape, BF16) for shape in shapes],
        in_specs=[pl.BlockSpec(memory_space=pltpu.SMEM)] + [vm] * len(operands),
        out_specs=[vm] * len(shapes),
        scratch_shapes=[VMEM((width, length), F32)] * 3,
        name="back",
    )(info, *operands)


def rotary(parents):
    length = parents.shape[0]
    token = jnp.arange(length, dtype=jnp.int32)
    trunk = 2 * SEG
    inside = token < trunk
    block = jnp.where(inside, 0, (token - trunk) // SEG + 1)
    offset = jnp.where(inside, token, token - trunk - (block - 1) * SEG)
    position = jnp.where(inside, 0, jnp.where(parents == 0, 2 * SEG, 3 * SEG)) + offset
    half = HD // 2
    frequency = ROPE_BASE ** (-(jnp.arange(half, dtype=F32) * 2.0 / HD))
    angles = frequency[:, None] * position.astype(F32)[None, :]
    return jnp.cos(angles), jnp.sin(angles)


def shards(
    dp,
    embedded,
    ids_two,
    ids_three,
    parents,
    table_two,
    table_three,
    w_two,
    w_three,
    norm_attn,
    w_query,
    w_key,
    w_value,
    w_output,
    norm_ffn,
    w_gate,
    w_up,
    w_down,
    cotangent,
):
    own_d = lax.axis_index("dp")
    own_t = lax.axis_index("tensor")
    own_rows, ng = table_two.shape
    rows, dim = embedded.shape
    width = w_query.shape[1]
    units = w_gate.shape[1]
    own_dim = w_query.shape[0]
    gain_one = norm_attn.reshape(1, dim)
    gain_two = norm_ffn.reshape(1, dim)

    ids = jnp.stack([ids_two, ids_three])
    info = jnp.concatenate(
        [jnp.stack([own_t, own_d]).astype(jnp.int32), parents.reshape(-1, SEG)[:, 0]]
    )
    cosine, sine = rotary(parents)

    digits = jnp.stack([ids_two // 256, ids_two % 256, ids_three // 256, ids_three % 256])
    digits = jnp.pad(digits.astype(BF16), ((0, 12), (0, 0)))
    first = pack_first(table_two.T, table_three.T, w_two, w_three)
    attn_pack, ffn_pack = pack(w_query, w_key, w_value, w_output, w_gate, w_up, w_down.T)
    token_pair = jnp.stack([embedded, cotangent])
    token_near = xor_tensor(token_pair, 1)
    if dp == 8:
        arrays, (got, token_near) = double_dp(
            first,
            (attn_pack, ffn_pack, cosine, sine, gain_one, gain_two, digits),
            lambda zero: [lookup(info, [zero], (0, 4), own_rows, ids, None), token_near],
        )
        _, two, one, three = arrays
        token_far = xor_tensor(after(token_pair, arrays[0]), 2)
        got = lookup(info, [two, one], (2, 6, 1, 5), own_rows, ids, got)
        attn_arrays, (got, token_far) = double_dp(
            after(attn_pack, arrays[0]),
            (got,),
            lambda zero: [lookup(info, [three], (3, 7), own_rows, ids, got, arrays), token_far],
        )
        wqkv, wo = assemble(info, attn_arrays, True)
        ffn_arrays, _ = double_dp(after(ffn_pack, two), (attn_arrays[1],))
        wqkv, ffn_zero = lax.optimization_barrier((wqkv, ffn_arrays[0]))
        ffns = (ffn_zero, *ffn_arrays[1:])
    else:
        every = lax.all_gather(first[:, :own_rows], "dp", axis=0)
        small = jnp.concatenate([w_two.astype(BF16).T, w_three.astype(BF16).T], axis=1)
        ups = lax.all_gather(small, "dp", axis=0, tiled=True).T
        wqkvo = lax.all_gather(attn_pack, "dp", axis=0, tiled=True).T
        wqkv, wo = wqkvo[: 3 * width], wqkvo[3 * width :]
        ffns = [lax.all_gather(ffn_pack, "dp", axis=0, tiled=True)]
        ffns += [jnp.zeros((8, SEG), BF16)] * 3
        token_far = xor_tensor(token_pair, 2)

        def take(i, so_far):
            piece = lax.dynamic_index_in_dim(every, i, 0, keepdims=False)
            at = jnp.stack([own_t, i]).astype(jnp.int32)
            return lookup(at, [piece], (0,), own_rows, ids, so_far)

        got = lax.fori_loop(0, dp, take, jnp.zeros((2 * ng, ids.shape[1]), BF16))
        got = jnp.concatenate([ups, got], axis=1)

    tokens = [token_pair, token_near, token_far, xor_tensor(token_far, 1)]
    sets = gather_tensor(got)
    outs = gather_tensor(after(wo, sets[2]))

    resid, normed, qkv, mixed, lse = front(info, sets, tokens, wqkv, gain_one, cosine, sine)
    mixed = after(mixed, outs[2])
    mixes = gather_tensor(mixed)
    (
        feed_stay, feed_leave, resid_own, normed_two, hidden, grads, grad_res, stay, leave,
        gain_part_two,
    ) = middle(info, mixes, outs, resid, gain_two, ffns, tokens)
    near = xor_tensor(leave, 1)
    near_far = add_round(stay[1], near[1])
    far = xor_tensor(near_far, 2)
    halves, out_pair = weigh(
        info, tokens, after(hidden, near_far), normed_two, grads, mixes, grad_res, dp, own_dim
    )
    ffn_sum = SumDp(halves, dp)
    far, _ = lax.optimization_barrier((far, halves))
    gmix = total((stay[0], near[0], far)).astype(BF16)

    gproj, stay, leave, up_stay, up_leave, row_stay, row_leave = back(
        info, qkv, gmix, mixed, lse, grad_res, resid, gain_one, gain_part_two, wqkv, sets,
        cosine, sine, (feed_stay, feed_leave), out_pair,
    )

    near = xor_tensor(row_leave, 1)
    near_far = add_round(row_stay[1], near[1])
    if dp == 8:
        near_far, ffn_sum.first = lax.optimization_barrier((near_far, ffn_sum.first))
        ffn_sum.across()
    far = xor_tensor(near_far, 2)
    gproj = after(gproj, near_far)
    attn_halves = weigh_turned(info, normed, gproj, dp, own_dim)
    attn_sum = SumDp(attn_halves, dp)
    far, _ = lax.optimization_barrier((far, attn_halves))
    row_total = total((row_stay[0], near[0], far)).astype(BF16)
    row_pack = jnp.concatenate([row_total, digits], axis=0)
    up_near = xor_tensor(after(up_leave, near_far), 1)
    up_near_far = after(add_round(up_stay[1], up_near[1]), far)
    up_far = xor_tensor(up_near_far, 2)
    token_near = xor_tensor(after(leave, far), 1)
    token_far = xor_tensor(after(add_round(stay[1], token_near[1]), up_near_far), 2)
    if dp == 8:
        zero = jnp.stack([row_pack, xor_dp(row_pack, 4, dp)])
        zero, attn_sum.first, up_far, ffn_sum.second = lax.optimization_barrier(
            (zero, attn_sum.first, up_far, ffn_sum.second)
        )
    below = add_round(add_round(up_stay[0], up_near[0]), up_far)
    wide_grad, gains = below[: 2 * ng + width], below[2 * ng + width : 2 * ng + width + 2]
    if dp == 8:
        folded = gains.reshape(2 * dim // (2 * ng), 2 * ng)
        halves = turn(info, wide_grad, folded, dp, own_dim)
        proj_sum = SumDp(halves, dp)
        ffn_sum.between()
        two, one, ffn_sum.third, proj_sum.first = lax.optimization_barrier(
            (xor_dp(zero, 2, dp), xor_dp(zero, 1, dp), ffn_sum.third, proj_sum.first)
        )
        three = xor_dp(two, 1, dp)
        attn_sum.first = after(attn_sum.first, two)
        attn_sum.across()
        proj_sum.across()
        zero = after(zero, attn_sum.stay, proj_sum.stay)
        table_grad = spread(info, [zero, two, one], own_rows, ng, None, False)
        attn_sum.second, proj_sum.second, token_far, table_grad = lax.optimization_barrier(
            (attn_sum.second, proj_sum.second, token_far, table_grad)
        )
        attn_sum.between()
        proj_sum.between()
        token_far, ffn_sum.third = (
            after(x, attn_sum.ours, proj_sum.ours) for x in (token_far, ffn_sum.third)
        )
        ffn_total = ffn_sum.total()
        sums = total((stay[0], token_near[0], token_far))
        embed_grad = sums[:rows].astype(BF16)
        output = (resid_own + sums[rows:]).astype(BF16)
        gate_grad, up_grad, down_grad = (
            ffn_total[:, i * units : (i + 1) * units] for i in range(3)
        )
        embed_grad, output, table_grad = lax.optimization_barrier(
            (embed_grad, output, table_grad)
        )
        table_grad = spread(info, [three], own_rows, ng, table_grad, True)
        *grads_done, folded = finish(attn_sum, proj_sum, ng)
        gains = folded.reshape(2, dim)
    else:
        every = lax.all_gather(row_pack, "dp", axis=0)

        def put(i, so_far):
            piece = lax.dynamic_index_in_dim(every, i, 0, keepdims=False)
            return spread(info, [piece], own_rows, ng, so_far, False)

        table_grad = lax.fori_loop(0, dp, put, jnp.zeros((2 * ng, own_rows), F32))
        table_grad = table_grad[:ng], table_grad[ng:]
        sums = total((stay[0], token_near[0], token_far))
        embed_grad = sums[:rows].astype(BF16)
        output = (resid_own + sums[rows:]).astype(BF16)
        ffn_total = ffn_sum.total()
        gate_grad, up_grad, down_grad = (
            ffn_total[:, i * units : (i + 1) * units] for i in range(3)
        )
        attn_total = attn_sum.total()
        wide_total = SumDp(turn(info, wide_grad, None, dp, own_dim), dp).total()
        grads_done = [attn_total[:, i * width : (i + 1) * width] for i in range(3)]
        grads_done += [wide_total[:, :ng].T, wide_total[:, ng : 2 * ng].T, wide_total[:, 2 * ng :].T]
        gains = lax.psum(gains.astype(F32), "dp")
    query_grad, key_grad, value_grad, two_grad, three_grad, output_grad = grads_done

    return (
        output,
        embed_grad,
        table_grad[0].T,
        table_grad[1].T,
        two_grad,
        three_grad,
        gains[0],
        query_grad,
        key_grad,
        value_grad,
        output_grad,
        gains[1],
        gate_grad,
        up_grad,
        down_grad.T,
    )


def solution(mesh):
    tokens = P(("dp", "tensor"), None)
    down, across = P("dp", "tensor"), P("tensor", "dp")
    in_specs = (
        (tokens, P("dp"), P("dp"), P("dp"), down, down, across, across, P())
        + (down, down, down, across, P(), down, down, across, tokens)
    )
    out_specs = (
        (tokens, tokens, down, down, across, across, P())
        + (down, down, down, across, P(), down, down, across)
    )
    body = functools.partial(shards, mesh.shape["dp"])
    return jax.shard_map(body, mesh=mesh, in_specs=in_specs, out_specs=out_specs, check_vma=False)
```

```python
import functools

import jax
import jax.numpy as jnp
from jax import lax
from jax.experimental import pallas as pl
from jax.experimental.pallas import tpu as pltpu
from jax.sharding import PartitionSpec as P

HD = 64
SEG = 128
TILE = 2 * SEG
EPS = 1e-05
MASKED = -1e30
ROPE_BASE = 10000.0
F32 = jnp.float32
BF16 = jnp.bfloat16
VMEM = pltpu.VMEM


def xor_tensor(value, step):
    return lax.ppermute(value, "tensor", [(i, i ^ step) for i in range(4)])


def xor_dp(value, step, count):
    return lax.ppermute(value, "dp", [(i, i ^ step) for i in range(count)])


def after(value, *others):
    return lax.optimization_barrier((value,) + others)[0]


def gather_tensor(value):
    far = xor_tensor(value, 2)
    near = xor_tensor(value, 1)
    return [value, near, far, xor_tensor(far, 1)]


def add_round(one, two):
    return (one.astype(F32) + two.astype(F32)).astype(BF16)


def scatter_tensor(stay, leave):
    come = xor_tensor(leave, 1)
    far = xor_tensor(add_round(stay[1], come[1]), 2)
    return stay[0], come[0], far


def total(terms):
    return terms[0].astype(F32) + terms[1].astype(F32) + terms[2].astype(F32)


def double_dp(value, others=(), window=lambda zero: ()):
    zero = jnp.stack([value, after(xor_dp(value, 4, 8), *others)])
    made = window(zero)
    two, one, *made = lax.optimization_barrier((xor_dp(zero, 2, 8), xor_dp(zero, 1, 8), *made))
    return (zero, two, one, xor_dp(two, 1, 8)), made


DOUBLED = (0, 4, 2, 6, 1, 5, 3, 7)
HALVED = (0, 2, 1, 3)


def halve_first(keep, come):
    return add_round(keep[:2], come[:2]), add_round(keep[2:], come[2:])


def halve_second(stay, come):
    return add_round(stay[0], come[0]), add_round(stay[1], come[1])


class SumDp:
    def __init__(self, halves, count):
        self.count, self.halves = count, halves
        if count == 8:
            away, self.keep = halves
            self.first = xor_dp(away, 1, count)

    def across(self):
        if self.count == 8:
            self.stay, leave = halve_first(self.keep, self.first)
            self.second = xor_dp(leave, 2, self.count)

    def total(self):
        if self.count != 8:
            values = self.halves[0].astype(F32)
            return lax.psum_scatter(values, "dp", scatter_dimension=0, tiled=True)[0]
        return self.ours.astype(F32) + self.third.astype(F32)

    def between(self):
        if self.count == 8:
            self.ours, leave = halve_second(self.stay, self.second)
            self.third = xor_dp(leave, 4, self.count)


def entries(refs):
    out = []
    for ref in refs:
        out += [ref] if len(ref.shape) == 2 else [ref.at[i] for i in range(ref.shape[0])]
    return out


def place_rows(info, refs, lane, whole_ref):
    for piece, xor in zip(entries(refs), DOUBLED):
        rows = piece.shape[0]
        at = pl.ds(pl.multiple_of((info[1] ^ xor) * rows, 16), rows)
        whole_ref[at, :] = piece[:, lane : lane + whole_ref.shape[1]]


def assemble_kernel(turn, info, *refs):
    pieces, out = refs[:4], refs[4]
    whole_ref = refs[-1] if turn else out
    place_rows(info, pieces, 0, whole_ref)
    if turn:
        turned = whole_ref[...].T
        out[...] = turned[: out.shape[0]]
        refs[5][...] = turned[out.shape[0] :]


def assemble(info, arrays, turn):
    rows, cols = arrays[0].shape[1:]
    shapes = [(8 * rows, cols)]
    if turn:
        shapes = [(cols - cols // 4, 8 * rows), (cols // 4, 8 * rows)]
    return pl.pallas_call(
        functools.partial(assemble_kernel, turn),
        out_shape=[jax.ShapeDtypeStruct(shape, BF16) for shape in shapes],
        in_specs=[pl.BlockSpec(memory_space=pltpu.SMEM)] + [pl.BlockSpec(memory_space=VMEM)] * 4,
        out_specs=[pl.BlockSpec(memory_space=VMEM)] * len(shapes),
        scratch_shapes=[VMEM((8 * rows, cols), BF16)] if turn else [],
        name="assemble",
    )(info, *arrays)


def pick(refs, which):
    value = refs[3][0]
    for k in range(3):
        value = jnp.where(which == k, refs[k][0], value)
    return value


def whole(shape):
    return pl.BlockSpec(shape, lambda *_: (0,) * len(shape))


def nn(a, b):
    return lax.dot_general(a, b, (((1,), (0,)), ((), ())), preferred_element_type=F32)


def nt(a, b):
    return lax.dot_general(a, b, (((1,), (1,)), ((), ())), preferred_element_type=F32)


def tn(a, b):
    return lax.dot_general(a, b, (((0,), (0,)), ((), ())), preferred_element_type=F32)


def pack_first_kernel(two, three, up_two, up_three, out):
    ng, rows = two.shape
    out[:ng, :rows] = two[...].astype(BF16)
    out[ng:, :rows] = three[...].astype(BF16)
    out[:, rows:] = jnp.zeros((2 * ng, SEG), BF16)
    if up_two.shape[1] == 2 * ng:
        small = jnp.concatenate([up_two[...], up_three[...]], axis=0)
        out[:, rows : rows + 2 * ng] = small.T.astype(BF16)


def pack_first(two, three, up_two, up_three):
    ng, rows = two.shape
    return pl.pallas_call(
        pack_first_kernel,
        out_shape=jax.ShapeDtypeStruct((2 * ng, rows + SEG), BF16),
        name="pack_first",
    )(two, three, up_two, up_three)


def pack_kernel(query, key, value, output, gate, up, down, attn, ffn):
    width, units = query.shape[1], gate.shape[1]
    for i, ref in enumerate((query, key, value)):
        attn[:, i * width : (i + 1) * width] = ref[...].astype(BF16)
    attn[:, 3 * width :] = output[...].T.astype(BF16)
    for i, ref in enumerate((gate, up, down)):
        ffn[:, i * units : (i + 1) * units] = ref[...].astype(BF16)


def pack(query, key, value, output, gate, up, down):
    rows, width = query.shape
    return pl.pallas_call(
        pack_kernel,
        out_shape=[
            jax.ShapeDtypeStruct((rows, 4 * width), BF16),
            jax.ShapeDtypeStruct((rows, 3 * gate.shape[1]), BF16),
        ],
        name="pack",
    )(query, key, value, output, gate, up, down)


def split_rows(info, whole_ref, outs, rows):
    if len(outs) == 1:
        for i in range(outs[0].shape[0]):
            outs[0][i] = whole_ref[i * rows : (i + 1) * rows, :]
        return
    for entry, xor in enumerate(HALVED):
        for out, other in zip(outs, (1, 0)):
            at = info[1] ^ (2 * xor + other)
            out[entry] = whole_ref[pl.ds(pl.multiple_of(at * rows, 16), rows), :]


def weigh_kernel(rows, halves, info, hidden, norm, grads, *refs):
    cots, mixes, grad, refs = refs[:4], refs[4:8], refs[8], refs[9:]
    outs, (stay, leave, turned, whole_ref) = refs[:halves], refs[halves:]
    at = grads.shape[1]
    for tile in range(4):
        cot = pick([ref.at[1:2] for ref in cots], tile ^ info[0])
        turned[:, tile * TILE : (tile + 1) * TILE] = cot.T
    whole_ref[:, at:] = nn(turned[...], hidden[...]).astype(BF16)
    turned[...] = norm[...].T
    whole_ref[:, :at] = nn(turned[...], grads[...]).astype(BF16)
    split_rows(info, whole_ref, outs, rows)
    for xor in range(4):
        (stay, leave)[xor % 2][xor // 2] = nn(mixes[xor][...], grad[...]).astype(BF16)


def weigh(info, tokens, hidden, norm, grads, mixes, grad, count, own_dim):
    length, dim = norm.shape
    lead = [4, 4] if count == 8 else [count]
    cols = hidden.shape[1] + grads.shape[1]
    shapes = [(n, own_dim, cols) for n in lead] + [(2, mixes[0].shape[0], dim)] * 2
    operands = [hidden, norm, grads, *tokens, *mixes, grad]
    vm = pl.BlockSpec(memory_space=VMEM)
    got = pl.pallas_call(
        functools.partial(weigh_kernel, own_dim, len(lead)),
        in_specs=[pl.BlockSpec(memory_space=pltpu.SMEM)] + [vm] * len(operands),
        out_specs=[vm] * len(shapes),
        scratch_shapes=[VMEM((dim, length), BF16), VMEM((dim, cols), BF16)],
        out_shape=[jax.ShapeDtypeStruct(shape, BF16) for shape in shapes],
        name="weigh",
    )(info, *operands)
    return got[: len(lead)], got[len(lead) :]


def weigh_turned_kernel(rows, info, left, right, *refs):
    outs, whole_ref = refs[:-1], refs[-1]
    whole_ref[...] = nn(right[...], left[...]).astype(BF16).T
    split_rows(info, whole_ref, outs, rows)


def turn_kernel(rows, info, wide, *refs):
    outs, whole_ref = refs[:-1], refs[-1]
    whole_ref[...] = wide[...].T
    split_rows(info, whole_ref, outs, rows)


def turn_below_kernel(rows, info, wide, below, *refs):
    outs = refs[:-1]
    turn_kernel(rows, info, wide, *(out.at[:, :rows] for out in outs), refs[-1])
    for out in outs:
        for z in range(out.shape[0]):
            out[z, rows:, : below.shape[1]] = below[...]


def split_call(body, info, operands, count, own_dim, cols, below=0):
    vm = pl.BlockSpec(memory_space=VMEM)
    lead = [4, 4] if count == 8 else [count]
    shapes = [jax.ShapeDtypeStruct((n, own_dim + below, cols), BF16) for n in lead]
    return pl.pallas_call(
        functools.partial(body, own_dim),
        out_shape=shapes,
        in_specs=[pl.BlockSpec(memory_space=pltpu.SMEM)] + [vm] * len(operands),
        out_specs=[vm] * len(shapes),
        scratch_shapes=[VMEM((count * own_dim, cols), BF16)],
        name="split",
    )(info, *operands)


def weigh_turned(info, left, right, count, own_dim):
    return split_call(weigh_turned_kernel, info, [left, right], count, own_dim, right.shape[0])


def turn(info, wide, below, count, own_dim):
    if below is None:
        return split_call(turn_kernel, info, [wide], count, own_dim, wide.shape[0])
    return split_call(
        turn_below_kernel, info, [wide, below], count, own_dim, wide.shape[0], below.shape[0]
    )


def finish_kernel(
    attn, attn_come, wide, wide_come, ffn, ffn_come,
    query, key, value, two, three, output, gains, gate, up, down,
):
    width, ng = query.shape[1], two.shape[0]
    rows = query.shape[0]
    sums = attn[...].astype(F32) + attn_come[...].astype(F32)
    for i, out in enumerate((query, key, value)):
        out[...] = sums[:, i * width : (i + 1) * width]
    sums = wide[...].astype(F32) + wide_come[...].astype(F32)
    turned = sums[:rows].T
    two[...] = turned[:ng]
    three[...] = turned[ng : 2 * ng]
    output[...] = turned[2 * ng :]
    gains[...] = sums[rows:, : gains.shape[1]]
    units = gate.shape[1]
    for i, out in enumerate((gate, up, down)):
        cut = slice(i * units, (i + 1) * units)
        out[...] = ffn[:, cut].astype(F32) + ffn_come[:, cut].astype(F32)


def finish(attn_sum, wide_sum, ffn_sum, ng):
    rows, cols = attn_sum.ours.shape
    width = cols // 3
    operands = [attn_sum.ours, attn_sum.third, wide_sum.ours, wide_sum.third]
    operands += [ffn_sum.ours, ffn_sum.third]
    below = wide_sum.ours.shape[0] - rows
    shapes = [(rows, width)] * 3 + [(ng, rows)] * 2 + [(width, rows), (below, 2 * ng)]
    shapes += [(rows, ffn_sum.ours.shape[1] // 3)] * 3
    vm = pl.BlockSpec(memory_space=VMEM)
    return pl.pallas_call(
        finish_kernel,
        out_shape=[jax.ShapeDtypeStruct(shape, F32) for shape in shapes],
        in_specs=[vm] * len(operands),
        out_specs=[vm] * len(shapes),
        name="finish",
    )(*operands)


def one_hot(low):
    rows = lax.broadcasted_iota(jnp.int32, (TILE, SEG), 0).astype(F32).astype(BF16)
    parts = [
        jnp.where(rows == low[:, c : c + SEG], BF16(1.0), BF16(0.0))
        for c in range(0, low.shape[1], SEG)
    ]
    return jnp.concatenate(parts, axis=1)


def lookup_kernel(owners, arrays, width, own_rows, start, end, *refs):
    info, ids = refs[0], refs[1]
    arrays, refs = refs[2 : 2 + arrays], refs[2 + arrays :]
    pieces = entries(arrays)
    count = len(owners)
    at = 0
    if end:
        ups, refs, out, whole_ref = refs[:4], refs[4:-2], refs[-2], refs[-1]
        at = out.shape[1] - ids.shape[1]
        place_rows(info, ups, own_rows, whole_ref)
        out[:, :at] = whole_ref[...].T[: 2 * width]
    else:
        out = refs[-1]
    prior = None if start else refs[0]
    chunks = own_rows // TILE
    for half in range(2):
        lanes = slice(half * width, (half + 1) * width)
        stacks = [
            jnp.concatenate([piece[lanes, c * TILE : (c + 1) * TILE] for c in range(chunks)], axis=0)
            for piece in pieces
        ]

        def part(n, carry):
            cut = pl.ds(pl.multiple_of(n * TILE, TILE), TILE)
            wanted = ids[half : half + 1, cut]
            high = wanted // TILE
            low = (wanted - high * TILE).astype(F32).astype(BF16)
            hot = one_hot(low)
            sofar = jnp.zeros((width, TILE), F32) if start else prior[lanes, cut].astype(F32)
            for stack, owner in zip(stacks, owners):
                got = nn(stack, hot)
                first = (info[1] ^ owner) * chunks
                for c in range(chunks):
                    mine = got[c * width : (c + 1) * width]
                    sofar = sofar + jnp.where(high == first + c, mine, 0.0)
            out[lanes, pl.ds(pl.multiple_of(at + n * TILE, TILE), TILE)] = sofar.astype(BF16)
            return carry

        lax.fori_loop(0, ids.shape[1] // TILE, part, 0)


def lookup(info, pieces, owners, own_rows, ids, prior, ups=()):
    width = pieces[0].shape[-2] // 2
    vm = pl.BlockSpec(memory_space=VMEM)
    operands = [info, ids, *pieces, *ups] + ([] if prior is None else [prior])
    at = 8 * ups[0].shape[1] if ups else 0
    return pl.pallas_call(
        functools.partial(
            lookup_kernel, owners, len(pieces), width, own_rows, prior is None, bool(ups)
        ),
        out_shape=jax.ShapeDtypeStruct((2 * width, at + ids.shape[1]), BF16),
        in_specs=[pl.BlockSpec(memory_space=pltpu.SMEM)] + [vm] * (len(operands) - 1),
        out_specs=vm,
        scratch_shapes=[VMEM((at, SEG), BF16)] if ups else [],
        name="lookup",
    )(*operands)


def spread_kernel(arrays, width, start, end, *refs):
    outs = refs[-2:] if end else refs[-1:]
    info, pieces = refs[0], entries(refs[1 : 1 + arrays])
    prior = None if start else refs[1 + arrays]
    own_rows = outs[0].shape[1]
    chunks = own_rows // TILE
    for half in range(2):
        lanes = slice(half * width, (half + 1) * width)
        sofar = None
        for piece in pieces:
            digits = piece[2 * width :, :]
            high, low = digits[2 * half : 2 * half + 1], digits[2 * half + 1 : 2 * half + 2]
            grads = piece[lanes, :]
            stack = [
                jnp.where(high == (info[1] * chunks + c).astype(F32).astype(BF16), grads, BF16(0.0))
                for c in range(chunks)
            ]
            got = nt(jnp.concatenate(stack, axis=0), one_hot(low))
            sofar = got if sofar is None else sofar + got
        for c in range(chunks):
            cut = slice(c * TILE, (c + 1) * TILE)
            part = sofar[c * width : (c + 1) * width]
            if not start:
                part = part + prior[lanes, cut]
            if end:
                outs[half][:, cut] = part
            else:
                outs[0][lanes, cut] = part


def spread(info, pieces, own_rows, width, prior, end):
    operands = [info, *pieces] + ([] if prior is None else [prior])
    vm = pl.BlockSpec(memory_space=VMEM)
    shapes = [(width, own_rows)] * 2 if end else [(2 * width, own_rows)]
    got = pl.pallas_call(
        functools.partial(spread_kernel, len(pieces), width, prior is None, end),
        out_shape=[jax.ShapeDtypeStruct(shape, F32) for shape in shapes],
        in_specs=[pl.BlockSpec(memory_space=pltpu.SMEM)] + [vm] * (len(operands) - 1),
        out_specs=[vm] * len(shapes),
        name="spread",
    )(*operands)
    return got if end else got[0]


def rope_into(out, row, values, cosine, sine, scale):
    half = HD // 2
    one, two = values[:half], values[half:]
    out[row : row + half, :] = (one * cosine - two * sine).astype(BF16) * scale
    out[row + half : row + HD, :] = (one * sine + two * cosine).astype(BF16) * scale


def key_offset(parent):
    return pl.multiple_of(jnp.where(parent > 0, parent + 1, 0) * SEG, SEG)


def block_keys(parent, start):
    key_at = lax.broadcasted_iota(jnp.int32, (4 * SEG, SEG), 0)
    query_at = lax.broadcasted_iota(jnp.int32, (4 * SEG, SEG), 1)
    limit = jnp.where(parent > 0, 4 * SEG, 3 * SEG)
    seen = (key_at < TILE) | ((key_at - TILE <= query_at) & (key_at < 3 * SEG))
    seen = seen | ((key_at >= 3 * SEG) & (key_at < limit))
    mine = pl.ds(pl.multiple_of(start, SEG), SEG)
    return (slice(0, TILE), mine, pl.ds(key_offset(parent), SEG)), seen


def trunk_seen():
    key_at = lax.broadcasted_iota(jnp.int32, (TILE, TILE), 0)
    return key_at <= lax.broadcasted_iota(jnp.int32, (TILE, TILE), 1)


def front_kernel(
    info,
    set0,
    set1,
    set2,
    set3,
    emb0,
    emb1,
    emb2,
    emb3,
    wqkv,
    gain,
    cos_ref,
    sin_ref,
    resid,
    normed,
    qkv,
    mixed,
    lse,
):
    length, dim = resid.shape
    sets = (set0, set1, set2, set3)
    rows = jnp.concatenate([ref[:, dim:] for ref in sets], axis=0)
    ups = jnp.concatenate([ref[:, :dim] for ref in sets], axis=0)
    own = [pick((emb0, emb1, emb2, emb3), i ^ info[0]) for i in range(length // TILE)]
    hidden = jnp.concatenate(own, axis=0).astype(F32) + tn(rows, ups)
    resid[...] = hidden
    rate = lax.rsqrt(jnp.mean(hidden * hidden, axis=-1, keepdims=True) + EPS)
    norm = (hidden * rate * gain[...]).astype(BF16)
    normed[...] = norm
    proj = nt(wqkv[...], norm)
    cosine, sine = cos_ref[...], sin_ref[...]
    width = mixed.shape[0]
    heads = width // HD
    for h in range(heads):
        rope_into(qkv, h * HD, proj[h * HD : (h + 1) * HD], cosine, sine, BF16(HD**-0.5))
        low = width + h * HD
        rope_into(qkv, low, proj[low : low + HD], cosine, sine, BF16(1.0))
    qkv[2 * width :, :] = proj[2 * width :].astype(BF16)

    def attend(h, lanes, cuts, seen):
        hs = slice(h * HD, (h + 1) * HD)
        ks = slice(width + h * HD, width + (h + 1) * HD)
        vs = slice(2 * width + h * HD, 2 * width + (h + 1) * HD)
        key = jnp.concatenate([qkv[ks, cut] for cut in cuts], axis=1)
        value = jnp.concatenate([qkv[vs, cut] for cut in cuts], axis=1)
        scores = jnp.where(seen, tn(key, qkv[hs, lanes]), MASKED)
        top = jnp.max(scores, axis=0, keepdims=True)
        weights = jnp.exp(scores - top)
        sums = jnp.sum(weights, axis=0, keepdims=True)
        got = nn(value, weights.astype(BF16))
        mixed[hs, lanes] = (got * (1.0 / sums)).astype(BF16)
        lse[h : h + 1, lanes] = top + jnp.log(sums)

    for h in range(heads):
        attend(h, slice(0, TILE), (slice(0, TILE),), trunk_seen())

    def block(j, carry):
        cuts, seen = block_keys(info[2 + j], j * SEG)
        for h in range(heads):
            attend(h, cuts[1], cuts, seen)
        return carry

    lax.fori_loop(TILE // SEG, length // SEG, block, 0)


def front(info, sets, tokens, wqkv, gain, cosine, sine):
    dim = tokens[0].shape[2]
    length = sets[0].shape[1] - dim
    width = wqkv.shape[0] // 3
    vm = pl.BlockSpec(memory_space=VMEM)
    operands = [*sets, *tokens, wqkv, gain, cosine, sine]
    shapes = [
        ((length, dim), F32),
        ((length, dim), BF16),
        ((3 * width, length), BF16),
        ((width, length), BF16),
        ((8, length), F32),
    ]
    return pl.pallas_call(
        front_kernel,
        out_shape=[jax.ShapeDtypeStruct(*shape) for shape in shapes],
        in_specs=[pl.BlockSpec(memory_space=pltpu.SMEM)] + [vm] * len(operands),
        out_specs=[vm] * len(shapes),
        name="front",
    )(info, *operands)


def slot_of(xor):
    return (xor & 1) * 2 + (xor >> 1)


def middle_kernel(
    who,
    mix0,
    mix1,
    mix2,
    mix3,
    out0,
    out1,
    out2,
    out3,
    resid,
    gain,
    ffn0,
    ffn1,
    ffn2,
    ffn3,
    cot0,
    cot1,
    cot2,
    cot3,
    feed_stay,
    feed_leave,
    resid_own,
    normed,
    hidden,
    grads,
    grad_res,
    mix_stay,
    mix_leave,
    grad_gain,
    ffn,
):
    units = hidden.shape[1]
    if len(ffn0.shape) == 3:
        place_rows(who, (ffn0, ffn1, ffn2, ffn3), 0, ffn)
    else:
        ffn[...] = ffn0[...]
    outs = jnp.concatenate([out0[...], out1[...], out2[...], out3[...]], axis=0)
    mix = jnp.concatenate([mix0[...], mix1[...], mix2[...], mix3[...]], axis=0)
    res = resid[...] + tn(mix, outs)
    tiles = range(res.shape[0] // TILE)
    for i in tiles:

        @pl.when(who[0] == i)
        def _():
            resid_own[...] = res[i * TILE : (i + 1) * TILE]

    rate = lax.rsqrt(jnp.mean(res * res, axis=-1, keepdims=True) + EPS)
    norm = (res * rate * gain[...]).astype(BF16)
    normed[...] = norm
    gate = nn(norm, ffn[:, :units])
    upward = nn(norm, ffn[:, units : 2 * units])
    sig = 1.0 / (1.0 + jnp.exp(-gate))
    silu = gate * sig
    hid = (silu * upward).astype(BF16)
    hidden[...] = hid
    fed = nt(hid, ffn[:, 2 * units :]).astype(BF16)
    for i in tiles:
        slot = slot_of(i ^ who[0])
        part = fed[i * TILE : (i + 1) * TILE]

        @pl.when(slot < 2)
        def _():
            feed_stay[slot % 2] = part

        @pl.when(slot >= 2)
        def _():
            feed_leave[slot % 2] = part

    cots = [ref.at[1:2] for ref in (cot0, cot1, cot2, cot3)]
    cot = jnp.concatenate([pick(cots, i ^ who[0]) for i in tiles], axis=0)
    back = nn(cot, ffn[:, 2 * units :])
    grad_gate = (back * upward * sig * (1.0 + gate * (1.0 - sig))).astype(BF16)
    grad_up = (back * silu).astype(BF16)
    grads[:, :units] = grad_gate
    grads[:, units:] = grad_up
    pulled = nt(grad_gate, ffn[:, :units]) + nt(grad_up, ffn[:, units : 2 * units])
    scaled = pulled * gain[...]
    dots = jnp.mean(scaled * res, axis=-1, keepdims=True)
    part = rate * scaled - res * (rate * rate * rate * dots) + 0.25 * cot.astype(F32)
    part = part.astype(BF16)
    grad_res[...] = part
    by_head = nt(outs, part).astype(BF16)
    width = out0.shape[0]
    for k in range(4):
        (mix_stay, mix_leave)[k % 2][k // 2] = by_head[k * width : (k + 1) * width]
    grad_gain[...] = jnp.sum(pulled * res * rate, axis=0, keepdims=True)


def middle(info, mixes, outs, resid, gain, ffns, tokens):
    length, dim = resid.shape
    width = mixes[0].shape[0]
    units = ffns[0].shape[-1] // 3
    vm = pl.BlockSpec(memory_space=VMEM)
    operands = [*mixes, *outs, resid, gain, *ffns, *tokens]
    shapes = [
        ((2, TILE, dim), BF16),
        ((2, TILE, dim), BF16),
        ((TILE, dim), F32),
        ((length, dim), BF16),
        ((length, units), BF16),
        ((length, 2 * units), BF16),
        ((length, dim), BF16),
        ((2, width, length), BF16),
        ((2, width, length), BF16),
        ((1, dim), F32),
    ]
    return pl.pallas_call(
        middle_kernel,
        in_specs=[pl.BlockSpec(memory_space=pltpu.SMEM)] + [vm] * len(operands),
        out_specs=[vm] * len(shapes),
        scratch_shapes=[VMEM((dim, 3 * units), BF16)],
        out_shape=[jax.ShapeDtypeStruct(*shape) for shape in shapes],
        name="middle",
    )(info, *operands)


def unrope_into(out, row, values, cosine, sine):
    half = HD // 2
    one, two = values[:half], values[half:]
    out[row : row + half, :] = (one * cosine + two * sine).astype(BF16)
    out[row + half : row + HD, :] = (two * cosine - one * sine).astype(BF16)


def back_kernel(
    info,
    qkv,
    gmix,
    mixed,
    lse,
    grad_res,
    resid,
    gain,
    gain_two,
    wqkv,
    set0,
    set1,
    set2,
    set3,
    cos_ref,
    sin_ref,
    feed_stay,
    feed_leave,
    out_stay,
    out_leave,
    gproj,
    stay,
    leave,
    up_stay,
    up_leave,
    row_stay,
    row_leave,
    keys_sum,
    vals_sum,
    query_sum,
):
    length, dim = resid.shape
    width = gmix.shape[0]
    heads = width // HD
    keys_sum[...] = jnp.zeros_like(keys_sum)
    vals_sum[...] = jnp.zeros_like(vals_sum)

    def pull(h, lanes, cuts, seen):
        hs = slice(h * HD, (h + 1) * HD)
        ks = slice(width + h * HD, width + (h + 1) * HD)
        vs = slice(2 * width + h * HD, 2 * width + (h + 1) * HD)
        query, grad = qkv[hs, lanes], gmix[hs, lanes]
        key = jnp.concatenate([qkv[ks, cut] for cut in cuts], axis=1)
        value = jnp.concatenate([qkv[vs, cut] for cut in cuts], axis=1)
        delta = jnp.sum(grad.astype(F32) * mixed[hs, lanes].astype(F32), axis=0, keepdims=True)
        scores = jnp.where(seen, tn(key, query), MASKED)
        probs = jnp.exp(scores - lse[h : h + 1, lanes])
        dval = nt(grad, probs.astype(BF16))
        dscore = (probs * (tn(value, grad) - delta)).astype(BF16)
        query_sum[hs, lanes] = nn(key, dscore) * HD**-0.5
        dkey = nt(query, dscore)
        at = 0
        for cut, size in zip(cuts, (TILE, SEG, SEG)):
            keys_sum[hs, cut] += dkey[:, at : at + size]
            vals_sum[hs, cut] += dval[:, at : at + size]
            at += size

    for h in range(heads):
        pull(h, slice(0, TILE), (slice(0, TILE),), trunk_seen())

    def tile(r, carry):
        for half in range(2):
            start = r * TILE + half * SEG
            cuts, seen = block_keys(info[2 + 2 * r + half], start)
            for h in range(heads):
                pull(h, cuts[1], cuts, seen)
        return carry

    lax.fori_loop(1, length // TILE, tile, 0)

    cosine, sine = cos_ref[...], sin_ref[...]
    for h in range(heads):
        hs = slice(h * HD, (h + 1) * HD)
        unrope_into(gproj, h * HD, query_sum[hs, :], cosine, sine)
        unrope_into(gproj, width + h * HD, keys_sum[hs, :], cosine, sine)
    gproj[2 * width :, :] = vals_sum[...].astype(BF16)
    pulled = tn(gproj[...], wqkv[...])
    hidden = resid[...]
    rate = lax.rsqrt(jnp.mean(hidden * hidden, axis=-1, keepdims=True) + EPS)
    scaled = pulled * gain[...]
    dots = jnp.mean(scaled * hidden, axis=-1, keepdims=True)
    part = grad_res[...].astype(F32) + rate * scaled - hidden * (rate * rate * rate * dots)
    part = part.astype(BF16)
    for i in range(length // TILE):
        slot = slot_of(i ^ info[0])
        piece = part[i * TILE : (i + 1) * TILE]

        @pl.when(slot < 2)
        def _():
            stay[slot % 2, :TILE] = piece

        @pl.when(slot >= 2)
        def _():
            leave[slot % 2, :TILE] = piece

    stay[:, TILE:] = feed_stay[...]
    leave[:, TILE:] = feed_leave[...]
    sets = (set0, set1, set2, set3)
    ng = set0.shape[0]
    ups = jnp.concatenate([ref[:, :dim] for ref in sets], axis=0)
    by_column = nt(ups, part).astype(BF16)
    rows = jnp.concatenate([ref[:, dim:] for ref in sets], axis=0)
    grad_ups = nn(rows, part).astype(BF16)
    grad_gain = jnp.sum(pulled * hidden * rate, axis=0, keepdims=True)
    gains = jnp.concatenate([grad_gain, gain_two[...], jnp.zeros((14, dim), F32)], axis=0)
    gains = gains.astype(BF16)
    for k in range(4):
        (row_stay, row_leave)[k % 2][k // 2] = by_column[k * ng : (k + 1) * ng]
        out = (up_stay, up_leave)[k % 2]
        out[k // 2, :ng, :] = grad_ups[k * ng : (k + 1) * ng]
        out[k // 2, ng : ng + width, :] = (out_stay, out_leave)[k % 2][k // 2]
        out[k // 2, ng + width :, :] = gains


def back(
    info, qkv, gmix, mixed, lse, grad_res, resid, gain, gain_part, wqkv, sets, cosine, sine, feeds, outs
):
    length, dim = resid.shape
    width = gmix.shape[0]
    ng = sets[0].shape[0]
    vm = pl.BlockSpec(memory_space=VMEM)
    operands = [qkv, gmix, mixed, lse, grad_res, resid, gain, gain_part, wqkv, *sets, cosine, sine]
    operands += [*feeds, *outs]
    shapes = [(3 * width, length)] + [(2, 2 * TILE, dim)] * 2
    shapes += [(2, ng + width + 16, dim)] * 2 + [(2, ng, length)] * 2
    return pl.pallas_call(
        back_kernel,
        out_shape=[jax.ShapeDtypeStruct(shape, BF16) for shape in shapes],
        in_specs=[pl.BlockSpec(memory_space=pltpu.SMEM)] + [vm] * len(operands),
        out_specs=[vm] * len(shapes),
        scratch_shapes=[VMEM((width, length), F32)] * 3,
        name="back",
    )(info, *operands)


def rotary(parents):
    length = parents.shape[0]
    token = jnp.arange(length, dtype=jnp.int32)
    trunk = 2 * SEG
    inside = token < trunk
    block = jnp.where(inside, 0, (token - trunk) // SEG + 1)
    offset = jnp.where(inside, token, token - trunk - (block - 1) * SEG)
    position = jnp.where(inside, 0, jnp.where(parents == 0, 2 * SEG, 3 * SEG)) + offset
    half = HD // 2
    frequency = ROPE_BASE ** (-(jnp.arange(half, dtype=F32) * 2.0 / HD))
    angles = frequency[:, None] * position.astype(F32)[None, :]
    return jnp.cos(angles), jnp.sin(angles)


def shards(
    dp,
    embedded,
    ids_two,
    ids_three,
    parents,
    table_two,
    table_three,
    w_two,
    w_three,
    norm_attn,
    w_query,
    w_key,
    w_value,
    w_output,
    norm_ffn,
    w_gate,
    w_up,
    w_down,
    cotangent,
):
    own_d = lax.axis_index("dp")
    own_t = lax.axis_index("tensor")
    own_rows, ng = table_two.shape
    rows, dim = embedded.shape
    width = w_query.shape[1]
    units = w_gate.shape[1]
    own_dim = w_query.shape[0]
    gain_one = norm_attn.reshape(1, dim)
    gain_two = norm_ffn.reshape(1, dim)

    ids = jnp.stack([ids_two, ids_three])
    info = jnp.concatenate(
        [jnp.stack([own_t, own_d]).astype(jnp.int32), parents.reshape(-1, SEG)[:, 0]]
    )
    cosine, sine = rotary(parents)

    digits = jnp.stack([ids_two // 256, ids_two % 256, ids_three // 256, ids_three % 256])
    digits = jnp.pad(digits.astype(BF16), ((0, 12), (0, 0)))
    first = pack_first(table_two.T, table_three.T, w_two, w_three)
    attn_pack, ffn_pack = pack(w_query, w_key, w_value, w_output, w_gate, w_up, w_down.T)
    token_pair = jnp.stack([embedded, cotangent])
    token_near = xor_tensor(token_pair, 1)
    if dp == 8:
        arrays, (got, token_near) = double_dp(
            first,
            (attn_pack, ffn_pack, cosine, sine, gain_one, gain_two, digits),
            lambda zero: [lookup(info, [zero], (0, 4), own_rows, ids, None), token_near],
        )
        _, two, one, three = arrays
        token_far = xor_tensor(after(token_pair, arrays[0]), 2)
        got = lookup(info, [two, one], (2, 6, 1, 5), own_rows, ids, got)
        attn_arrays, (got, token_far) = double_dp(
            after(attn_pack, arrays[0]),
            (got,),
            lambda zero: [lookup(info, [three], (3, 7), own_rows, ids, got, arrays), token_far],
        )
        wqkv, wo = assemble(info, attn_arrays, True)
        ffn_arrays, _ = double_dp(after(ffn_pack, two), (attn_arrays[1],))
        wqkv, ffn_zero = lax.optimization_barrier((wqkv, ffn_arrays[0]))
        ffns = (ffn_zero, *ffn_arrays[1:])
    else:
        every = lax.all_gather(first[:, :own_rows], "dp", axis=0)
        small = jnp.concatenate([w_two.astype(BF16).T, w_three.astype(BF16).T], axis=1)
        ups = lax.all_gather(small, "dp", axis=0, tiled=True).T
        wqkvo = lax.all_gather(attn_pack, "dp", axis=0, tiled=True).T
        wqkv, wo = wqkvo[: 3 * width], wqkvo[3 * width :]
        ffns = [lax.all_gather(ffn_pack, "dp", axis=0, tiled=True)]
        ffns += [jnp.zeros((8, SEG), BF16)] * 3
        token_far = xor_tensor(token_pair, 2)

        def take(i, so_far):
            piece = lax.dynamic_index_in_dim(every, i, 0, keepdims=False)
            at = jnp.stack([own_t, i]).astype(jnp.int32)
            return lookup(at, [piece], (0,), own_rows, ids, so_far)

        got = lax.fori_loop(0, dp, take, jnp.zeros((2 * ng, ids.shape[1]), BF16))
        got = jnp.concatenate([ups, got], axis=1)

    tokens = [token_pair, token_near, token_far, xor_tensor(token_far, 1)]
    sets = gather_tensor(got)
    outs = gather_tensor(after(wo, sets[2]))

    resid, normed, qkv, mixed, lse = front(info, sets, tokens, wqkv, gain_one, cosine, sine)
    mixed = after(mixed, outs[2])
    mixes = gather_tensor(mixed)
    (
        feed_stay, feed_leave, resid_own, normed_two, hidden, grads, grad_res, stay, leave,
        gain_part_two,
    ) = middle(info, mixes, outs, resid, gain_two, ffns, tokens)
    near = xor_tensor(leave, 1)
    near_far = add_round(stay[1], near[1])
    far = xor_tensor(near_far, 2)
    halves, out_pair = weigh(
        info, tokens, after(hidden, near_far), normed_two, grads, mixes, grad_res, dp, own_dim
    )
    ffn_sum = SumDp(halves, dp)
    far, _ = lax.optimization_barrier((far, halves))
    gmix = total((stay[0], near[0], far)).astype(BF16)

    gproj, stay, leave, up_stay, up_leave, row_stay, row_leave = back(
        info, qkv, gmix, mixed, lse, grad_res, resid, gain_one, gain_part_two, wqkv, sets,
        cosine, sine, (feed_stay, feed_leave), out_pair,
    )

    near = xor_tensor(row_leave, 1)
    near_far = add_round(row_stay[1], near[1])
    if dp == 8:
        near_far, ffn_sum.first = lax.optimization_barrier((near_far, ffn_sum.first))
        ffn_sum.across()
    far = xor_tensor(near_far, 2)
    gproj = after(gproj, near_far)
    attn_halves = weigh_turned(info, normed, gproj, dp, own_dim)
    attn_sum = SumDp(attn_halves, dp)
    far, _ = lax.optimization_barrier((far, attn_halves))
    row_total = total((row_stay[0], near[0], far)).astype(BF16)
    row_pack = jnp.concatenate([row_total, digits], axis=0)
    up_near = xor_tensor(after(up_leave, near_far), 1)
    up_near_far = after(add_round(up_stay[1], up_near[1]), far)
    up_far = xor_tensor(up_near_far, 2)
    token_near = xor_tensor(after(leave, far), 1)
    token_far = xor_tensor(after(add_round(stay[1], token_near[1]), up_near_far), 2)
    if dp == 8:
        zero = jnp.stack([row_pack, xor_dp(row_pack, 4, dp)])
        zero, attn_sum.first, up_far, ffn_sum.second = lax.optimization_barrier(
            (zero, attn_sum.first, up_far, ffn_sum.second)
        )
    below = add_round(add_round(up_stay[0], up_near[0]), up_far)
    wide_grad, gains = below[: 2 * ng + width], below[2 * ng + width : 2 * ng + width + 2]
    if dp == 8:
        folded = gains.reshape(2 * dim // (2 * ng), 2 * ng)
        halves = turn(info, wide_grad, folded, dp, own_dim)
        proj_sum = SumDp(halves, dp)
        ffn_sum.between()
        two, one, ffn_sum.third, proj_sum.first = lax.optimization_barrier(
            (xor_dp(zero, 2, dp), xor_dp(zero, 1, dp), ffn_sum.third, proj_sum.first)
        )
        three = xor_dp(two, 1, dp)
        attn_sum.first = after(attn_sum.first, two)
        attn_sum.across()
        proj_sum.across()
        zero = after(zero, attn_sum.stay, proj_sum.stay)
        table_grad = spread(info, [zero, two, one], own_rows, ng, None, False)
        attn_sum.second, proj_sum.second, token_far, table_grad = lax.optimization_barrier(
            (attn_sum.second, proj_sum.second, token_far, table_grad)
        )
        attn_sum.between()
        proj_sum.between()
        token_far, ffn_sum.third = (
            after(x, attn_sum.ours, proj_sum.ours) for x in (token_far, ffn_sum.third)
        )
        sums = total((stay[0], token_near[0], token_far))
        embed_grad = sums[:rows].astype(BF16)
        output = (resid_own + sums[rows:]).astype(BF16)
        embed_grad, output, table_grad = lax.optimization_barrier(
            (embed_grad, output, table_grad)
        )
        table_grad = spread(info, [three], own_rows, ng, table_grad, True)
        *grads_done, folded, gate_grad, up_grad, down_grad = finish(
            attn_sum, proj_sum, ffn_sum, ng
        )
        gains = folded.reshape(2, dim)
    else:
        every = lax.all_gather(row_pack, "dp", axis=0)

        def put(i, so_far):
            piece = lax.dynamic_index_in_dim(every, i, 0, keepdims=False)
            return spread(info, [piece], own_rows, ng, so_far, False)

        table_grad = lax.fori_loop(0, dp, put, jnp.zeros((2 * ng, own_rows), F32))
        table_grad = table_grad[:ng], table_grad[ng:]
        sums = total((stay[0], token_near[0], token_far))
        embed_grad = sums[:rows].astype(BF16)
        output = (resid_own + sums[rows:]).astype(BF16)
        ffn_total = ffn_sum.total()
        gate_grad, up_grad, down_grad = (
            ffn_total[:, i * units : (i + 1) * units] for i in range(3)
        )
        attn_total = attn_sum.total()
        wide_total = SumDp(turn(info, wide_grad, None, dp, own_dim), dp).total()
        grads_done = [attn_total[:, i * width : (i + 1) * width] for i in range(3)]
        grads_done += [wide_total[:, :ng].T, wide_total[:, ng : 2 * ng].T, wide_total[:, 2 * ng :].T]
        gains = lax.psum(gains.astype(F32), "dp")
    query_grad, key_grad, value_grad, two_grad, three_grad, output_grad = grads_done

    return (
        output,
        embed_grad,
        table_grad[0].T,
        table_grad[1].T,
        two_grad,
        three_grad,
        gains[0],
        query_grad,
        key_grad,
        value_grad,
        output_grad,
        gains[1],
        gate_grad,
        up_grad,
        down_grad.T,
    )


def solution(mesh):
    tokens = P(("dp", "tensor"), None)
    down, across = P("dp", "tensor"), P("tensor", "dp")
    in_specs = (
        (tokens, P("dp"), P("dp"), P("dp"), down, down, across, across, P())
        + (down, down, down, across, P(), down, down, across, tokens)
    )
    out_specs = (
        (tokens, tokens, down, down, across, across, P())
        + (down, down, down, across, P(), down, down, across)
    )
    body = functools.partial(shards, mesh.shape["dp"])
    return jax.shard_map(body, mesh=mesh, in_specs=in_specs, out_specs=out_specs, check_vma=False)
```

```python
import functools

import jax
import jax.numpy as jnp
from jax import lax
from jax.experimental import pallas as pl
from jax.experimental.pallas import tpu as pltpu
from jax.sharding import PartitionSpec as P

HD = 64
SEG = 128
TILE = 2 * SEG
EPS = 1e-05
MASKED = -1e30
ROPE_BASE = 10000.0
F32 = jnp.float32
BF16 = jnp.bfloat16
VMEM = pltpu.VMEM


def xor_tensor(value, step):
    return lax.ppermute(value, "tensor", [(i, i ^ step) for i in range(4)])


def xor_dp(value, step, count):
    return lax.ppermute(value, "dp", [(i, i ^ step) for i in range(count)])


def after(value, *others):
    return lax.optimization_barrier((value,) + others)[0]


def gather_tensor(value):
    far = xor_tensor(value, 2)
    near = xor_tensor(value, 1)
    return [value, near, far, xor_tensor(far, 1)]


def add_round(one, two):
    return (one.astype(F32) + two.astype(F32)).astype(BF16)


def scatter_tensor(stay, leave):
    come = xor_tensor(leave, 1)
    far = xor_tensor(add_round(stay[1], come[1]), 2)
    return stay[0], come[0], far


def total(terms):
    return terms[0].astype(F32) + terms[1].astype(F32) + terms[2].astype(F32)


def double_dp(value, others=(), window=lambda zero: ()):
    zero = jnp.stack([value, after(xor_dp(value, 4, 8), *others)])
    made = window(zero)
    two, one, *made = lax.optimization_barrier((xor_dp(zero, 2, 8), xor_dp(zero, 1, 8), *made))
    return (zero, two, one, xor_dp(two, 1, 8)), made


DOUBLED = (0, 4, 2, 6, 1, 5, 3, 7)
HALVED = (0, 2, 1, 3)


def halve_first(keep, come):
    return add_round(keep[:2], come[:2]), add_round(keep[2:], come[2:])


def halve_second(stay, come):
    return add_round(stay[0], come[0]), add_round(stay[1], come[1])


class SumDp:
    def __init__(self, halves, count):
        self.count, self.halves = count, halves
        if count == 8:
            away, self.keep = halves
            self.first = xor_dp(away, 1, count)

    def across(self):
        if self.count == 8:
            self.stay, leave = halve_first(self.keep, self.first)
            self.second = xor_dp(leave, 2, self.count)

    def total(self):
        if self.count != 8:
            values = self.halves[0].astype(F32)
            return lax.psum_scatter(values, "dp", scatter_dimension=0, tiled=True)[0]
        return self.ours.astype(F32) + self.third.astype(F32)

    def between(self):
        if self.count == 8:
            self.ours, leave = halve_second(self.stay, self.second)
            self.third = xor_dp(leave, 4, self.count)


def entries(refs):
    out = []
    for ref in refs:
        out += [ref] if len(ref.shape) == 2 else [ref.at[i] for i in range(ref.shape[0])]
    return out


def place_rows(info, refs, lane, whole_ref):
    for piece, xor in zip(entries(refs), DOUBLED):
        rows = piece.shape[0]
        at = pl.ds(pl.multiple_of((info[1] ^ xor) * rows, 16), rows)
        whole_ref[at, :] = piece[:, lane : lane + whole_ref.shape[1]]


def assemble_kernel(turn, info, *refs):
    pieces, out = refs[:4], refs[4]
    whole_ref = refs[-1] if turn else out
    place_rows(info, pieces, 0, whole_ref)
    if turn:
        turned = whole_ref[...].T
        out[...] = turned[: out.shape[0]]
        refs[5][...] = turned[out.shape[0] :]


def assemble(info, arrays, turn):
    rows, cols = arrays[0].shape[1:]
    shapes = [(8 * rows, cols)]
    if turn:
        shapes = [(cols - cols // 4, 8 * rows), (cols // 4, 8 * rows)]
    return pl.pallas_call(
        functools.partial(assemble_kernel, turn),
        out_shape=[jax.ShapeDtypeStruct(shape, BF16) for shape in shapes],
        in_specs=[pl.BlockSpec(memory_space=pltpu.SMEM)] + [pl.BlockSpec(memory_space=VMEM)] * 4,
        out_specs=[pl.BlockSpec(memory_space=VMEM)] * len(shapes),
        scratch_shapes=[VMEM((8 * rows, cols), BF16)] if turn else [],
        name="assemble",
    )(info, *arrays)


def pick(refs, which):
    value = refs[3][0]
    for k in range(3):
        value = jnp.where(which == k, refs[k][0], value)
    return value


def whole(shape):
    return pl.BlockSpec(shape, lambda *_: (0,) * len(shape))


def nn(a, b):
    return lax.dot_general(a, b, (((1,), (0,)), ((), ())), preferred_element_type=F32)


def nt(a, b):
    return lax.dot_general(a, b, (((1,), (1,)), ((), ())), preferred_element_type=F32)


def tn(a, b):
    return lax.dot_general(a, b, (((0,), (0,)), ((), ())), preferred_element_type=F32)


def pack_first_kernel(two, three, up_two, up_three, out):
    ng, rows = two.shape
    out[:ng, :rows] = two[...].astype(BF16)
    out[ng:, :rows] = three[...].astype(BF16)
    out[:, rows:] = jnp.zeros((2 * ng, SEG), BF16)
    if up_two.shape[1] == 2 * ng:
        small = jnp.concatenate([up_two[...], up_three[...]], axis=0)
        out[:, rows : rows + 2 * ng] = small.T.astype(BF16)


def pack_first(two, three, up_two, up_three):
    ng, rows = two.shape
    return pl.pallas_call(
        pack_first_kernel,
        out_shape=jax.ShapeDtypeStruct((2 * ng, rows + SEG), BF16),
        name="pack_first",
    )(two, three, up_two, up_three)


def pack_kernel(query, key, value, output, gate, up, down, attn, ffn):
    width, units = query.shape[1], gate.shape[1]
    for i, ref in enumerate((query, key, value)):
        attn[:, i * width : (i + 1) * width] = ref[...].astype(BF16)
    attn[:, 3 * width :] = output[...].T.astype(BF16)
    for i, ref in enumerate((gate, up, down)):
        ffn[:, i * units : (i + 1) * units] = ref[...].astype(BF16)


def pack(query, key, value, output, gate, up, down):
    rows, width = query.shape
    return pl.pallas_call(
        pack_kernel,
        out_shape=[
            jax.ShapeDtypeStruct((rows, 4 * width), BF16),
            jax.ShapeDtypeStruct((rows, 3 * gate.shape[1]), BF16),
        ],
        name="pack",
    )(query, key, value, output, gate, up, down)


def split_rows(info, whole_ref, outs, rows):
    if len(outs) == 1:
        for i in range(outs[0].shape[0]):
            outs[0][i] = whole_ref[i * rows : (i + 1) * rows, :]
        return
    for entry, xor in enumerate(HALVED):
        for out, other in zip(outs, (1, 0)):
            at = info[1] ^ (2 * xor + other)
            out[entry] = whole_ref[pl.ds(pl.multiple_of(at * rows, 16), rows), :]


def weigh_kernel(rows, halves, info, hidden, norm, grads, *refs):
    cots, mixes, grad, refs = refs[:4], refs[4:8], refs[8], refs[9:]
    outs, (stay, leave, turned, whole_ref) = refs[:halves], refs[halves:]
    at = grads.shape[1]
    for tile in range(4):
        cot = pick([ref.at[1:2] for ref in cots], tile ^ info[0])
        turned[:, tile * TILE : (tile + 1) * TILE] = cot.T
    whole_ref[:, at:] = nn(turned[...], hidden[...]).astype(BF16)
    turned[...] = norm[...].T
    whole_ref[:, :at] = nn(turned[...], grads[...]).astype(BF16)
    split_rows(info, whole_ref, outs, rows)
    for xor in range(4):
        (stay, leave)[xor % 2][xor // 2] = nn(mixes[xor][...], grad[...]).astype(BF16)


def weigh(info, tokens, hidden, norm, grads, mixes, grad, count, own_dim):
    length, dim = norm.shape
    lead = [4, 4] if count == 8 else [count]
    cols = hidden.shape[1] + grads.shape[1]
    shapes = [(n, own_dim, cols) for n in lead] + [(2, mixes[0].shape[0], dim)] * 2
    operands = [hidden, norm, grads, *tokens, *mixes, grad]
    vm = pl.BlockSpec(memory_space=VMEM)
    got = pl.pallas_call(
        functools.partial(weigh_kernel, own_dim, len(lead)),
        in_specs=[pl.BlockSpec(memory_space=pltpu.SMEM)] + [vm] * len(operands),
        out_specs=[vm] * len(shapes),
        scratch_shapes=[VMEM((dim, length), BF16), VMEM((dim, cols), BF16)],
        out_shape=[jax.ShapeDtypeStruct(shape, BF16) for shape in shapes],
        name="weigh",
    )(info, *operands)
    return got[: len(lead)], got[len(lead) :]


def weigh_turned_kernel(rows, info, left, right, *refs):
    outs, whole_ref = refs[:-1], refs[-1]
    whole_ref[...] = nn(right[...], left[...]).astype(BF16).T
    split_rows(info, whole_ref, outs, rows)


def turn_kernel(rows, info, wide, *refs):
    outs, whole_ref = refs[:-1], refs[-1]
    whole_ref[...] = wide[...].T
    split_rows(info, whole_ref, outs, rows)


def turn_below_kernel(rows, info, wide, below, *refs):
    outs = refs[:-1]
    turn_kernel(rows, info, wide, *(out.at[:, :rows] for out in outs), refs[-1])
    for out in outs:
        for z in range(out.shape[0]):
            out[z, rows:, : below.shape[1]] = below[...]


def split_call(body, info, operands, count, own_dim, cols, below=0):
    vm = pl.BlockSpec(memory_space=VMEM)
    lead = [4, 4] if count == 8 else [count]
    shapes = [jax.ShapeDtypeStruct((n, own_dim + below, cols), BF16) for n in lead]
    return pl.pallas_call(
        functools.partial(body, own_dim),
        out_shape=shapes,
        in_specs=[pl.BlockSpec(memory_space=pltpu.SMEM)] + [vm] * len(operands),
        out_specs=[vm] * len(shapes),
        scratch_shapes=[VMEM((count * own_dim, cols), BF16)],
        name="split",
    )(info, *operands)


def weigh_turned(info, left, right, count, own_dim):
    return split_call(weigh_turned_kernel, info, [left, right], count, own_dim, right.shape[0])


def turn(info, wide, below, count, own_dim):
    if below is None:
        return split_call(turn_kernel, info, [wide], count, own_dim, wide.shape[0])
    return split_call(
        turn_below_kernel, info, [wide, below], count, own_dim, wide.shape[0], below.shape[0]
    )


def finish_kernel(
    attn, attn_come, wide, wide_come, ffn, ffn_come,
    query, key, value, two, three, output, gain, other_gain, gate, up, down,
):
    width, ng = query.shape[1], two.shape[0]
    rows = query.shape[0]
    sums = attn[...].astype(F32) + attn_come[...].astype(F32)
    for i, out in enumerate((query, key, value)):
        out[...] = sums[:, i * width : (i + 1) * width]
    sums = wide[...].astype(F32) + wide_come[...].astype(F32)
    turned = sums[:rows].T
    two[...] = turned[:ng]
    three[...] = turned[ng : 2 * ng]
    output[...] = turned[2 * ng :]
    lines, lanes = gain.shape
    gain[...] = sums[rows : rows + lines, :lanes]
    other_gain[...] = sums[rows + lines :, :lanes]
    units = gate.shape[1]
    for i, out in enumerate((gate, up, down)):
        cut = slice(i * units, (i + 1) * units)
        out[...] = ffn[:, cut].astype(F32) + ffn_come[:, cut].astype(F32)


def finish(attn_sum, wide_sum, ffn_sum, ng):
    rows, cols = attn_sum.ours.shape
    width = cols // 3
    operands = [attn_sum.ours, attn_sum.third, wide_sum.ours, wide_sum.third]
    operands += [ffn_sum.ours, ffn_sum.third]
    below = wide_sum.ours.shape[0] - rows
    shapes = [(rows, width)] * 3 + [(ng, rows)] * 2 + [(width, rows)] + [(below // 2, 2 * ng)] * 2
    shapes += [(rows, ffn_sum.ours.shape[1] // 3)] * 3
    vm = pl.BlockSpec(memory_space=VMEM)
    return pl.pallas_call(
        finish_kernel,
        out_shape=[jax.ShapeDtypeStruct(shape, F32) for shape in shapes],
        in_specs=[vm] * len(operands),
        out_specs=[vm] * len(shapes),
        name="finish",
    )(*operands)


def one_hot(low):
    rows = lax.broadcasted_iota(jnp.int32, (TILE, SEG), 0).astype(F32).astype(BF16)
    parts = [
        jnp.where(rows == low[:, c : c + SEG], BF16(1.0), BF16(0.0))
        for c in range(0, low.shape[1], SEG)
    ]
    return jnp.concatenate(parts, axis=1)


def lookup_kernel(owners, arrays, width, own_rows, start, end, *refs):
    info, ids = refs[0], refs[1]
    arrays, refs = refs[2 : 2 + arrays], refs[2 + arrays :]
    pieces = entries(arrays)
    count = len(owners)
    at = 0
    if end:
        ups, refs, out, whole_ref = refs[:4], refs[4:-2], refs[-2], refs[-1]
        at = out.shape[1] - ids.shape[1]
        place_rows(info, ups, own_rows, whole_ref)
        out[:, :at] = whole_ref[...].T[: 2 * width]
    else:
        out = refs[-1]
    prior = None if start else refs[0]
    chunks = own_rows // TILE
    for half in range(2):
        lanes = slice(half * width, (half + 1) * width)
        stacks = [
            jnp.concatenate([piece[lanes, c * TILE : (c + 1) * TILE] for c in range(chunks)], axis=0)
            for piece in pieces
        ]

        def part(n, carry):
            cut = pl.ds(pl.multiple_of(n * TILE, TILE), TILE)
            wanted = ids[half : half + 1, cut]
            high = wanted // TILE
            low = (wanted - high * TILE).astype(F32).astype(BF16)
            hot = one_hot(low)
            sofar = jnp.zeros((width, TILE), F32) if start else prior[lanes, cut].astype(F32)
            for stack, owner in zip(stacks, owners):
                got = nn(stack, hot)
                first = (info[1] ^ owner) * chunks
                for c in range(chunks):
                    mine = got[c * width : (c + 1) * width]
                    sofar = sofar + jnp.where(high == first + c, mine, 0.0)
            out[lanes, pl.ds(pl.multiple_of(at + n * TILE, TILE), TILE)] = sofar.astype(BF16)
            return carry

        lax.fori_loop(0, ids.shape[1] // TILE, part, 0)


def lookup(info, pieces, owners, own_rows, ids, prior, ups=()):
    width = pieces[0].shape[-2] // 2
    vm = pl.BlockSpec(memory_space=VMEM)
    operands = [info, ids, *pieces, *ups] + ([] if prior is None else [prior])
    at = 8 * ups[0].shape[1] if ups else 0
    return pl.pallas_call(
        functools.partial(
            lookup_kernel, owners, len(pieces), width, own_rows, prior is None, bool(ups)
        ),
        out_shape=jax.ShapeDtypeStruct((2 * width, at + ids.shape[1]), BF16),
        in_specs=[pl.BlockSpec(memory_space=pltpu.SMEM)] + [vm] * (len(operands) - 1),
        out_specs=vm,
        scratch_shapes=[VMEM((at, SEG), BF16)] if ups else [],
        name="lookup",
    )(*operands)


def spread_kernel(arrays, width, start, end, *refs):
    outs = refs[-2:] if end else refs[-1:]
    info, pieces = refs[0], entries(refs[1 : 1 + arrays])
    prior = None if start else refs[1 + arrays]
    own_rows = outs[0].shape[1]
    chunks = own_rows // TILE
    for half in range(2):
        lanes = slice(half * width, (half + 1) * width)
        sofar = None
        for piece in pieces:
            digits = piece[2 * width :, :]
            high, low = digits[2 * half : 2 * half + 1], digits[2 * half + 1 : 2 * half + 2]
            grads = piece[lanes, :]
            stack = [
                jnp.where(high == (info[1] * chunks + c).astype(F32).astype(BF16), grads, BF16(0.0))
                for c in range(chunks)
            ]
            got = nt(jnp.concatenate(stack, axis=0), one_hot(low))
            sofar = got if sofar is None else sofar + got
        for c in range(chunks):
            cut = slice(c * TILE, (c + 1) * TILE)
            part = sofar[c * width : (c + 1) * width]
            if not start:
                part = part + prior[lanes, cut]
            if end:
                outs[half][:, cut] = part
            else:
                outs[0][lanes, cut] = part


def spread(info, pieces, own_rows, width, prior, end):
    operands = [info, *pieces] + ([] if prior is None else [prior])
    vm = pl.BlockSpec(memory_space=VMEM)
    shapes = [(width, own_rows)] * 2 if end else [(2 * width, own_rows)]
    got = pl.pallas_call(
        functools.partial(spread_kernel, len(pieces), width, prior is None, end),
        out_shape=[jax.ShapeDtypeStruct(shape, F32) for shape in shapes],
        in_specs=[pl.BlockSpec(memory_space=pltpu.SMEM)] + [vm] * (len(operands) - 1),
        out_specs=[vm] * len(shapes),
        name="spread",
    )(*operands)
    return got if end else got[0]


def rope_into(out, row, values, cosine, sine, scale):
    half = HD // 2
    one, two = values[:half], values[half:]
    out[row : row + half, :] = (one * cosine - two * sine).astype(BF16) * scale
    out[row + half : row + HD, :] = (one * sine + two * cosine).astype(BF16) * scale


def key_offset(parent):
    return pl.multiple_of(jnp.where(parent > 0, parent + 1, 0) * SEG, SEG)


def block_keys(parent, start):
    key_at = lax.broadcasted_iota(jnp.int32, (4 * SEG, SEG), 0)
    query_at = lax.broadcasted_iota(jnp.int32, (4 * SEG, SEG), 1)
    limit = jnp.where(parent > 0, 4 * SEG, 3 * SEG)
    seen = (key_at < TILE) | ((key_at - TILE <= query_at) & (key_at < 3 * SEG))
    seen = seen | ((key_at >= 3 * SEG) & (key_at < limit))
    mine = pl.ds(pl.multiple_of(start, SEG), SEG)
    return (slice(0, TILE), mine, pl.ds(key_offset(parent), SEG)), seen


def trunk_seen():
    key_at = lax.broadcasted_iota(jnp.int32, (TILE, TILE), 0)
    return key_at <= lax.broadcasted_iota(jnp.int32, (TILE, TILE), 1)


def front_kernel(
    info,
    set0,
    set1,
    set2,
    set3,
    emb0,
    emb1,
    emb2,
    emb3,
    wqkv,
    gain,
    cos_ref,
    sin_ref,
    resid,
    normed,
    qkv,
    mixed,
    lse,
):
    length, dim = resid.shape
    sets = (set0, set1, set2, set3)
    rows = jnp.concatenate([ref[:, dim:] for ref in sets], axis=0)
    ups = jnp.concatenate([ref[:, :dim] for ref in sets], axis=0)
    own = [pick((emb0, emb1, emb2, emb3), i ^ info[0]) for i in range(length // TILE)]
    hidden = jnp.concatenate(own, axis=0).astype(F32) + tn(rows, ups)
    resid[...] = hidden
    rate = lax.rsqrt(jnp.mean(hidden * hidden, axis=-1, keepdims=True) + EPS)
    norm = (hidden * rate * gain[...]).astype(BF16)
    normed[...] = norm
    proj = nt(wqkv[...], norm)
    cosine, sine = cos_ref[...], sin_ref[...]
    width = mixed.shape[0]
    heads = width // HD
    for h in range(heads):
        rope_into(qkv, h * HD, proj[h * HD : (h + 1) * HD], cosine, sine, BF16(HD**-0.5))
        low = width + h * HD
        rope_into(qkv, low, proj[low : low + HD], cosine, sine, BF16(1.0))
    qkv[2 * width :, :] = proj[2 * width :].astype(BF16)

    def attend(h, lanes, cuts, seen):
        hs = slice(h * HD, (h + 1) * HD)
        ks = slice(width + h * HD, width + (h + 1) * HD)
        vs = slice(2 * width + h * HD, 2 * width + (h + 1) * HD)
        key = jnp.concatenate([qkv[ks, cut] for cut in cuts], axis=1)
        value = jnp.concatenate([qkv[vs, cut] for cut in cuts], axis=1)
        scores = jnp.where(seen, tn(key, qkv[hs, lanes]), MASKED)
        top = jnp.max(scores, axis=0, keepdims=True)
        weights = jnp.exp(scores - top)
        sums = jnp.sum(weights, axis=0, keepdims=True)
        got = nn(value, weights.astype(BF16))
        mixed[hs, lanes] = (got * (1.0 / sums)).astype(BF16)
        lse[h : h + 1, lanes] = top + jnp.log(sums)

    for h in range(heads):
        attend(h, slice(0, TILE), (slice(0, TILE),), trunk_seen())

    def block(j, carry):
        cuts, seen = block_keys(info[2 + j], j * SEG)
        for h in range(heads):
            attend(h, cuts[1], cuts, seen)
        return carry

    lax.fori_loop(TILE // SEG, length // SEG, block, 0)


def front(info, sets, tokens, wqkv, gain, cosine, sine):
    dim = tokens[0].shape[2]
    length = sets[0].shape[1] - dim
    width = wqkv.shape[0] // 3
    vm = pl.BlockSpec(memory_space=VMEM)
    operands = [*sets, *tokens, wqkv, gain, cosine, sine]
    shapes = [
        ((length, dim), F32),
        ((length, dim), BF16),
        ((3 * width, length), BF16),
        ((width, length), BF16),
        ((8, length), F32),
    ]
    return pl.pallas_call(
        front_kernel,
        out_shape=[jax.ShapeDtypeStruct(*shape) for shape in shapes],
        in_specs=[pl.BlockSpec(memory_space=pltpu.SMEM)] + [vm] * len(operands),
        out_specs=[vm] * len(shapes),
        name="front",
    )(info, *operands)


def slot_of(xor):
    return (xor & 1) * 2 + (xor >> 1)


def middle_kernel(
    who,
    mix0,
    mix1,
    mix2,
    mix3,
    out0,
    out1,
    out2,
    out3,
    resid,
    gain,
    ffn0,
    ffn1,
    ffn2,
    ffn3,
    cot0,
    cot1,
    cot2,
    cot3,
    feed_stay,
    feed_leave,
    resid_own,
    normed,
    hidden,
    grads,
    grad_res,
    mix_stay,
    mix_leave,
    grad_gain,
    ffn,
):
    units = hidden.shape[1]
    if len(ffn0.shape) == 3:
        place_rows(who, (ffn0, ffn1, ffn2, ffn3), 0, ffn)
    else:
        ffn[...] = ffn0[...]
    outs = jnp.concatenate([out0[...], out1[...], out2[...], out3[...]], axis=0)
    mix = jnp.concatenate([mix0[...], mix1[...], mix2[...], mix3[...]], axis=0)
    res = resid[...] + tn(mix, outs)
    tiles = range(res.shape[0] // TILE)
    for i in tiles:

        @pl.when(who[0] == i)
        def _():
            resid_own[...] = res[i * TILE : (i + 1) * TILE]

    rate = lax.rsqrt(jnp.mean(res * res, axis=-1, keepdims=True) + EPS)
    norm = (res * rate * gain[...]).astype(BF16)
    normed[...] = norm
    gate = nn(norm, ffn[:, :units])
    upward = nn(norm, ffn[:, units : 2 * units])
    sig = 1.0 / (1.0 + jnp.exp(-gate))
    silu = gate * sig
    hid = (silu * upward).astype(BF16)
    hidden[...] = hid
    fed = nt(hid, ffn[:, 2 * units :]).astype(BF16)
    for i in tiles:
        slot = slot_of(i ^ who[0])
        part = fed[i * TILE : (i + 1) * TILE]

        @pl.when(slot < 2)
        def _():
            feed_stay[slot % 2] = part

        @pl.when(slot >= 2)
        def _():
            feed_leave[slot % 2] = part

    cots = [ref.at[1:2] for ref in (cot0, cot1, cot2, cot3)]
    cot = jnp.concatenate([pick(cots, i ^ who[0]) for i in tiles], axis=0)
    back = nn(cot, ffn[:, 2 * units :])
    grad_gate = (back * upward * sig * (1.0 + gate * (1.0 - sig))).astype(BF16)
    grad_up = (back * silu).astype(BF16)
    grads[:, :units] = grad_gate
    grads[:, units:] = grad_up
    pulled = nt(grad_gate, ffn[:, :units]) + nt(grad_up, ffn[:, units : 2 * units])
    scaled = pulled * gain[...]
    dots = jnp.mean(scaled * res, axis=-1, keepdims=True)
    part = rate * scaled - res * (rate * rate * rate * dots) + 0.25 * cot.astype(F32)
    part = part.astype(BF16)
    grad_res[...] = part
    by_head = nt(outs, part).astype(BF16)
    width = out0.shape[0]
    for k in range(4):
        (mix_stay, mix_leave)[k % 2][k // 2] = by_head[k * width : (k + 1) * width]
    grad_gain[...] = jnp.sum(pulled * res * rate, axis=0, keepdims=True)


def middle(info, mixes, outs, resid, gain, ffns, tokens):
    length, dim = resid.shape
    width = mixes[0].shape[0]
    units = ffns[0].shape[-1] // 3
    vm = pl.BlockSpec(memory_space=VMEM)
    operands = [*mixes, *outs, resid, gain, *ffns, *tokens]
    shapes = [
        ((2, TILE, dim), BF16),
        ((2, TILE, dim), BF16),
        ((TILE, dim), F32),
        ((length, dim), BF16),
        ((length, units), BF16),
        ((length, 2 * units), BF16),
        ((length, dim), BF16),
        ((2, width, length), BF16),
        ((2, width, length), BF16),
        ((1, dim), F32),
    ]
    return pl.pallas_call(
        middle_kernel,
        in_specs=[pl.BlockSpec(memory_space=pltpu.SMEM)] + [vm] * len(operands),
        out_specs=[vm] * len(shapes),
        scratch_shapes=[VMEM((dim, 3 * units), BF16)],
        out_shape=[jax.ShapeDtypeStruct(*shape) for shape in shapes],
        name="middle",
    )(info, *operands)


def unrope_into(out, row, values, cosine, sine):
    half = HD // 2
    one, two = values[:half], values[half:]
    out[row : row + half, :] = (one * cosine + two * sine).astype(BF16)
    out[row + half : row + HD, :] = (two * cosine - one * sine).astype(BF16)


def back_kernel(
    info,
    qkv,
    gmix,
    mixed,
    lse,
    grad_res,
    resid,
    gain,
    gain_two,
    wqkv,
    set0,
    set1,
    set2,
    set3,
    cos_ref,
    sin_ref,
    feed_stay,
    feed_leave,
    out_stay,
    out_leave,
    gproj,
    stay,
    leave,
    up_stay,
    up_leave,
    row_stay,
    row_leave,
    keys_sum,
    vals_sum,
    query_sum,
):
    length, dim = resid.shape
    width = gmix.shape[0]
    heads = width // HD
    keys_sum[...] = jnp.zeros_like(keys_sum)
    vals_sum[...] = jnp.zeros_like(vals_sum)

    def pull(h, lanes, cuts, seen):
        hs = slice(h * HD, (h + 1) * HD)
        ks = slice(width + h * HD, width + (h + 1) * HD)
        vs = slice(2 * width + h * HD, 2 * width + (h + 1) * HD)
        query, grad = qkv[hs, lanes], gmix[hs, lanes]
        key = jnp.concatenate([qkv[ks, cut] for cut in cuts], axis=1)
        value = jnp.concatenate([qkv[vs, cut] for cut in cuts], axis=1)
        delta = jnp.sum(grad.astype(F32) * mixed[hs, lanes].astype(F32), axis=0, keepdims=True)
        scores = jnp.where(seen, tn(key, query), MASKED)
        probs = jnp.exp(scores - lse[h : h + 1, lanes])
        dval = nt(grad, probs.astype(BF16))
        dscore = (probs * (tn(value, grad) - delta)).astype(BF16)
        query_sum[hs, lanes] = nn(key, dscore) * HD**-0.5
        dkey = nt(query, dscore)
        at = 0
        for cut, size in zip(cuts, (TILE, SEG, SEG)):
            keys_sum[hs, cut] += dkey[:, at : at + size]
            vals_sum[hs, cut] += dval[:, at : at + size]
            at += size

    for h in range(heads):
        pull(h, slice(0, TILE), (slice(0, TILE),), trunk_seen())

    def tile(r, carry):
        for half in range(2):
            start = r * TILE + half * SEG
            cuts, seen = block_keys(info[2 + 2 * r + half], start)
            for h in range(heads):
                pull(h, cuts[1], cuts, seen)
        return carry

    lax.fori_loop(1, length // TILE, tile, 0)

    cosine, sine = cos_ref[...], sin_ref[...]
    for h in range(heads):
        hs = slice(h * HD, (h + 1) * HD)
        unrope_into(gproj, h * HD, query_sum[hs, :], cosine, sine)
        unrope_into(gproj, width + h * HD, keys_sum[hs, :], cosine, sine)
    gproj[2 * width :, :] = vals_sum[...].astype(BF16)
    pulled = tn(gproj[...], wqkv[...])
    hidden = resid[...]
    rate = lax.rsqrt(jnp.mean(hidden * hidden, axis=-1, keepdims=True) + EPS)
    scaled = pulled * gain[...]
    dots = jnp.mean(scaled * hidden, axis=-1, keepdims=True)
    part = grad_res[...].astype(F32) + rate * scaled - hidden * (rate * rate * rate * dots)
    part = part.astype(BF16)
    for i in range(length // TILE):
        slot = slot_of(i ^ info[0])
        piece = part[i * TILE : (i + 1) * TILE]

        @pl.when(slot < 2)
        def _():
            stay[slot % 2, :TILE] = piece

        @pl.when(slot >= 2)
        def _():
            leave[slot % 2, :TILE] = piece

    stay[:, TILE:] = feed_stay[...]
    leave[:, TILE:] = feed_leave[...]
    sets = (set0, set1, set2, set3)
    ng = set0.shape[0]
    ups = jnp.concatenate([ref[:, :dim] for ref in sets], axis=0)
    by_column = nt(ups, part).astype(BF16)
    rows = jnp.concatenate([ref[:, dim:] for ref in sets], axis=0)
    grad_ups = nn(rows, part).astype(BF16)
    grad_gain = jnp.sum(pulled * hidden * rate, axis=0, keepdims=True)
    gains = jnp.concatenate([grad_gain, gain_two[...], jnp.zeros((14, dim), F32)], axis=0)
    gains = gains.astype(BF16)
    for k in range(4):
        (row_stay, row_leave)[k % 2][k // 2] = by_column[k * ng : (k + 1) * ng]
        out = (up_stay, up_leave)[k % 2]
        out[k // 2, :ng, :] = grad_ups[k * ng : (k + 1) * ng]
        out[k // 2, ng : ng + width, :] = (out_stay, out_leave)[k % 2][k // 2]
        out[k // 2, ng + width :, :] = gains


def back(
    info, qkv, gmix, mixed, lse, grad_res, resid, gain, gain_part, wqkv, sets, cosine, sine, feeds, outs
):
    length, dim = resid.shape
    width = gmix.shape[0]
    ng = sets[0].shape[0]
    vm = pl.BlockSpec(memory_space=VMEM)
    operands = [qkv, gmix, mixed, lse, grad_res, resid, gain, gain_part, wqkv, *sets, cosine, sine]
    operands += [*feeds, *outs]
    shapes = [(3 * width, length)] + [(2, 2 * TILE, dim)] * 2
    shapes += [(2, ng + width + 16, dim)] * 2 + [(2, ng, length)] * 2
    return pl.pallas_call(
        back_kernel,
        out_shape=[jax.ShapeDtypeStruct(shape, BF16) for shape in shapes],
        in_specs=[pl.BlockSpec(memory_space=pltpu.SMEM)] + [vm] * len(operands),
        out_specs=[vm] * len(shapes),
        scratch_shapes=[VMEM((width, length), F32)] * 3,
        name="back",
    )(info, *operands)


def rotary(parents):
    length = parents.shape[0]
    token = jnp.arange(length, dtype=jnp.int32)
    trunk = 2 * SEG
    inside = token < trunk
    block = jnp.where(inside, 0, (token - trunk) // SEG + 1)
    offset = jnp.where(inside, token, token - trunk - (block - 1) * SEG)
    position = jnp.where(inside, 0, jnp.where(parents == 0, 2 * SEG, 3 * SEG)) + offset
    half = HD // 2
    frequency = ROPE_BASE ** (-(jnp.arange(half, dtype=F32) * 2.0 / HD))
    angles = frequency[:, None] * position.astype(F32)[None, :]
    return jnp.cos(angles), jnp.sin(angles)


def shards(
    dp,
    embedded,
    ids_two,
    ids_three,
    parents,
    table_two,
    table_three,
    w_two,
    w_three,
    norm_attn,
    w_query,
    w_key,
    w_value,
    w_output,
    norm_ffn,
    w_gate,
    w_up,
    w_down,
    cotangent,
):
    own_d = lax.axis_index("dp")
    own_t = lax.axis_index("tensor")
    own_rows, ng = table_two.shape
    rows, dim = embedded.shape
    width = w_query.shape[1]
    units = w_gate.shape[1]
    own_dim = w_query.shape[0]
    gain_one = norm_attn.reshape(1, dim)
    gain_two = norm_ffn.reshape(1, dim)

    ids = jnp.stack([ids_two, ids_three])
    info = jnp.concatenate(
        [jnp.stack([own_t, own_d]).astype(jnp.int32), parents.reshape(-1, SEG)[:, 0]]
    )
    cosine, sine = rotary(parents)

    digits = jnp.stack([ids_two // 256, ids_two % 256, ids_three // 256, ids_three % 256])
    digits = jnp.pad(digits.astype(BF16), ((0, 12), (0, 0)))
    first = pack_first(table_two.T, table_three.T, w_two, w_three)
    attn_pack, ffn_pack = pack(w_query, w_key, w_value, w_output, w_gate, w_up, w_down.T)
    token_pair = jnp.stack([embedded, cotangent])
    token_near = xor_tensor(token_pair, 1)
    if dp == 8:
        arrays, (got, token_near) = double_dp(
            first,
            (attn_pack, ffn_pack, cosine, sine, gain_one, gain_two, digits),
            lambda zero: [lookup(info, [zero], (0, 4), own_rows, ids, None), token_near],
        )
        _, two, one, three = arrays
        token_far = xor_tensor(after(token_pair, arrays[0]), 2)
        got = lookup(info, [two, one], (2, 6, 1, 5), own_rows, ids, got)
        attn_arrays, (got, token_far) = double_dp(
            after(attn_pack, arrays[0]),
            (got,),
            lambda zero: [lookup(info, [three], (3, 7), own_rows, ids, got, arrays), token_far],
        )
        wqkv, wo = assemble(info, attn_arrays, True)
        ffn_arrays, _ = double_dp(after(ffn_pack, two), (attn_arrays[1],))
        wqkv, ffn_zero = lax.optimization_barrier((wqkv, ffn_arrays[0]))
        ffns = (ffn_zero, *ffn_arrays[1:])
    else:
        every = lax.all_gather(first[:, :own_rows], "dp", axis=0)
        small = jnp.concatenate([w_two.astype(BF16).T, w_three.astype(BF16).T], axis=1)
        ups = lax.all_gather(small, "dp", axis=0, tiled=True).T
        wqkvo = lax.all_gather(attn_pack, "dp", axis=0, tiled=True).T
        wqkv, wo = wqkvo[: 3 * width], wqkvo[3 * width :]
        ffns = [lax.all_gather(ffn_pack, "dp", axis=0, tiled=True)]
        ffns += [jnp.zeros((8, SEG), BF16)] * 3
        token_far = xor_tensor(token_pair, 2)

        def take(i, so_far):
            piece = lax.dynamic_index_in_dim(every, i, 0, keepdims=False)
            at = jnp.stack([own_t, i]).astype(jnp.int32)
            return lookup(at, [piece], (0,), own_rows, ids, so_far)

        got = lax.fori_loop(0, dp, take, jnp.zeros((2 * ng, ids.shape[1]), BF16))
        got = jnp.concatenate([ups, got], axis=1)

    tokens = [token_pair, token_near, token_far, xor_tensor(token_far, 1)]
    sets = gather_tensor(got)
    outs = gather_tensor(after(wo, sets[2]))

    resid, normed, qkv, mixed, lse = front(info, sets, tokens, wqkv, gain_one, cosine, sine)
    mixed = after(mixed, outs[2])
    mixes = gather_tensor(mixed)
    (
        feed_stay, feed_leave, resid_own, normed_two, hidden, grads, grad_res, stay, leave,
        gain_part_two,
    ) = middle(info, mixes, outs, resid, gain_two, ffns, tokens)
    near = xor_tensor(leave, 1)
    near_far = add_round(stay[1], near[1])
    far = xor_tensor(near_far, 2)
    halves, out_pair = weigh(
        info, tokens, after(hidden, near_far), normed_two, grads, mixes, grad_res, dp, own_dim
    )
    ffn_sum = SumDp(halves, dp)
    far, _ = lax.optimization_barrier((far, halves))
    gmix = total((stay[0], near[0], far)).astype(BF16)

    gproj, stay, leave, up_stay, up_leave, row_stay, row_leave = back(
        info, qkv, gmix, mixed, lse, grad_res, resid, gain_one, gain_part_two, wqkv, sets,
        cosine, sine, (feed_stay, feed_leave), out_pair,
    )

    near = xor_tensor(row_leave, 1)
    near_far = add_round(row_stay[1], near[1])
    if dp == 8:
        near_far, ffn_sum.first = lax.optimization_barrier((near_far, ffn_sum.first))
        ffn_sum.across()
    far = xor_tensor(near_far, 2)
    gproj = after(gproj, near_far)
    attn_halves = weigh_turned(info, normed, gproj, dp, own_dim)
    attn_sum = SumDp(attn_halves, dp)
    far, _ = lax.optimization_barrier((far, attn_halves))
    row_total = total((row_stay[0], near[0], far)).astype(BF16)
    row_pack = jnp.concatenate([row_total, digits], axis=0)
    up_near = xor_tensor(after(up_leave, near_far), 1)
    up_near_far = after(add_round(up_stay[1], up_near[1]), far)
    up_far = xor_tensor(up_near_far, 2)
    token_near = xor_tensor(after(leave, far), 1)
    token_far = xor_tensor(after(add_round(stay[1], token_near[1]), up_near_far), 2)
    if dp == 8:
        zero = jnp.stack([row_pack, xor_dp(row_pack, 4, dp)])
        zero, attn_sum.first, up_far, ffn_sum.second = lax.optimization_barrier(
            (zero, attn_sum.first, up_far, ffn_sum.second)
        )
    below = add_round(add_round(up_stay[0], up_near[0]), up_far)
    wide_grad, gains = below[: 2 * ng + width], below[2 * ng + width : 2 * ng + width + 2]
    if dp == 8:
        folded = gains.reshape(2 * dim // (2 * ng), 2 * ng)
        halves = turn(info, wide_grad, folded, dp, own_dim)
        proj_sum = SumDp(halves, dp)
        ffn_sum.between()
        two, one, ffn_sum.third, proj_sum.first = lax.optimization_barrier(
            (xor_dp(zero, 2, dp), xor_dp(zero, 1, dp), ffn_sum.third, proj_sum.first)
        )
        three = xor_dp(two, 1, dp)
        attn_sum.first = after(attn_sum.first, two)
        attn_sum.across()
        proj_sum.across()
        zero = after(zero, attn_sum.stay, proj_sum.stay)
        table_grad = spread(info, [zero, two, one], own_rows, ng, None, False)
        attn_sum.second, proj_sum.second, token_far, table_grad = lax.optimization_barrier(
            (attn_sum.second, proj_sum.second, token_far, table_grad)
        )
        attn_sum.between()
        proj_sum.between()
        token_far, ffn_sum.third = (
            after(x, attn_sum.ours, proj_sum.ours) for x in (token_far, ffn_sum.third)
        )
        sums = total((stay[0], token_near[0], token_far))
        embed_grad = sums[:rows].astype(BF16)
        output = (resid_own + sums[rows:]).astype(BF16)
        embed_grad, output, table_grad = lax.optimization_barrier(
            (embed_grad, output, table_grad)
        )
        table_grad = spread(info, [three], own_rows, ng, table_grad, True)
        *grads_done, gain, other_gain, gate_grad, up_grad, down_grad = finish(
            attn_sum, proj_sum, ffn_sum, ng
        )
        gains = gain.reshape(dim), other_gain.reshape(dim)
    else:
        every = lax.all_gather(row_pack, "dp", axis=0)

        def put(i, so_far):
            piece = lax.dynamic_index_in_dim(every, i, 0, keepdims=False)
            return spread(info, [piece], own_rows, ng, so_far, False)

        table_grad = lax.fori_loop(0, dp, put, jnp.zeros((2 * ng, own_rows), F32))
        table_grad = table_grad[:ng], table_grad[ng:]
        sums = total((stay[0], token_near[0], token_far))
        embed_grad = sums[:rows].astype(BF16)
        output = (resid_own + sums[rows:]).astype(BF16)
        ffn_total = ffn_sum.total()
        gate_grad, up_grad, down_grad = (
            ffn_total[:, i * units : (i + 1) * units] for i in range(3)
        )
        attn_total = attn_sum.total()
        wide_total = SumDp(turn(info, wide_grad, None, dp, own_dim), dp).total()
        grads_done = [attn_total[:, i * width : (i + 1) * width] for i in range(3)]
        grads_done += [wide_total[:, :ng].T, wide_total[:, ng : 2 * ng].T, wide_total[:, 2 * ng :].T]
        gains = lax.psum(gains.astype(F32), "dp")
    query_grad, key_grad, value_grad, two_grad, three_grad, output_grad = grads_done

    return (
        output,
        embed_grad,
        table_grad[0].T,
        table_grad[1].T,
        two_grad,
        three_grad,
        gains[0],
        query_grad,
        key_grad,
        value_grad,
        output_grad,
        gains[1],
        gate_grad,
        up_grad,
        down_grad.T,
    )


def solution(mesh):
    tokens = P(("dp", "tensor"), None)
    down, across = P("dp", "tensor"), P("tensor", "dp")
    in_specs = (
        (tokens, P("dp"), P("dp"), P("dp"), down, down, across, across, P())
        + (down, down, down, across, P(), down, down, across, tokens)
    )
    out_specs = (
        (tokens, tokens, down, down, across, across, P())
        + (down, down, down, across, P(), down, down, across)
    )
    body = functools.partial(shards, mesh.shape["dp"])
    return jax.shard_map(body, mesh=mesh, in_specs=in_specs, out_specs=out_specs, check_vma=False)
```
